256 devices in a mesh: frames: 8 (over z_lo, y), slab: 32 (over z_hi, x, core).
Axes of the slice: x: 4, y: 4, z: 8 (z_hi: 4, z_lo: 2; z = z_hi * 2 + z_lo), core: 2. Of those that a mesh axis runs over, the one named last changes fastest.
Arguments:
- raw_movie: bfloat16 [16, 2048, 128], P('frames', 'slab'), may hold values from -18 to 18
- shifts: int32 [2, 16, 64, 1], P(None, 'frames', 'slab'), may hold values from -3 to 3
- footprints: bfloat16 [1024, 16, 16], P('slab'), may hold values from 0.049804688 to 1
- anchors: int32 [1024, 2], P('slab'), may hold values from 0 to 2032, as said below
- block_of: int32 [1024], P('slab'), may hold values from 0 to 3, as said below
- init_traces: float32 [1024, 16], P('slab', 'frames'), may hold values from -6 to 6
Outputs:
- traces_z: float32 [1024, 16], P('slab', 'frames')
- residual: float32 [16, 2048, 128], P('frames', 'slab')
The draws below stay inside these ranges and needn't reach their ends.
Inputs may be any that keep to these rules, and one draw needn't show every extreme that they name: `anchors`: the tile of a source owned by slab s (sources s * 32 to s * 32 + 31) has its top row in s * 64 - 16 // 2 to s * 64 + 64 - 16 // 2 - 1, moved into the grid where it would leave it; its left column lies in 0 to 112. `block_of`: among the 32 sources of one slab, each block number is held by at most 16 sources, and some block number by exactly 16.
All inputs are finite; a program needn't handle non-finite values.
Results may differ from the reference program's by a relative error of at most 0.003.
Values may be sent and summed in bfloat16 or wider, within the bound.
A program may use at most 64 MiB of HBM per device.

```python
import jax
import jax.numpy as jnp
from jax import lax

ROWS = 64
COLS = 128
K_DEV = 32
TILE = 16
SHIFT = 3
PATCH_R = 32
PATCH_C = 128
BLOCKS = 4
SWEEPS = 3
FRAMES = 16
NROWS = 2048
SOURCES = 1024
NPR = 64
NPC = 1
BMAX = 16


def draw_raw_movie(key, part):
    frame_ramp = 1.0 + 2.0 * jnp.arange(FRAMES, dtype=jnp.float32) / max(FRAMES - 1, 1)
    pattern = jnp.clip(jax.random.normal(key, (FRAMES, NROWS, COLS), jnp.float32), -6.0, 6.0)
    return (pattern * frame_ramp[:, None, None]).astype(jnp.bfloat16)


def draw_anchors(key, part):
    subkeys = jax.random.split(key, 2)
    owner_slab = jnp.arange(SOURCES, dtype=jnp.int32) // K_DEV
    row_anchor = owner_slab * ROWS - TILE // 2 + jax.random.randint(subkeys[0], (SOURCES,), 0, ROWS, dtype=jnp.int32)
    row_anchor = jnp.clip(row_anchor, 0, NROWS - TILE)
    col_anchor = jax.random.randint(subkeys[1], (SOURCES,), 0, COLS - TILE + 1, dtype=jnp.int32)
    return jnp.stack([row_anchor, col_anchor], axis=1).astype(jnp.int32)


def draw_block_of(key, part):
    subkeys = jax.random.split(key, 3)
    slab_total = SOURCES // K_DEV
    heavy = jax.random.randint(subkeys[0], (slab_total, 1), 0, BLOCKS, dtype=jnp.int32)
    orders = jax.vmap(lambda single_key: jax.random.permutation(single_key, K_DEV))(jax.random.split(subkeys[1], slab_total))
    others = (heavy + 1 + jax.random.randint(subkeys[2], (slab_total, K_DEV), 0, BLOCKS - 1, dtype=jnp.int32)) % BLOCKS
    forced = orders < BMAX
    return jnp.where(forced, heavy, others).reshape(SOURCES).astype(jnp.int32)


def with_ends(entries, rng, least, high):
    shape = entries.shape
    spot = [jax.random.randint(jax.random.fold_in(rng, axis), (), 0, shape[axis]) for axis in range(len(shape))]
    entries = entries.at[tuple(spot)].set(least)
    longest = shape.index(max(shape))
    spot[longest] = (spot[longest] + 1) % shape[longest]
    return entries.at[tuple(spot)].set(high)


def block_scale(rng, dims, shards, least, high):
    gain = 1.0
    for dim, parts in shards:
        draws = jax.random.uniform(jax.random.fold_in(jax.random.fold_in(rng, 6), dim), (parts,), jnp.float32, least / len(shards), high / len(shards))
        gain = gain * jnp.repeat(jnp.exp(draws), dims[dim] // parts).reshape((-1,) + (1,) * (len(dims) - 1 - dim))
    return gain


def normal_values(stream_key, dims, deviation, most, shards=(), kind=jnp.bfloat16):
    gain = block_scale(stream_key, dims, shards, -0.22, 0.18) if shards else 1.0
    entries = jax.random.normal(stream_key, dims, jnp.float32) * deviation * gain
    return jnp.minimum(jnp.maximum(entries, -most), most).astype(kind)


def setup_inputs(seed: int = 0) -> dict:
    key_list = jax.random.split(jax.random.key(seed), 7)
    raw_movie = draw_raw_movie(jax.random.fold_in(key_list[6], 71), 0)
    shifts = with_ends(jax.random.randint(key_list[1], (2, FRAMES, NPR, NPC), -SHIFT, SHIFT + 1), jax.random.fold_in(key_list[1], 1), -SHIFT, SHIFT).astype(jnp.int32)
    footprints = jnp.clip(0.049804688 + 0.9501953 * jax.random.uniform(key_list[2], (SOURCES, TILE, TILE), jnp.float32) ** block_scale(key_list[2], (SOURCES, TILE, TILE), ((0, 32),), -0.2, 0.2), 0.049804688, 1.0).astype(jnp.bfloat16)
    anchors = draw_anchors(jax.random.fold_in(key_list[6], 71), 0)
    block_of = draw_block_of(jax.random.fold_in(key_list[6], 71), 0)
    init_traces = normal_values(key_list[5], (SOURCES, FRAMES), 1.0, 6.0, ((0, 32), (1, 8)), jnp.float32)
    return {"raw_movie": raw_movie, "shifts": shifts, "footprints": footprints, "anchors": anchors, "block_of": block_of, "init_traces": init_traces}


WEIGHT_NEAR = 0.75
WEIGHT_FAR = 0.25
EPSILON = 1e-05

def warp_frame(padded, rows_shift, cols_shift):
    count_r, count_c = rows_shift.shape

    def one_patch(patch_row, patch_col, row_shift, col_shift):
        window = lax.dynamic_slice(padded, (SHIFT + 1 + patch_row * PATCH_R + row_shift, SHIFT + patch_col * PATCH_C + col_shift), (PATCH_R + 1, PATCH_C)).astype(jnp.float32)
        return WEIGHT_NEAR * window[:-1] + WEIGHT_FAR * window[1:]
    across = jax.vmap(one_patch, in_axes=(None, 0, 0, 0))
    layout = jax.vmap(across, in_axes=(0, None, 0, 0))(jnp.arange(count_r, dtype=jnp.int32), jnp.arange(count_c, dtype=jnp.int32), rows_shift, cols_shift)
    return layout.transpose(0, 2, 1, 3).reshape(count_r * PATCH_R, count_c * PATCH_C)

def reference(raw_movie, shifts, footprints, anchors, block_of, init_traces):
    padded = jnp.pad(raw_movie, ((0, 0), (SHIFT + 1, SHIFT + 1), (SHIFT, SHIFT)))
    corrected = jax.vmap(warp_frame)(padded, shifts[0], shifts[1]).astype(jnp.bfloat16)
    offsets = jnp.arange(TILE, dtype=jnp.int32)
    tile_rows = anchors[:, 0][:, None, None] + offsets[None, :, None]
    tile_cols = anchors[:, 1][:, None, None] + offsets[None, None, :]
    weights = footprints.astype(jnp.float32)
    norm_sq = lax.optimization_barrier(jnp.sum(weights * weights, axis=(1, 2)))
    block_masks = [block_of == block_idx for block_idx in range(BLOCKS)]

    def render(values):
        canvas = jnp.zeros((NROWS, COLS), jnp.float32)
        return canvas.at[tile_rows, tile_cols].add(weights * values[:, None, None])

    def solve_frame(inputs):
        frame_image, first_traces = inputs
        residual = frame_image.astype(jnp.float32) - render(first_traces)
        traces = first_traces
        for sweep_idx in range(SWEEPS):
            for block_idx in range(BLOCKS):
                projected = lax.optimization_barrier(jnp.sum(residual[tile_rows, tile_cols] * weights, axis=(1, 2)))
                change = jnp.where(block_masks[block_idx], projected / norm_sq, jnp.zeros_like(projected))
                traces = traces + change
                residual = residual - render(change)
        return (traces, residual)
    traces, residual = lax.map(solve_frame, (corrected, init_traces.T))
    traces = traces.T
    trace_mean = lax.optimization_barrier(jnp.mean(traces, axis=1, keepdims=True))
    square_mean = lax.optimization_barrier(jnp.mean(traces * traces, axis=1, keepdims=True))
    spread = square_mean - trace_mean * trace_mean
    traces_z = (traces - trace_mean) / jnp.sqrt(spread + EPSILON)
    return (traces_z, residual)
```

```python
import functools

import jax
import jax.numpy as jnp
from jax import lax
from jax.experimental import pallas as pl
from jax.experimental.pallas import tpu as pltpu
from jax.sharding import PartitionSpec as P

ROWS = 64
COLS = 128
KD = 32
TILE = 16
RIM = 8
EXT = 80
BLOCKS = 4
SWEEPS = 3
STEPS = BLOCKS * SWEEPS
HALO = STEPS
SLOTS = 2 * HALO + 1
CHUNKS = (SLOTS + 3) // 4
EPSILON = 1e-05
MESH = pl.DeviceIdType.MESH
F32 = jnp.float32
BF16 = jnp.bfloat16
NT = (((1,), (1,)), ((), ()))


def iota(shape, dim):
    return lax.broadcasted_iota(jnp.int32, shape, dim)


def mm(a, b):
    return jnp.dot(a, b, preferred_element_type=F32)


def mm_nt(a, b):
    return lax.dot_general(a, b, NT, preferred_element_type=F32)


def split(x):
    hi = x.astype(BF16).astype(F32)
    return hi, x - hi


def place_columns(packed, col, wide_ref):
    lane_group = iota((TILE, COLS), 1) // TILE
    for g in range(4):
        rows = packed[g * TILE : (g + 1) * TILE, :]
        lhs = jnp.concatenate(
            [jnp.where(lane_group == kk, rows, 0.0).astype(BF16) for kk in range(8)], axis=0
        )
        anchor = jnp.broadcast_to(col[8 * g : 8 * g + 8, None, :], (8, TILE, COLS))
        offset = (iota((8, TILE, COLS), 2) - iota((8, TILE, COLS), 1)).astype(F32)
        onehot = jnp.where(anchor == offset, 1.0, 0.0).astype(BF16).reshape(COLS, COLS)
        wide_ref[g * COLS : (g + 1) * COLS, :] = mm(lhs, onehot)


def place_rows(row, wide_ref, first, count):
    known = {}
    bits = [((row >> b) & 1) == 1 for b in range(6)]

    def at(level, y):
        if y < 0 or y > TILE - 1 + (1 << level) - 1:
            return None
        if level == 0:
            if (0, y) not in known:
                known[0, y] = wide_ref[pl.ds(y, KD, stride=TILE), :]
            return known[0, y]
        if (level, y) not in known:
            moved = at(level - 1, y - (1 << (level - 1)))
            kept = at(level - 1, y)
            zero = jnp.zeros((KD, COLS), F32)
            bit = bits[level - 1]
            known[level, y] = jnp.where(
                bit, zero if moved is None else moved, zero if kept is None else kept
            )
        return known[level, y]

    return [at(6, y) for y in range(first, first + count)]


def kernel(
    n_slab,
    n_frames,
    raw_ref,
    shift_ref,
    foot_ref,
    anchor_ref,
    block_ref,
    trace_ref,
    z_ref,
    res_ref,
    pkt_out,
    pkt_in,
    inbox,
    mom_out,
    mom_in,
    wide,
    image,
    rawx,
    mixed,
    corr,
    band,
    xrow,
    e1_send,
    e1_recv,
    e2_send,
    e2_recv,
    e3_send,
    e3_recv,
):
    me = lax.axis_index("slab")
    frame = lax.axis_index("frames")

    def slab_at(offset):
        return lax.rem(me + offset + 2 * n_slab, n_slab)

    def frame_at(offset):
        return lax.rem(frame + offset, n_frames)

    barrier = pltpu.get_barrier_semaphore()

    def greet_slab(i, carry):
        for sign in (1, -1):
            pl.semaphore_signal(
                barrier, 1, device_id={"slab": slab_at(sign * i)}, device_id_type=MESH
            )
        return carry

    def greet_frame(i, carry):
        pl.semaphore_signal(barrier, 1, device_id={"frames": frame_at(i)}, device_id_type=MESH)
        return carry

    lax.fori_loop(1, HALO + 1, greet_slab, 0)
    lax.fori_loop(1, n_frames, greet_frame, 0)

    foot = foot_ref[...]
    packed = jnp.zeros((4 * TILE, COLS), F32)
    for kk in range(8):
        piece = jnp.concatenate([foot[8 * g + kk] for g in range(4)], axis=0)
        spread = jnp.where(iota((TILE, COLS), 1) - kk * TILE == iota((TILE, COLS), 0), 1.0, 0.0)
        packed = packed + mm(piece, spread.astype(BF16))
    packed = packed.astype(BF16)
    own_row = (anchor_ref[:, 0:1] - (me * ROWS - RIM)) + jnp.zeros((KD, COLS), jnp.int32)
    own_col = (anchor_ref[:, 1:2] + jnp.zeros((KD, COLS), jnp.int32)).astype(F32)
    start = trace_ref[...]
    t_hi, t_rest = split(start)
    t_mid, t_lo = split(t_rest)
    lane = iota((KD, COLS), 1)
    small = jnp.where(lane == 0, own_row.astype(F32), 0.0)
    small = jnp.where(lane == 1, own_col, small)
    for i, part in enumerate((t_hi, t_mid, t_lo)):
        for t in range(2):
            small = jnp.where(lane == 2 + 2 * i + t, part[:, t : t + 1], small)
    for side, patch in ((0, 0), (1, 1)):
        mine = small
        for which in range(2):
            for t in range(2):
                value = jnp.full((KD, COLS), shift_ref[which, t, patch, 0], jnp.int32).astype(F32)
                mine = jnp.where(lane == 8 + 2 * which + t, value, mine)
        top = 0 if side == 0 else ROWS - 16
        for t in range(2):
            pkt_out[side, 16 * t : 16 * t + 16, :] = raw_ref[t, top : top + 16, :]
        pkt_out[side, 32:96, :] = packed
        pkt_out[side, 96:128, :] = mine.astype(BF16)

    pl.semaphore_wait(barrier, 2 * HALO + n_frames - 1)

    def packet(side):
        return pltpu.make_async_remote_copy(
            src_ref=pkt_out.at[side],
            dst_ref=pkt_in.at[1 - side],
            send_sem=e1_send.at[side],
            recv_sem=e1_recv.at[1 - side],
            device_id={"slab": slab_at(-1 if side == 0 else 1)},
            device_id_type=MESH,
        )

    to_left, to_right = packet(0), packet(1)
    to_left.start()
    to_right.start()

    image[...] = jnp.zeros(image.shape, BF16)
    place_columns(packed, own_col, wide)
    for y, value in enumerate(place_rows(own_row, wide, 0, EXT)):
        if value is not None:
            image[0:KD, y * COLS : (y + 1) * COLS] = value.astype(BF16)
    own = image[0:KD, :]
    gram_own = mm_nt(own, own)
    eye = iota((KD, KD), 0) == iota((KD, KD), 1)
    norm_sq = jnp.sum(jnp.where(eye, gram_own, 0.0), axis=0, keepdims=True)
    for t in range(2):
        rawx[t * 96 + 16 : t * 96 + 80, :] = raw_ref[t].astype(F32)

    to_left.wait()
    to_right.wait()

    smalls = []
    valid = []
    for side in range(2):
        inside = me > 0 if side == 0 else me < n_slab - 1
        keep = jnp.where(inside, 1.0, 0.0).astype(F32)
        valid.append(keep)
        info = pkt_in[side, 96:128, :].astype(F32) * keep
        smalls.append(info)
        place_columns(
            pkt_in[side, 32:96, :], info[:, 1:2] + jnp.zeros((KD, COLS), F32), wide
        )
        row = (info[:, 0:1] + jnp.zeros((KD, COLS), F32)).astype(jnp.int32)
        first = ROWS if side == 0 else 0
        low = 96 if side == 0 else 32
        for i, value in enumerate(place_rows(row, wide, first, 16)):
            if value is not None:
                y = i if side == 0 else ROWS + i
                image[low : low + KD, y * COLS : (y + 1) * COLS] = (value * keep).astype(BF16)
        for t in range(2):
            at = t * 96 + (0 if side == 0 else 80)
            rawx[at : at + 16, :] = pkt_in[side, 16 * t : 16 * t + 16, :].astype(F32) * keep
    gram_left = mm_nt(image[96:128, 0 : 16 * COLS], image[0:KD, 0 : 16 * COLS])
    gram_right = mm_nt(image[32:64, ROWS * COLS :], image[0:KD, ROWS * COLS :])

    for t in range(2):
        mixed[t * 96 : t * 96 + 88, :] = (
            0.75 * rawx[t * 96 + 4 : t * 96 + 92, :] + 0.25 * rawx[t * 96 + 5 : t * 96 + 93, :]
        )
        for y0, n in ((-RIM, RIM), (0, 32), (32, 32), (ROWS, RIM)):
            if 0 <= y0 < ROWS:
                down = jnp.full((n, COLS), shift_ref[0, t, y0 // 32, 0], jnp.int32).astype(F32)
                across = jnp.full((n, COLS), shift_ref[1, t, y0 // 32, 0], jnp.int32).astype(F32)
            else:
                info = smalls[0 if y0 < 0 else 1]
                down = jnp.broadcast_to(info[0:1, 8 + t : 9 + t], (n, COLS))
                across = jnp.broadcast_to(info[0:1, 10 + t : 11 + t], (n, COLS))
            picked = jnp.zeros((n, COLS), F32)
            for a in range(-3, 4):
                at = t * 96 + y0 + 12 + a
                picked = jnp.where(down == a, mixed[at : at + n, :], picked)
            place = iota((n, COLS), 1)
            moved = jnp.zeros((n, COLS), F32)
            for c in range(-3, 4):
                turned = picked if c == 0 else pltpu.roll(picked, (-c) % COLS, 1)
                within = (place + c >= 0) & (place + c < COLS)
                moved = jnp.where((across == c) & within, turned, moved)
            moved = moved.astype(BF16).astype(F32)
            if y0 < 0:
                moved = moved * valid[0]
            if y0 >= ROWS:
                moved = moved * valid[1]
            at = t * EXT + y0 + RIM
            corr[at : at + n, :] = moved
    corr[2 * EXT :, :] = jnp.zeros((6 * EXT, COLS), F32)
    frames_rows = jnp.concatenate([corr[pl.ds(y, 8, stride=EXT), :] for y in range(EXT)], axis=1)
    q = mm_nt(frames_rows.astype(BF16), image[0:KD, :])

    old = [start]
    for info in smalls:
        old.append(info[:, 2:4] + info[:, 4:6] + info[:, 6:8])
    grams = (gram_own, gram_left, gram_right)
    mine = inbox.at[HALO]
    mine[:, 0:32] = gram_left
    mine[:, 32:64] = gram_own
    mine[:, 64:96] = gram_right
    mine[:, 96:128] = jnp.zeros((KD, KD), F32)
    for t in range(2):
        rendered = sum(
            jnp.sum(gram * x[:, t : t + 1], axis=0, keepdims=True) for gram, x in zip(grams, old)
        )
        mine[t : t + 1, 96:128] = q[t : t + 1, :] - rendered
    mine[2:3, 96:128] = 1.0 / norm_sq
    mine[3:4, 96:128] = block_ref[...].astype(F32)

    def message(offset):
        slot = HALO - offset
        return pltpu.make_async_remote_copy(
            src_ref=inbox.at[HALO],
            dst_ref=inbox.at[slot],
            send_sem=e2_send.at[slot],
            recv_sem=e2_recv.at[slot],
            device_id={"slab": slab_at(offset)},
            device_id_type=MESH,
        )

    def send(i, carry):
        message(i).start()
        message(-i).start()
        return carry

    def arrive(i, carry):
        message(i).wait()
        message(-i).wait()
        return carry

    lax.fori_loop(1, HALO + 1, send, 0)

    lanes8 = iota((8, COLS), 1)
    wide_lane = iota((KD, COLS), 1)
    wide_row = iota((KD, COLS), 0)
    first_rows = []
    for x, low in zip(old, (0, 96, 32)):
        first_rows.append(
            [
                jnp.sum(
                    jnp.where(wide_lane - low == wide_row, x[:, t : t + 1], 0.0),
                    axis=0,
                    keepdims=True,
                )
                for t in range(2)
            ]
        )

    def rows_of(pair):
        sub = iota((8, COLS), 0)
        return jnp.where(sub == 0, pair[0], 0.0) + jnp.where(sub == 1, pair[1], 0.0)

    own_x, left_x, right_x = (rows_of(pair) for pair in first_rows)

    lax.fori_loop(1, HALO + 1, arrive, 0)

    def block_of_slot(slot, which, lane_chunk):
        value = inbox[slot]
        turn = (32 * (lane_chunk - which)) % COLS
        return value if turn == 0 else pltpu.roll(value, turn, 1)

    lane_chunk = wide_lane // 32
    scal = []
    for m in range(CHUNKS):
        keeps = []
        for i in range(4):
            slot = 4 * m + i
            if slot >= SLOTS:
                keeps.append(None)
                continue
            where = me + (slot - HALO)
            keeps.append(jnp.where((where >= 0) & (where < n_slab), 1.0, 0.0).astype(F32))
        tops = jnp.zeros((8, COLS), F32)
        for i in range(4):
            if keeps[i] is None:
                continue
            top = inbox[4 * m + i, 0:8, :]
            turn = (32 * (i - 3)) % COLS
            top = top if turn == 0 else pltpu.roll(top, turn, 1)
            tops = tops + jnp.where(lanes8 // 32 == i, top * keeps[i], 0.0)
        scal.append(tops)
        parts = []
        for rows in range(8):
            terms = []
            if rows < 4:
                terms = [(rows, 1), (rows + 1, 0), (rows - 1, 2)]
            elif rows == 4:
                terms = [(3, 2)]
            elif rows == 7:
                terms = [(0, 0)]
            total = jnp.zeros((KD, COLS), F32)
            for i, which in terms:
                if 0 <= i < 4 and keeps[i] is not None:
                    value = block_of_slot(4 * m + i, which, i) * keeps[i]
                    total = total + jnp.where(lane_chunk == i, value, 0.0)
            parts.append(total)
        for rows, total in enumerate(parts):
            hi, lo = split(total)
            band[m, rows * KD : (rows + 1) * KD, 0:COLS] = hi.astype(BF16)
            band[m, rows * KD : (rows + 1) * KD, COLS:] = lo.astype(BF16)

    state = list(scal)
    gains = [
        [
            jnp.where(tops[3:4, :] == float(b), tops[2:3, :], 0.0)
            for b in range(BLOCKS)
        ]
        for tops in scal
    ]
    total2 = jnp.where(lanes8 >= 96, left_x, 0.0)
    total3 = own_x + right_x
    for step in range(1, STEPS + 1):
        b = (step - 1) % BLOCKS
        low, high = max(step - 1, 0) // 4, min(2 * HALO + 1 - step, SLOTS - 1) // 4
        change = {m: state[m] * gains[m][b] for m in range(low, high + 1)}
        total2 = total2 + change[2]
        total3 = total3 + change[3]
        if step == STEPS:
            break
        zero = jnp.zeros((8, COLS), F32)
        for m in range(step // 4, (2 * HALO - step) // 4 + 1):
            beside = jnp.where(
                lanes8 >= 96,
                change.get(m - 1, zero),
                jnp.where(lanes8 < 32, change.get(m + 1, zero), 0.0),
            )
            a_hi, a_lo = split(change[m])
            b_hi, b_lo = split(beside)
            lhs = jnp.concatenate(
                [jnp.concatenate([a_hi, a_lo], axis=0), jnp.concatenate([b_hi, b_lo], axis=0)],
                axis=1,
            ).astype(BF16)
            out = mm(lhs, band[m])
            state[m] = state[m] - (out[0:8, 0:COLS] + out[8:16, 0:COLS] + out[0:8, COLS:])

    own_lane = lanes8 < 32
    two_rows = iota((8, COLS), 0) < 2
    final = jnp.where(own_lane & two_rows, total3, 0.0)
    mom_out[0:1, :] = jnp.sum(final, axis=0, keepdims=True)
    mom_out[1:2, :] = jnp.sum(final * final, axis=0, keepdims=True)
    mom_out[2:8, :] = jnp.zeros((6, COLS), F32)

    def moments(i):
        return pltpu.make_async_remote_copy(
            src_ref=mom_out,
            dst_ref=mom_in.at[n_frames - i],
            send_sem=e3_send.at[n_frames - i],
            recv_sem=e3_recv.at[n_frames - i],
            device_id={"frames": frame_at(i)},
            device_id_type=MESH,
        )

    def send_moments(i, carry):
        moments(i).start()
        return carry

    def arrive_moments(i, carry):
        moments(i).wait()
        return carry

    lax.fori_loop(1, n_frames, send_moments, 0)

    all_x = jnp.where(lanes8 < 64, total3, jnp.where(lanes8 >= 96, total2, 0.0))
    x_hi, x_lo = split(all_x)
    lhs = jnp.concatenate([x_hi, x_lo], axis=0).astype(BF16)
    pieces = (
        mm(lhs, image[:, RIM * COLS : 16 * COLS]),
        mm(lhs[:, 0:KD], image[0:KD, 16 * COLS : ROWS * COLS]),
        mm(lhs, image[:, ROWS * COLS : (ROWS + RIM) * COLS]),
    )
    y = 0
    for piece in pieces:
        rendered = piece[0:8, :] + piece[8:16, :]
        for i in range(piece.shape[1] // COLS):
            rows = corr[pl.ds(y + RIM, 8, stride=EXT), :] - rendered[:, i * COLS : (i + 1) * COLS]
            res_ref[pl.ds(y, 2, stride=ROWS), :] = rows[0:2, :]
            y += 1

    lax.fori_loop(1, n_frames, arrive_moments, 0)
    sums = mom_out[...]
    for i in range(1, n_frames):
        sums = sums + mom_in[i]
    count = 2 * n_frames
    mean = sums[0:1, :] / count
    square = sums[1:2, :] / count
    spread = square - mean * mean
    z_row = (total3[0:2, :] - mean) / jnp.sqrt(spread + EPSILON)
    pick = (wide_lane == wide_row) & (wide_lane < KD)
    cols = [
        jnp.sum(jnp.where(pick, z_row[t : t + 1, :], 0.0), axis=1, keepdims=True)
        for t in range(2)
    ]
    z_ref[:, 0:1] = cols[0]
    z_ref[:, 1:2] = cols[1]


def shards(n_slab, n_frames, raw_movie, shifts, footprints, anchors, block_of, init_traces):
    vmem = pl.BlockSpec(memory_space=pltpu.VMEM)
    smem = pl.BlockSpec(memory_space=pltpu.SMEM)
    dma = pltpu.SemaphoreType.DMA
    traces_z, residual = pl.pallas_call(
        functools.partial(kernel, n_slab, n_frames),
        out_shape=(
            jax.ShapeDtypeStruct((KD, 2), F32),
            jax.ShapeDtypeStruct((2 * ROWS, COLS), F32),
        ),
        in_specs=[vmem, smem, vmem, vmem, vmem, vmem],
        out_specs=(vmem, vmem),
        scratch_shapes=[
            pltpu.VMEM((2, 128, COLS), BF16),
            pltpu.VMEM((2, 128, COLS), BF16),
            pltpu.VMEM((SLOTS, KD, COLS), F32),
            pltpu.VMEM((8, COLS), F32),
            pltpu.VMEM((n_frames, 8, COLS), F32),
            pltpu.VMEM((KD * TILE, COLS), F32),
            pltpu.VMEM((128, EXT * COLS), BF16),
            pltpu.VMEM((192, COLS), F32),
            pltpu.VMEM((192, COLS), F32),
            pltpu.VMEM((8 * EXT, COLS), F32),
            pltpu.VMEM((CHUNKS, 256, 256), BF16),
            pltpu.VMEM((8, COLS), F32),
            dma((2,)),
            dma((2,)),
            dma((SLOTS,)),
            dma((SLOTS,)),
            dma((n_frames,)),
            dma((n_frames,)),
        ],
        compiler_params=pltpu.CompilerParams(collective_id=0, has_side_effects=True),
    )(raw_movie, shifts, footprints, anchors, block_of.reshape(1, KD), init_traces)
    return traces_z, residual.reshape(2, ROWS, COLS)


def solution(mesh):
    in_specs = (
        P("frames", "slab", None),
        P(None, "frames", "slab", None),
        P("slab", None, None),
        P("slab", None),
        P("slab"),
        P("slab", "frames"),
    )
    out_specs = (P("slab", "frames"), P("frames", "slab", None))
    body = functools.partial(shards, mesh.shape["slab"], mesh.shape["frames"])
    return jax.shard_map(body, mesh=mesh, in_specs=in_specs, out_specs=out_specs, check_vma=False)
```

```python
import functools

import jax
import jax.numpy as jnp
from jax import lax
from jax.experimental import pallas as pl
from jax.experimental.pallas import tpu as pltpu
from jax.sharding import PartitionSpec as P

ROWS = 64
COLS = 128
KD = 32
TILE = 16
RIM = 8
EXT = 80
BLOCKS = 4
SWEEPS = 3
STEPS = BLOCKS * SWEEPS
HALO = STEPS
SLOTS = 2 * HALO + 1
CHUNKS = (SLOTS + 3) // 4
EPSILON = 1e-05
MESH = pl.DeviceIdType.MESH
F32 = jnp.float32
BF16 = jnp.bfloat16
NT = (((1,), (1,)), ((), ()))


def iota(shape, dim):
    return lax.broadcasted_iota(jnp.int32, shape, dim)


def mm(a, b):
    return jnp.dot(a, b, preferred_element_type=F32)


def mm_nt(a, b):
    return lax.dot_general(a, b, NT, preferred_element_type=F32)


def split(x):
    hi = x.astype(BF16).astype(F32)
    return hi, x - hi


def column_of(row):
    square = iota((KD, KD), 0) == iota((KD, KD), 1)
    return jnp.sum(jnp.where(square, row, 0.0), axis=1, keepdims=True)


def tile_map():
    lane = iota((COLS, 8 * COLS), 1)
    return jnp.where(
        iota((COLS, 8 * COLS), 0) == (lane // COLS) * TILE + lane % TILE, 1.0, 0.0
    ).astype(BF16)


def place_columns(flat, col, tiles):
    stacked = jnp.concatenate([flat[:, 0:COLS], flat[:, COLS:]], axis=0)
    spread = mm(stacked, tiles)
    own_group = iota((KD, COLS), 1) // TILE == iota((KD, COLS), 0) % 8
    rows = [
        jnp.where(
            own_group,
            spread[KD * (i // 8) : KD * (i // 8) + KD, (i % 8) * COLS : (i % 8 + 1) * COLS],
            0.0,
        )
        for i in range(TILE)
    ]
    anchor = col + jnp.zeros((KD, COLS), F32)
    offset = (iota((8, TILE, COLS), 2) - iota((8, TILE, COLS), 1)).astype(F32)
    out = []
    for g in range(4):
        lhs = jnp.concatenate([r[8 * g : 8 * g + 8, :] for r in rows], axis=0).astype(BF16)
        place = jnp.broadcast_to(anchor[8 * g : 8 * g + 8, None, :], (8, TILE, COLS))
        onehot = jnp.where(place == offset, 1.0, 0.0).astype(BF16).reshape(COLS, COLS)
        out.append(mm(lhs, onehot))
    return [
        jnp.concatenate([out[g][8 * i : 8 * i + 8, :] for g in range(4)], axis=0)
        for i in range(TILE)
    ]


def place_rows(row, tile_rows, first, count):
    known = {}
    bits = [((row >> b) & 1) == 1 for b in range(6)]

    def at(level, y):
        if y < 0 or y > TILE - 1 + (1 << level) - 1:
            return None
        if level == 0:
            return tile_rows[y]
        if (level, y) not in known:
            moved = at(level - 1, y - (1 << (level - 1)))
            kept = at(level - 1, y)
            zero = jnp.zeros((KD, COLS), F32)
            bit = bits[level - 1]
            known[level, y] = jnp.where(
                bit, zero if moved is None else moved, zero if kept is None else kept
            )
        return known[level, y]

    return [at(6, y) for y in range(first, first + count)]


def kernel(
    n_slab,
    n_frames,
    raw_ref,
    shift_ref,
    foot_ref,
    anchor_ref,
    block_ref,
    trace_ref,
    z_ref,
    res_ref,
    pkt_out,
    pkt_in,
    inbox,
    mom_out,
    mom_in,
    image,
    rawx,
    mixed,
    corr,
    band,
    e1_send,
    e1_recv,
    e2_send,
    e2_recv,
    e3_send,
    e3_recv,
):
    me = lax.axis_index("slab")
    frame = lax.axis_index("frames")

    def slab_at(offset):
        return lax.rem(me + offset + 2 * n_slab, n_slab)

    def frame_at(offset):
        return lax.rem(frame + offset, n_frames)

    barrier = pltpu.get_barrier_semaphore()

    def greet_slab(i, carry):
        for sign in (1, -1):
            pl.semaphore_signal(
                barrier, 1, device_id={"slab": slab_at(sign * i)}, device_id_type=MESH
            )
        return carry

    def greet_frame(i, carry):
        pl.semaphore_signal(barrier, 1, device_id={"frames": frame_at(i)}, device_id_type=MESH)
        return carry

    lax.fori_loop(1, HALO + 1, greet_slab, 0)
    lax.fori_loop(1, n_frames, greet_frame, 0)

    eye = iota((KD, KD), 0) == iota((KD, KD), 1)
    flat = mm_nt(jnp.where(eye, 1.0, 0.0).astype(BF16), foot_ref[...]).astype(BF16)
    own_row = column_of((anchor_ref[0:1, :] - (me * ROWS - RIM)).astype(F32))
    own_col = column_of(anchor_ref[1:2, :].astype(F32))
    start = [column_of(trace_ref[t : t + 1, :]) for t in range(2)]
    lane = iota((KD, COLS), 1)
    small = jnp.where(lane == 0, own_row, 0.0)
    small = jnp.where(lane == 1, own_col, small)
    for t in range(2):
        t_hi, t_rest = split(start[t])
        t_mid, t_lo = split(t_rest)
        for i, part in enumerate((t_hi, t_mid, t_lo)):
            small = jnp.where(lane == 2 + 2 * i + t, part, small)
    for side, patch in ((0, 0), (1, 1)):
        mine = small
        for which in range(2):
            for t in range(2):
                value = jnp.full((KD, COLS), shift_ref[which, t, 0, patch], jnp.int32).astype(F32)
                mine = jnp.where(lane == 8 + 2 * which + t, value, mine)
        top = 0 if side == 0 else ROWS - 16
        for t in range(2):
            pkt_out[side, 16 * t : 16 * t + 16, :] = raw_ref[t, top : top + 16, :]
        pkt_out[side, 32:64, :] = flat[:, 0:COLS]
        pkt_out[side, 64:96, :] = flat[:, COLS:]
        pkt_out[side, 96:128, :] = mine.astype(BF16)

    pl.semaphore_wait(barrier, 2 * HALO + n_frames - 1)

    def packet(side):
        return pltpu.make_async_remote_copy(
            src_ref=pkt_out.at[side],
            dst_ref=pkt_in.at[1 - side],
            send_sem=e1_send.at[side],
            recv_sem=e1_recv.at[1 - side],
            device_id={"slab": slab_at(-1 if side == 0 else 1)},
            device_id_type=MESH,
        )

    to_left, to_right = packet(0), packet(1)
    to_left.start()
    to_right.start()

    image[...] = jnp.zeros(image.shape, BF16)
    tiles = tile_map()
    own_int = (own_row + jnp.zeros((KD, COLS), F32)).astype(jnp.int32)
    for y, value in enumerate(place_rows(own_int, place_columns(flat, own_col, tiles), 0, EXT)):
        if value is not None:
            image[0:KD, y * COLS : (y + 1) * COLS] = value.astype(BF16)
    own = image[0:KD, :]
    gram_own = mm_nt(own, own)
    norm_sq = jnp.sum(jnp.where(eye, gram_own, 0.0), axis=0, keepdims=True)
    for t in range(2):
        rawx[t * 96 + 16 : t * 96 + 80, :] = raw_ref[t].astype(F32)

    to_left.wait()
    to_right.wait()

    smalls = []
    valid = []
    for side in range(2):
        inside = me > 0 if side == 0 else me < n_slab - 1
        keep = jnp.where(inside, 1.0, 0.0).astype(F32)
        valid.append(keep)
        info = pkt_in[side, 96:128, :].astype(F32) * keep
        smalls.append(info)
        theirs = jnp.concatenate([pkt_in[side, 32:64, :], pkt_in[side, 64:96, :]], axis=1)
        wide = place_columns(theirs, info[:, 1:2], tiles)
        row = (info[:, 0:1] + jnp.zeros((KD, COLS), F32)).astype(jnp.int32)
        first = ROWS if side == 0 else 0
        low = 96 if side == 0 else 32
        for i, value in enumerate(place_rows(row, wide, first, 16)):
            if value is not None:
                y = i if side == 0 else ROWS + i
                image[low : low + KD, y * COLS : (y + 1) * COLS] = (value * keep).astype(BF16)
        for t in range(2):
            at = t * 96 + (0 if side == 0 else 80)
            rawx[at : at + 16, :] = pkt_in[side, 16 * t : 16 * t + 16, :].astype(F32) * keep
    gram_left = mm_nt(image[96:128, 0 : 16 * COLS], image[0:KD, 0 : 16 * COLS])
    gram_right = mm_nt(image[32:64, ROWS * COLS :], image[0:KD, ROWS * COLS :])

    for t in range(2):
        mixed[t * 96 : t * 96 + 88, :] = (
            0.75 * rawx[t * 96 + 4 : t * 96 + 92, :] + 0.25 * rawx[t * 96 + 5 : t * 96 + 93, :]
        )
        for y0, n in ((-RIM, RIM), (0, 32), (32, 32), (ROWS, RIM)):
            if 0 <= y0 < ROWS:
                down = jnp.full((n, COLS), shift_ref[0, t, 0, y0 // 32], jnp.int32).astype(F32)
                across = jnp.full((n, COLS), shift_ref[1, t, 0, y0 // 32], jnp.int32).astype(F32)
            else:
                info = smalls[0 if y0 < 0 else 1]
                down = jnp.broadcast_to(info[0:1, 8 + t : 9 + t], (n, COLS))
                across = jnp.broadcast_to(info[0:1, 10 + t : 11 + t], (n, COLS))
            picked = jnp.zeros((n, COLS), F32)
            for a in range(-3, 4):
                at = t * 96 + y0 + 12 + a
                picked = jnp.where(down == a, mixed[at : at + n, :], picked)
            place = iota((n, COLS), 1)
            moved = jnp.zeros((n, COLS), F32)
            for c in range(-3, 4):
                turned = picked if c == 0 else pltpu.roll(picked, (-c) % COLS, 1)
                within = (place + c >= 0) & (place + c < COLS)
                moved = jnp.where((across == c) & within, turned, moved)
            moved = moved.astype(BF16).astype(F32)
            if y0 < 0:
                moved = moved * valid[0]
            if y0 >= ROWS:
                moved = moved * valid[1]
            at = t * EXT + y0 + RIM
            corr[at : at + n, :] = moved
    corr[2 * EXT :, :] = jnp.zeros((6 * EXT, COLS), F32)
    frames_rows = jnp.concatenate([corr[pl.ds(y, 8, stride=EXT), :] for y in range(EXT)], axis=1)
    q = mm_nt(frames_rows.astype(BF16), image[0:KD, :])

    old = [start]
    for info in smalls:
        exact = info[:, 2:4] + info[:, 4:6] + info[:, 6:8]
        old.append([exact[:, t : t + 1] for t in range(2)])
    grams = (gram_own, gram_left, gram_right)
    mine = inbox.at[HALO]
    mine[:, 0:32] = gram_left
    mine[:, 32:64] = gram_own
    mine[:, 64:96] = gram_right
    mine[:, 96:128] = jnp.zeros((KD, KD), F32)
    for t in range(2):
        rendered = sum(
            jnp.sum(gram * x[t], axis=0, keepdims=True) for gram, x in zip(grams, old)
        )
        mine[t : t + 1, 96:128] = q[t : t + 1, :] - rendered
    mine[2:3, 96:128] = 1.0 / norm_sq
    mine[3:4, 96:128] = block_ref[...].astype(F32)

    def message(offset):
        slot = HALO - offset
        return pltpu.make_async_remote_copy(
            src_ref=inbox.at[HALO],
            dst_ref=inbox.at[slot],
            send_sem=e2_send.at[slot],
            recv_sem=e2_recv.at[slot],
            device_id={"slab": slab_at(offset)},
            device_id_type=MESH,
        )

    def send(i, carry):
        message(i).start()
        message(-i).start()
        return carry

    def arrive(i, carry):
        message(i).wait()
        message(-i).wait()
        return carry

    lax.fori_loop(1, HALO + 1, send, 0)

    lanes8 = iota((8, COLS), 1)
    wide_lane = iota((KD, COLS), 1)
    wide_row = iota((KD, COLS), 0)
    first_rows = []
    for x, low in zip(old, (0, 96, 32)):
        first_rows.append(
            [
                jnp.sum(
                    jnp.where(wide_lane - low == wide_row, x[t], 0.0),
                    axis=0,
                    keepdims=True,
                )
                for t in range(2)
            ]
        )

    def rows_of(pair):
        sub = iota((8, COLS), 0)
        return jnp.where(sub == 0, pair[0], 0.0) + jnp.where(sub == 1, pair[1], 0.0)

    own_x, left_x, right_x = (rows_of(pair) for pair in first_rows)

    lax.fori_loop(1, HALO + 1, arrive, 0)

    def block_of_slot(slot, which, lane_chunk):
        value = inbox[slot]
        turn = (32 * (lane_chunk - which)) % COLS
        return value if turn == 0 else pltpu.roll(value, turn, 1)

    lane_chunk = wide_lane // 32
    scal = []
    for m in range(CHUNKS):
        keeps = []
        for i in range(4):
            slot = 4 * m + i
            if slot >= SLOTS:
                keeps.append(None)
                continue
            where = me + (slot - HALO)
            keeps.append(jnp.where((where >= 0) & (where < n_slab), 1.0, 0.0).astype(F32))
        tops = jnp.zeros((8, COLS), F32)
        for i in range(4):
            if keeps[i] is None:
                continue
            top = inbox[4 * m + i, 0:8, :]
            turn = (32 * (i - 3)) % COLS
            top = top if turn == 0 else pltpu.roll(top, turn, 1)
            tops = tops + jnp.where(lanes8 // 32 == i, top * keeps[i], 0.0)
        scal.append(tops)
        parts = []
        for rows in range(8):
            terms = []
            if rows < 4:
                terms = [(rows, 1), (rows + 1, 0), (rows - 1, 2)]
            elif rows == 4:
                terms = [(3, 2)]
            elif rows == 7:
                terms = [(0, 0)]
            total = jnp.zeros((KD, COLS), F32)
            for i, which in terms:
                if 0 <= i < 4 and keeps[i] is not None:
                    value = block_of_slot(4 * m + i, which, i) * keeps[i]
                    total = total + jnp.where(lane_chunk == i, value, 0.0)
            parts.append(total)
        for rows, total in enumerate(parts):
            hi, lo = split(total)
            band[m, rows * KD : (rows + 1) * KD, 0:COLS] = hi.astype(BF16)
            band[m, rows * KD : (rows + 1) * KD, COLS:] = lo.astype(BF16)

    state = list(scal)
    gains = [
        [
            jnp.where(tops[3:4, :] == float(b), tops[2:3, :], 0.0)
            for b in range(BLOCKS)
        ]
        for tops in scal
    ]
    total2 = jnp.where(lanes8 >= 96, left_x, 0.0)
    total3 = own_x + right_x
    for step in range(1, STEPS + 1):
        b = (step - 1) % BLOCKS
        low, high = max(step - 1, 0) // 4, min(2 * HALO + 1 - step, SLOTS - 1) // 4
        change = {m: state[m] * gains[m][b] for m in range(low, high + 1)}
        total2 = total2 + change[2]
        total3 = total3 + change[3]
        if step == STEPS:
            break
        zero = jnp.zeros((8, COLS), F32)
        for m in range(step // 4, (2 * HALO - step) // 4 + 1):
            beside = jnp.where(
                lanes8 >= 96,
                change.get(m - 1, zero),
                jnp.where(lanes8 < 32, change.get(m + 1, zero), 0.0),
            )
            a_hi, a_lo = split(change[m])
            b_hi, b_lo = split(beside)
            lhs = jnp.concatenate(
                [jnp.concatenate([a_hi, a_lo], axis=0), jnp.concatenate([b_hi, b_lo], axis=0)],
                axis=1,
            ).astype(BF16)
            out = mm(lhs, band[m])
            state[m] = state[m] - (out[0:8, 0:COLS] + out[8:16, 0:COLS] + out[0:8, COLS:])

    own_lane = lanes8 < 32
    two_rows = iota((8, COLS), 0) < 2
    final = jnp.where(own_lane & two_rows, total3, 0.0)
    mom_out[0:1, :] = jnp.sum(final, axis=0, keepdims=True)
    mom_out[1:2, :] = jnp.sum(final * final, axis=0, keepdims=True)
    mom_out[2:8, :] = jnp.zeros((6, COLS), F32)

    def moments(i):
        return pltpu.make_async_remote_copy(
            src_ref=mom_out,
            dst_ref=mom_in.at[n_frames - i],
            send_sem=e3_send.at[n_frames - i],
            recv_sem=e3_recv.at[n_frames - i],
            device_id={"frames": frame_at(i)},
            device_id_type=MESH,
        )

    def send_moments(i, carry):
        moments(i).start()
        return carry

    def arrive_moments(i, carry):
        moments(i).wait()
        return carry

    lax.fori_loop(1, n_frames, send_moments, 0)

    all_x = jnp.where(lanes8 < 64, total3, jnp.where(lanes8 >= 96, total2, 0.0))
    x_hi, x_lo = split(all_x)
    lhs = jnp.concatenate([x_hi, x_lo], axis=0).astype(BF16)
    pieces = (
        mm(lhs, image[:, RIM * COLS : 16 * COLS]),
        mm(lhs[:, 0:KD], image[0:KD, 16 * COLS : ROWS * COLS]),
        mm(lhs, image[:, ROWS * COLS : (ROWS + RIM) * COLS]),
    )
    y = 0
    for piece in pieces:
        rendered = piece[0:8, :] + piece[8:16, :]
        for i in range(piece.shape[1] // COLS):
            rows = corr[pl.ds(y + RIM, 8, stride=EXT), :] - rendered[:, i * COLS : (i + 1) * COLS]
            res_ref[pl.ds(y, 2, stride=ROWS), :] = rows[0:2, :]
            y += 1

    lax.fori_loop(1, n_frames, arrive_moments, 0)
    sums = mom_out[...]
    for i in range(1, n_frames):
        sums = sums + mom_in[i]
    count = 2 * n_frames
    mean = sums[0:1, :] / count
    square = sums[1:2, :] / count
    spread = square - mean * mean
    z_row = (total3[0:2, :] - mean) / jnp.sqrt(spread + EPSILON)
    z_ref[...] = z_row[:, 0:KD]


def shards(n_slab, n_frames, raw_movie, shifts, footprints, anchors, block_of, init_traces):
    vmem = pl.BlockSpec(memory_space=pltpu.VMEM)
    smem = pl.BlockSpec(memory_space=pltpu.SMEM)
    dma = pltpu.SemaphoreType.DMA
    traces_z, residual = pl.pallas_call(
        functools.partial(kernel, n_slab, n_frames),
        out_shape=(
            jax.ShapeDtypeStruct((2, KD), F32),
            jax.ShapeDtypeStruct((2 * ROWS, COLS), F32),
        ),
        in_specs=[vmem, smem, vmem, vmem, vmem, vmem],
        out_specs=(vmem, vmem),
        scratch_shapes=[
            pltpu.VMEM((2, 128, COLS), BF16),
            pltpu.VMEM((2, 128, COLS), BF16),
            pltpu.VMEM((SLOTS, KD, COLS), F32),
            pltpu.VMEM((8, COLS), F32),
            pltpu.VMEM((n_frames, 8, COLS), F32),
            pltpu.VMEM((128, EXT * COLS), BF16),
            pltpu.VMEM((192, COLS), F32),
            pltpu.VMEM((192, COLS), F32),
            pltpu.VMEM((8 * EXT, COLS), F32),
            pltpu.VMEM((CHUNKS, 256, 256), BF16),
            dma((2,)),
            dma((2,)),
            dma((SLOTS,)),
            dma((SLOTS,)),
            dma((n_frames,)),
            dma((n_frames,)),
        ],
        compiler_params=pltpu.CompilerParams(collective_id=0, has_side_effects=True),
    )(
        raw_movie,
        shifts.transpose(0, 1, 3, 2),
        footprints.transpose(1, 2, 0).reshape(TILE * TILE, KD),
        anchors.T,
        block_of.reshape(1, KD),
        init_traces.T,
    )
    return traces_z.T, residual.reshape(2, ROWS, COLS)


def solution(mesh):
    in_specs = (
        P("frames", "slab", None),
        P(None, "frames", "slab", None),
        P("slab", None, None),
        P("slab", None),
        P("slab"),
        P("slab", "frames"),
    )
    out_specs = (P("slab", "frames"), P("frames", "slab", None))
    body = functools.partial(shards, mesh.shape["slab"], mesh.shape["frames"])
    return jax.shard_map(body, mesh=mesh, in_specs=in_specs, out_specs=out_specs, check_vma=False)
```

```python
import functools

import jax
import jax.numpy as jnp
from jax import lax
from jax.experimental import pallas as pl
from jax.experimental.pallas import tpu as pltpu
from jax.sharding import PartitionSpec as P

ROWS = 64
COLS = 128
KD = 32
TILE = 16
RIM = 8
EXT = 80
BLOCKS = 4
SWEEPS = 3
STEPS = BLOCKS * SWEEPS
HALO = STEPS
SLOTS = 2 * HALO + 1
CHUNKS = (SLOTS + 3) // 4
EPSILON = 1e-05
MESH = pl.DeviceIdType.MESH
F32 = jnp.float32
BF16 = jnp.bfloat16
NT = (((1,), (1,)), ((), ()))


def iota(shape, dim):
    return lax.broadcasted_iota(jnp.int32, shape, dim)


def mm(a, b):
    return jnp.dot(a, b, preferred_element_type=F32)


def mm_nt(a, b):
    return lax.dot_general(a, b, NT, preferred_element_type=F32)


def split(x):
    hi = x.astype(BF16).astype(F32)
    return hi, x - hi


def column_of(row):
    square = iota((KD, KD), 0) == iota((KD, KD), 1)
    return jnp.sum(jnp.where(square, row, 0.0), axis=1, keepdims=True)


def tile_map():
    lane = iota((COLS, 8 * COLS), 1)
    return jnp.where(
        iota((COLS, 8 * COLS), 0) == (lane // COLS) * TILE + lane % TILE, 1.0, 0.0
    ).astype(BF16)


def place_columns(flat, col, tiles):
    stacked = jnp.concatenate([flat[:, 0:COLS], flat[:, COLS:]], axis=0)
    spread = mm(stacked, tiles)
    own_group = iota((KD, COLS), 1) // TILE == iota((KD, COLS), 0) % 8
    rows = [
        jnp.where(
            own_group,
            spread[KD * (i // 8) : KD * (i // 8) + KD, (i % 8) * COLS : (i % 8 + 1) * COLS],
            0.0,
        )
        for i in range(TILE)
    ]
    anchor = col + jnp.zeros((KD, COLS), F32)
    offset = (iota((8, TILE, COLS), 2) - iota((8, TILE, COLS), 1)).astype(F32)
    out = []
    for g in range(4):
        lhs = jnp.concatenate([r[8 * g : 8 * g + 8, :] for r in rows], axis=0).astype(BF16)
        place = jnp.broadcast_to(anchor[8 * g : 8 * g + 8, None, :], (8, TILE, COLS))
        onehot = jnp.where(place == offset, 1.0, 0.0).astype(BF16).reshape(COLS, COLS)
        out.append(mm(lhs, onehot))
    return [
        jnp.concatenate([out[g][8 * i : 8 * i + 8, :] for g in range(4)], axis=0)
        for i in range(TILE)
    ]


def place_rows(row, tile_rows, first, count):
    known = {}
    bits = [((row >> b) & 1) == 1 for b in range(6)]

    def at(level, y):
        if y < 0 or y > TILE - 1 + (1 << level) - 1:
            return None
        if level == 0:
            return tile_rows[y]
        if (level, y) not in known:
            moved = at(level - 1, y - (1 << (level - 1)))
            kept = at(level - 1, y)
            zero = jnp.zeros((KD, COLS), F32)
            bit = bits[level - 1]
            known[level, y] = jnp.where(
                bit, zero if moved is None else moved, zero if kept is None else kept
            )
        return known[level, y]

    return [at(6, y) for y in range(first, first + count)]


def kernel(
    n_slab,
    n_frames,
    raw_ref,
    shift_ref,
    foot_ref,
    anchor_ref,
    block_ref,
    trace_ref,
    z_ref,
    res_ref,
    pkt_out,
    pkt_in,
    early,
    late,
    mom_out,
    mom_in,
    image,
    rawx,
    mixed,
    corr,
    band,
    square,
    e1_send,
    e1_recv,
    early_send,
    early_recv,
    late_send,
    late_recv,
    e3_send,
    e3_recv,
):
    me = lax.axis_index("slab")
    frame = lax.axis_index("frames")

    def slab_at(offset):
        return lax.rem(me + offset + 2 * n_slab, n_slab)

    def frame_at(offset):
        return lax.rem(frame + offset, n_frames)

    barrier = pltpu.get_barrier_semaphore()

    def greet_slab(i, carry):
        for sign in (1, -1):
            pl.semaphore_signal(
                barrier,
                1,
                device_id={"slab": slab_at(sign * (HALO + 1 - i))},
                device_id_type=MESH,
            )
        return carry

    def greet_frame(i, carry):
        pl.semaphore_signal(barrier, 1, device_id={"frames": frame_at(i)}, device_id_type=MESH)
        return carry

    lax.fori_loop(1, HALO + 1, greet_slab, 0)
    lax.fori_loop(1, n_frames, greet_frame, 0)

    eye = iota((KD, KD), 0) == iota((KD, KD), 1)
    flat = mm_nt(jnp.where(eye, 1.0, 0.0).astype(BF16), foot_ref[...]).astype(BF16)
    own_row = column_of((anchor_ref[0:1, :] - (me * ROWS - RIM)).astype(F32))
    own_col = column_of(anchor_ref[1:2, :].astype(F32))
    start = [column_of(trace_ref[t : t + 1, :]) for t in range(2)]
    lane = iota((KD, COLS), 1)
    small = jnp.where(lane == 0, own_row, 0.0)
    small = jnp.where(lane == 1, own_col, small)
    for t in range(2):
        t_hi, t_rest = split(start[t])
        t_mid, t_lo = split(t_rest)
        for i, part in enumerate((t_hi, t_mid, t_lo)):
            small = jnp.where(lane == 2 + 2 * i + t, part, small)
    for side, patch in ((0, 0), (1, 1)):
        mine = small
        for which in range(2):
            for t in range(2):
                value = jnp.full((KD, COLS), shift_ref[which, t, 0, patch], jnp.int32).astype(F32)
                mine = jnp.where(lane == 8 + 2 * which + t, value, mine)
        top = 0 if side == 0 else ROWS - 16
        for t in range(2):
            pkt_out[side, 16 * t : 16 * t + 16, :] = raw_ref[t, top : top + 16, :]
        pkt_out[side, 32:64, :] = flat[:, 0:COLS]
        pkt_out[side, 64:96, :] = flat[:, COLS:]
        pkt_out[side, 96:128, :] = mine.astype(BF16)

    pl.semaphore_wait(barrier, 2 * HALO + n_frames - 1)

    def packet(side):
        return pltpu.make_async_remote_copy(
            src_ref=pkt_out.at[side],
            dst_ref=pkt_in.at[1 - side],
            send_sem=e1_send.at[side],
            recv_sem=e1_recv.at[1 - side],
            device_id={"slab": slab_at(-1 if side == 0 else 1)},
            device_id_type=MESH,
        )

    to_left, to_right = packet(0), packet(1)
    to_left.start()
    to_right.start()

    image[...] = jnp.zeros(image.shape, BF16)
    tiles = tile_map()
    own_int = (own_row + jnp.zeros((KD, COLS), F32)).astype(jnp.int32)
    for y, value in enumerate(place_rows(own_int, place_columns(flat, own_col, tiles), 0, EXT)):
        if value is not None:
            image[0:KD, y * COLS : (y + 1) * COLS] = value.astype(BF16)
    own = image[0:KD, :]
    gram_own = mm_nt(own, own)
    norm_sq = jnp.sum(jnp.where(eye, gram_own, 0.0), axis=0, keepdims=True)
    def message(ref, send_sem, recv_sem, offset):
        slot = HALO - offset
        return pltpu.make_async_remote_copy(
            src_ref=ref.at[HALO],
            dst_ref=ref.at[slot],
            send_sem=send_sem.at[slot],
            recv_sem=recv_sem.at[slot],
            device_id={"slab": slab_at(offset)},
            device_id_type=MESH,
        )

    def send(ref, send_sem, recv_sem, i, carry):
        message(ref, send_sem, recv_sem, HALO + 1 - i).start()
        message(ref, send_sem, recv_sem, i - HALO - 1).start()
        return carry

    def arrive(ref, send_sem, recv_sem, i, carry):
        message(ref, send_sem, recv_sem, i).wait()
        message(ref, send_sem, recv_sem, -i).wait()
        return carry

    early_set = (early, early_send, early_recv)
    late_set = (late, late_send, late_recv)

    def compact(gram):
        square[:, 0:KD] = gram
        total = square[0:8, :]
        for g in range(1, 4):
            total = total + pltpu.roll(square[8 * g : 8 * g + 8, :], KD * g, 1)
        return total

    square[...] = jnp.zeros((KD, COLS), F32)
    early[HALO, 0:8, :] = compact(gram_own)
    early[HALO, 8:16, :] = jnp.zeros((8, COLS), F32)
    early[HALO, 8:9, 0:KD] = 1.0 / norm_sq
    early[HALO, 9:10, 0:KD] = block_ref[...].astype(F32)
    lax.fori_loop(1, HALO + 1, functools.partial(send, *early_set), 0)

    def mix(t, low, high):
        at = t * 96 + low + 4
        mixed[t * 96 + low : t * 96 + high, :] = (
            0.75 * rawx[at : at + high - low, :] + 0.25 * rawx[at + 1 : at + 1 + high - low, :]
        )

    def correct(t, y0, n, down, across, keep):
        picked = jnp.zeros((n, COLS), F32)
        for a in range(-3, 4):
            at = t * 96 + y0 + 12 + a
            picked = jnp.where(down == a, mixed[at : at + n, :], picked)
        place = iota((n, COLS), 1)
        moved = jnp.zeros((n, COLS), F32)
        for c in range(-3, 4):
            turned = picked if c == 0 else pltpu.roll(picked, (-c) % COLS, 1)
            within = (place + c >= 0) & (place + c < COLS)
            moved = jnp.where((across == c) & within, turned, moved)
        moved = moved.astype(BF16).astype(F32)
        if keep is not None:
            moved = moved * keep
        at = t * EXT + y0 + RIM
        corr[at : at + n, :] = moved

    def correct_own(t, y0, n):
        down, across = (
            jnp.full((n, COLS), shift_ref[which, t, 0, y0 // 32], jnp.int32).astype(F32)
            for which in range(2)
        )
        correct(t, y0, n, down, across, None)

    def frame_rows(low, high):
        rows = [corr[pl.ds(y, 8, stride=EXT), :] for y in range(low, high)]
        return jnp.concatenate(rows, axis=1).astype(BF16)

    corr[2 * EXT :, :] = jnp.zeros((6 * EXT, COLS), F32)
    for t in range(2):
        rawx[t * 96 + 16 : t * 96 + 80, :] = raw_ref[t].astype(F32)
        mix(t, 12, 75)
        correct_own(t, 8, 24)
        correct_own(t, 32, 24)
    q_inner = mm_nt(frame_rows(16, ROWS), image[0:KD, 16 * COLS : ROWS * COLS])

    to_left.wait()
    to_right.wait()

    smalls = []
    valid = []
    for side in range(2):
        inside = me > 0 if side == 0 else me < n_slab - 1
        keep = jnp.where(inside, 1.0, 0.0).astype(F32)
        valid.append(keep)
        info = pkt_in[side, 96:128, :].astype(F32) * keep
        smalls.append(info)
        theirs = jnp.concatenate([pkt_in[side, 32:64, :], pkt_in[side, 64:96, :]], axis=1)
        wide = place_columns(theirs, info[:, 1:2], tiles)
        row = (info[:, 0:1] + jnp.zeros((KD, COLS), F32)).astype(jnp.int32)
        first = ROWS if side == 0 else 0
        low = 96 if side == 0 else 32
        for i, value in enumerate(place_rows(row, wide, first, 16)):
            if value is not None:
                y = i if side == 0 else ROWS + i
                image[low : low + KD, y * COLS : (y + 1) * COLS] = (value * keep).astype(BF16)
        for t in range(2):
            at = t * 96 + (0 if side == 0 else 80)
            rawx[at : at + 16, :] = pkt_in[side, 16 * t : 16 * t + 16, :].astype(F32) * keep
    gram_left = mm_nt(image[96:128, 0 : 16 * COLS], image[0:KD, 0 : 16 * COLS])
    gram_right = mm_nt(image[32:64, ROWS * COLS :], image[0:KD, ROWS * COLS :])

    for t in range(2):
        mix(t, 0, 12)
        mix(t, 75, 88)
        correct_own(t, 0, RIM)
        correct_own(t, ROWS - RIM, RIM)
        for side, y0 in ((0, -RIM), (1, ROWS)):
            info = smalls[side]
            down = jnp.broadcast_to(info[0:1, 8 + t : 9 + t], (RIM, COLS))
            across = jnp.broadcast_to(info[0:1, 10 + t : 11 + t], (RIM, COLS))
            correct(t, y0, RIM, down, across, valid[side])
    q = (
        q_inner
        + mm_nt(frame_rows(0, 16), image[0:KD, 0 : 16 * COLS])
        + mm_nt(frame_rows(ROWS, EXT), image[0:KD, ROWS * COLS :])
    )

    old = [start]
    for info in smalls:
        exact = info[:, 2:4] + info[:, 4:6] + info[:, 6:8]
        old.append([exact[:, t : t + 1] for t in range(2)])
    grams = (gram_own, gram_left, gram_right)
    late[HALO, 0:8, :] = compact(gram_left)
    late[HALO, 8:16, :] = jnp.zeros((8, COLS), F32)
    for t in range(2):
        rendered = sum(
            jnp.sum(gram * x[t], axis=0, keepdims=True) for gram, x in zip(grams, old)
        )
        late[HALO, 8 + t : 9 + t, 0:KD] = q[t : t + 1, :] - rendered
    lax.fori_loop(1, HALO + 1, functools.partial(send, *late_set), 0)

    lanes8 = iota((8, COLS), 1)
    wide_lane = iota((KD, COLS), 1)
    wide_row = iota((KD, COLS), 0)
    first_rows = []
    for x, low in zip(old, (0, 96, 32)):
        first_rows.append(
            [
                jnp.sum(
                    jnp.where(wide_lane - low == wide_row, x[t], 0.0),
                    axis=0,
                    keepdims=True,
                )
                for t in range(2)
            ]
        )

    def rows_of(pair):
        sub = iota((8, COLS), 0)
        return jnp.where(sub == 0, pair[0], 0.0) + jnp.where(sub == 1, pair[1], 0.0)

    own_x, left_x, right_x = (rows_of(pair) for pair in first_rows)

    lax.fori_loop(1, HALO + 1, functools.partial(arrive, *early_set), 0)
    lax.fori_loop(1, HALO + 1, functools.partial(arrive, *late_set), 0)

    group8 = lanes8 // KD

    def turned(value, turn):
        return value if turn % COLS == 0 else pltpu.roll(value, turn % COLS, 1)

    def keep_of(slot):
        where = me + (slot - HALO)
        return jnp.where((where >= 0) & (where < n_slab), 1.0, 0.0).astype(F32)

    def spread(tile, i):
        parts = [jnp.where(group8 == i, turned(tile, KD * (i - g)), 0.0) for g in range(4)]
        return jnp.concatenate(parts, axis=0)

    zero32 = jnp.zeros((KD, COLS), F32)
    zero8 = jnp.zeros((8, COLS), F32)
    state, gains = [], []
    before = zero32
    for m in range(CHUNKS):
        p_rows, gain_rows, diag, links = zero8, zero8, [], []
        for i in range(4):
            slot = 4 * m + i
            if slot < SLOTS:
                keep = keep_of(slot)
                rows = jnp.where(group8 == i, turned(late[slot, 8:16, :], KD * i), 0.0)
                p_rows = p_rows + rows * keep
                rows = jnp.where(group8 == i, turned(early[slot, 8:16, :], KD * i), 0.0)
                gain_rows = gain_rows + rows * keep
                diag.append(spread(early[slot, 0:8, :] * keep, i))
            else:
                diag.append(zero32)
            after = slot + 1
            if after < SLOTS:
                links.append(spread(late[after, 0:8, :] * keep_of(after), (i + 1) % 4))
            else:
                links.append(zero32)
        state.append(p_rows)
        gains.append(
            [jnp.where(gain_rows[1:2, :] == float(b), gain_rows[0:1, :], 0.0) for b in range(BLOCKS)]
        )
        upper = jnp.concatenate(links, axis=0)
        lower = upper.T
        corner = lower[0:KD, :]
        blocks = []
        for i in range(4):
            value = diag[i]
            if i < 3:
                value = value + links[i]
            if i > 0:
                value = value + lower[KD * i : KD * i + KD, :]
            blocks.append(value)
        for at, value in ((0, blocks[0]), (1, blocks[1]), (2, blocks[2]), (3, blocks[3]), (4, corner), (5, zero32), (6, zero32), (7, before)):
            hi, lo = split(value)
            band[m, at * KD : (at + 1) * KD, 0:COLS] = hi.astype(BF16)
            band[m, at * KD : (at + 1) * KD, COLS:] = lo.astype(BF16)
        before = links[3]

    total2 = jnp.where(lanes8 >= 96, left_x, 0.0)
    total3 = own_x + right_x
    for step in range(1, STEPS + 1):
        b = (step - 1) % BLOCKS
        low, high = max(step - 1, 0) // 4, min(2 * HALO + 1 - step, SLOTS - 1) // 4
        change = {m: state[m] * gains[m][b] for m in range(low, high + 1)}
        total2 = total2 + change[2]
        total3 = total3 + change[3]
        if step == STEPS:
            break
        zero = jnp.zeros((8, COLS), F32)
        for m in range(step // 4, (2 * HALO - step) // 4 + 1):
            beside = jnp.where(
                lanes8 >= 96,
                change.get(m - 1, zero),
                jnp.where(lanes8 < 32, change.get(m + 1, zero), 0.0),
            )
            a_hi, a_lo = split(change[m])
            b_hi, b_lo = split(beside)
            lhs = jnp.concatenate(
                [jnp.concatenate([a_hi, a_lo], axis=0), jnp.concatenate([b_hi, b_lo], axis=0)],
                axis=1,
            ).astype(BF16)
            out = mm(lhs, band[m])
            state[m] = state[m] - (out[0:8, 0:COLS] + out[8:16, 0:COLS] + out[0:8, COLS:])

    own_lane = lanes8 < 32
    two_rows = iota((8, COLS), 0) < 2
    final = jnp.where(own_lane & two_rows, total3, 0.0)
    mom_out[0:1, :] = jnp.sum(final, axis=0, keepdims=True)
    mom_out[1:2, :] = jnp.sum(final * final, axis=0, keepdims=True)
    mom_out[2:8, :] = jnp.zeros((6, COLS), F32)

    def moments(i):
        return pltpu.make_async_remote_copy(
            src_ref=mom_out,
            dst_ref=mom_in.at[n_frames - i],
            send_sem=e3_send.at[n_frames - i],
            recv_sem=e3_recv.at[n_frames - i],
            device_id={"frames": frame_at(i)},
            device_id_type=MESH,
        )

    def send_moments(i, carry):
        moments(i).start()
        return carry

    def arrive_moments(i, carry):
        moments(i).wait()
        return carry

    lax.fori_loop(1, n_frames, send_moments, 0)

    all_x = jnp.where(lanes8 < 64, total3, jnp.where(lanes8 >= 96, total2, 0.0))
    x_hi, x_lo = split(all_x)
    lhs = jnp.concatenate([x_hi, x_lo], axis=0).astype(BF16)
    pieces = (
        mm(lhs, image[:, RIM * COLS : 16 * COLS]),
        mm(lhs[:, 0:KD], image[0:KD, 16 * COLS : ROWS * COLS]),
        mm(lhs, image[:, ROWS * COLS : (ROWS + RIM) * COLS]),
    )
    y = 0
    for piece in pieces:
        rendered = piece[0:8, :] + piece[8:16, :]
        for i in range(piece.shape[1] // COLS):
            rows = corr[pl.ds(y + RIM, 8, stride=EXT), :] - rendered[:, i * COLS : (i + 1) * COLS]
            res_ref[pl.ds(y, 2, stride=ROWS), :] = rows[0:2, :]
            y += 1

    lax.fori_loop(1, n_frames, arrive_moments, 0)
    sums = mom_out[...]
    for i in range(1, n_frames):
        sums = sums + mom_in[i]
    count = 2 * n_frames
    mean = sums[0:1, :] / count
    square = sums[1:2, :] / count
    spread = square - mean * mean
    z_row = (total3[0:2, :] - mean) / jnp.sqrt(spread + EPSILON)
    z_ref[...] = z_row[:, 0:KD]


def hand_on(z_ref, res_ref, z_out, res_out):
    z_out[...] = z_ref[...]
    res_out[...] = res_ref[...]


def shards(n_slab, n_frames, raw_movie, shifts, footprints, anchors, block_of, init_traces):
    vmem = pl.BlockSpec(memory_space=pltpu.VMEM)
    smem = pl.BlockSpec(memory_space=pltpu.SMEM)
    dma = pltpu.SemaphoreType.DMA
    traces_z, residual = pl.pallas_call(
        functools.partial(kernel, n_slab, n_frames),
        out_shape=(
            jax.ShapeDtypeStruct((2, KD), F32),
            jax.ShapeDtypeStruct((2 * ROWS, COLS), F32),
        ),
        in_specs=[vmem, smem, vmem, vmem, vmem, vmem],
        out_specs=(vmem, vmem),
        scratch_shapes=[
            pltpu.VMEM((2, 128, COLS), BF16),
            pltpu.VMEM((2, 128, COLS), BF16),
            pltpu.VMEM((SLOTS, 16, COLS), F32),
            pltpu.VMEM((SLOTS, 16, COLS), F32),
            pltpu.VMEM((8, COLS), F32),
            pltpu.VMEM((n_frames, 8, COLS), F32),
            pltpu.VMEM((128, EXT * COLS), BF16),
            pltpu.VMEM((192, COLS), F32),
            pltpu.VMEM((192, COLS), F32),
            pltpu.VMEM((8 * EXT, COLS), F32),
            pltpu.VMEM((CHUNKS, 256, 256), BF16),
            pltpu.VMEM((KD, COLS), F32),
            dma((2,)),
            dma((2,)),
            dma((SLOTS,)),
            dma((SLOTS,)),
            dma((SLOTS,)),
            dma((SLOTS,)),
            dma((n_frames,)),
            dma((n_frames,)),
        ],
        compiler_params=pltpu.CompilerParams(collective_id=0, has_side_effects=True),
    )(
        raw_movie,
        shifts.transpose(0, 1, 3, 2),
        footprints.transpose(1, 2, 0).reshape(TILE * TILE, KD),
        anchors.T,
        block_of.reshape(1, KD),
        init_traces.T,
    )
    traces_z, residual = pl.pallas_call(
        hand_on,
        out_shape=(
            jax.ShapeDtypeStruct((2, KD), F32),
            jax.ShapeDtypeStruct((2 * ROWS, COLS), F32),
        ),
    )(traces_z, residual)
    return traces_z.T, residual.reshape(2, ROWS, COLS)


def solution(mesh):
    in_specs = (
        P("frames", "slab", None),
        P(None, "frames", "slab", None),
        P("slab", None, None),
        P("slab", None),
        P("slab"),
        P("slab", "frames"),
    )
    out_specs = (P("slab", "frames"), P("frames", "slab", None))
    body = functools.partial(shards, mesh.shape["slab"], mesh.shape["frames"])
    return jax.shard_map(body, mesh=mesh, in_specs=in_specs, out_specs=out_specs, check_vma=False)
```

```python
import functools

import jax
import jax.numpy as jnp
from jax import lax
from jax.experimental import pallas as pl
from jax.experimental.pallas import tpu as pltpu
from jax.sharding import PartitionSpec as P

ROWS = 64
COLS = 128
KD = 32
TILE = 16
RIM = 8
EXT = 80
BLOCKS = 4
SWEEPS = 3
STEPS = BLOCKS * SWEEPS
HALO = STEPS
SLOTS = 2 * HALO + 1
CHUNKS = (SLOTS + 3) // 4
EPSILON = 1e-05
MESH = pl.DeviceIdType.MESH
F32 = jnp.float32
BF16 = jnp.bfloat16
NT = (((1,), (1,)), ((), ()))


def iota(shape, dim):
    return lax.broadcasted_iota(jnp.int32, shape, dim)


def mm(a, b):
    return jnp.dot(a, b, preferred_element_type=F32)


def mm_nt(a, b):
    return lax.dot_general(a, b, NT, preferred_element_type=F32)


def split(x):
    hi = x.astype(BF16).astype(F32)
    return hi, x - hi


def column_of(row):
    square = iota((KD, KD), 0) == iota((KD, KD), 1)
    return jnp.sum(jnp.where(square, row, 0.0), axis=1, keepdims=True)


def tile_map():
    lane = iota((COLS, 8 * COLS), 1)
    return jnp.where(
        iota((COLS, 8 * COLS), 0) == (lane // COLS) * TILE + lane % TILE, 1.0, 0.0
    ).astype(BF16)


def place_columns(flat, col, tiles):
    stacked = jnp.concatenate([flat[:, 0:COLS], flat[:, COLS:]], axis=0)
    spread = mm(stacked, tiles)
    own_group = iota((KD, COLS), 1) // TILE == iota((KD, COLS), 0) % 8
    rows = [
        jnp.where(
            own_group,
            spread[KD * (i // 8) : KD * (i // 8) + KD, (i % 8) * COLS : (i % 8 + 1) * COLS],
            0.0,
        )
        for i in range(TILE)
    ]
    anchor = col + jnp.zeros((KD, COLS), F32)
    offset = (iota((8, TILE, COLS), 2) - iota((8, TILE, COLS), 1)).astype(F32)
    out = []
    for g in range(4):
        lhs = jnp.concatenate([r[8 * g : 8 * g + 8, :] for r in rows], axis=0).astype(BF16)
        place = jnp.broadcast_to(anchor[8 * g : 8 * g + 8, None, :], (8, TILE, COLS))
        onehot = jnp.where(place == offset, 1.0, 0.0).astype(BF16).reshape(COLS, COLS)
        out.append(mm(lhs, onehot))
    return [
        jnp.concatenate([out[g][8 * i : 8 * i + 8, :] for g in range(4)], axis=0)
        for i in range(TILE)
    ]


def place_rows(row, tile_rows, first, count):
    known = {}
    bits = [((row >> b) & 1) == 1 for b in range(6)]

    def at(level, y):
        if y < 0 or y > TILE - 1 + (1 << level) - 1:
            return None
        if level == 0:
            return tile_rows[y]
        if (level, y) not in known:
            moved = at(level - 1, y - (1 << (level - 1)))
            kept = at(level - 1, y)
            zero = jnp.zeros((KD, COLS), F32)
            bit = bits[level - 1]
            known[level, y] = jnp.where(
                bit, zero if moved is None else moved, zero if kept is None else kept
            )
        return known[level, y]

    return [at(6, y) for y in range(first, first + count)]


def kernel(
    n_slab,
    n_frames,
    raw_ref,
    shift_ref,
    foot_ref,
    anchor_ref,
    block_ref,
    trace_ref,
    z_ref,
    res_ref,
    pkt_out,
    pkt_in,
    early,
    late,
    mom_out,
    mom_in,
    image,
    rawx,
    mixed,
    corr,
    band,
    square,
    e1_send,
    e1_recv,
    early_send,
    early_recv,
    late_send,
    late_recv,
    e3_send,
    e3_recv,
):
    me = lax.axis_index("slab")
    frame = lax.axis_index("frames")

    def slab_at(offset):
        return lax.rem(me + offset + 2 * n_slab, n_slab)

    def frame_at(offset):
        return lax.rem(frame + offset, n_frames)

    barrier = pltpu.get_barrier_semaphore()

    def greet_slab(i, carry):
        for sign in (1, -1):
            pl.semaphore_signal(
                barrier,
                1,
                device_id={"slab": slab_at(sign * (HALO + 1 - i))},
                device_id_type=MESH,
            )
        return carry

    def greet_frame(i, carry):
        pl.semaphore_signal(barrier, 1, device_id={"frames": frame_at(i)}, device_id_type=MESH)
        return carry

    lax.fori_loop(1, HALO + 1, greet_slab, 0)
    lax.fori_loop(1, n_frames, greet_frame, 0)

    eye = iota((KD, KD), 0) == iota((KD, KD), 1)
    flat = mm_nt(jnp.where(eye, 1.0, 0.0).astype(BF16), foot_ref[...]).astype(BF16)
    own_row = column_of((anchor_ref[0:1, :] - (me * ROWS - RIM)).astype(F32))
    own_col = column_of(anchor_ref[1:2, :].astype(F32))
    start = [column_of(trace_ref[t : t + 1, :]) for t in range(2)]
    lane = iota((KD, COLS), 1)
    small = jnp.where(lane == 0, own_row, 0.0)
    small = jnp.where(lane == 1, own_col, small)
    for t in range(2):
        t_hi, t_rest = split(start[t])
        t_mid, t_lo = split(t_rest)
        for i, part in enumerate((t_hi, t_mid, t_lo)):
            small = jnp.where(lane == 2 + 2 * i + t, part, small)
    for side, patch in ((0, 0), (1, 1)):
        mine = small
        for which in range(2):
            for t in range(2):
                value = jnp.full((KD, COLS), shift_ref[which, t, 0, patch], jnp.int32).astype(F32)
                mine = jnp.where(lane == 8 + 2 * which + t, value, mine)
        top = 0 if side == 0 else ROWS - 16
        for t in range(2):
            pkt_out[side, 16 * t : 16 * t + 16, :] = raw_ref[t, top : top + 16, :]
        pkt_out[side, 32:64, :] = flat[:, 0:COLS]
        pkt_out[side, 64:96, :] = flat[:, COLS:]
        pkt_out[side, 96:128, :] = mine.astype(BF16)

    pl.semaphore_wait(barrier, 2 * HALO + n_frames - 1)

    def packet(side):
        return pltpu.make_async_remote_copy(
            src_ref=pkt_out.at[side],
            dst_ref=pkt_in.at[1 - side],
            send_sem=e1_send.at[side],
            recv_sem=e1_recv.at[1 - side],
            device_id={"slab": slab_at(-1 if side == 0 else 1)},
            device_id_type=MESH,
        )

    to_left, to_right = packet(0), packet(1)
    to_left.start()
    to_right.start()

    image[...] = jnp.zeros(image.shape, BF16)
    tiles = tile_map()
    own_int = (own_row + jnp.zeros((KD, COLS), F32)).astype(jnp.int32)
    for y, value in enumerate(place_rows(own_int, place_columns(flat, own_col, tiles), 0, EXT)):
        if value is not None:
            image[0:KD, y * COLS : (y + 1) * COLS] = value.astype(BF16)
    own = image[0:KD, :]
    gram_own = mm_nt(own, own)
    norm_sq = jnp.sum(jnp.where(eye, gram_own, 0.0), axis=0, keepdims=True)
    def message(ref, send_sem, recv_sem, offset):
        slot = HALO - offset
        return pltpu.make_async_remote_copy(
            src_ref=ref.at[HALO, 0:10],
            dst_ref=ref.at[slot, 0:10],
            send_sem=send_sem.at[slot],
            recv_sem=recv_sem.at[slot],
            device_id={"slab": slab_at(offset)},
            device_id_type=MESH,
        )

    def send(ref, send_sem, recv_sem, i, carry):
        message(ref, send_sem, recv_sem, HALO + 1 - i).start()
        message(ref, send_sem, recv_sem, i - HALO - 1).start()
        return carry

    def arrive(ref, send_sem, recv_sem, i, carry):
        message(ref, send_sem, recv_sem, i).wait()
        message(ref, send_sem, recv_sem, -i).wait()
        return carry

    early_set = (early, early_send, early_recv)
    late_set = (late, late_send, late_recv)

    def compact(gram):
        square[:, 0:KD] = gram
        total = square[0:8, :]
        for g in range(1, 4):
            total = total + pltpu.roll(square[8 * g : 8 * g + 8, :], KD * g, 1)
        return total

    square[...] = jnp.zeros((KD, COLS), F32)
    early[HALO, 0:8, :] = compact(gram_own)
    early[HALO, 8:16, :] = jnp.zeros((8, COLS), F32)
    early[HALO, 8:9, 0:KD] = 1.0 / norm_sq
    early[HALO, 9:10, 0:KD] = block_ref[...].astype(F32)
    lax.fori_loop(1, HALO + 1, functools.partial(send, *early_set), 0)

    def mix(t, low, high):
        at = t * 96 + low + 4
        mixed[t * 96 + low : t * 96 + high, :] = (
            0.75 * rawx[at : at + high - low, :] + 0.25 * rawx[at + 1 : at + 1 + high - low, :]
        )

    def correct(t, y0, n, down, across, keep):
        picked = jnp.zeros((n, COLS), F32)
        for a in range(-3, 4):
            at = t * 96 + y0 + 12 + a
            picked = jnp.where(down == a, mixed[at : at + n, :], picked)
        place = iota((n, COLS), 1)
        moved = jnp.zeros((n, COLS), F32)
        for c in range(-3, 4):
            turned = picked if c == 0 else pltpu.roll(picked, (-c) % COLS, 1)
            within = (place + c >= 0) & (place + c < COLS)
            moved = jnp.where((across == c) & within, turned, moved)
        moved = moved.astype(BF16).astype(F32)
        if keep is not None:
            moved = moved * keep
        at = t * EXT + y0 + RIM
        corr[at : at + n, :] = moved

    def correct_own(t, y0, n):
        down, across = (
            jnp.full((n, COLS), shift_ref[which, t, 0, y0 // 32], jnp.int32).astype(F32)
            for which in range(2)
        )
        correct(t, y0, n, down, across, None)

    def frame_rows(low, high):
        rows = [corr[pl.ds(y, 8, stride=EXT), :] for y in range(low, high)]
        return jnp.concatenate(rows, axis=1).astype(BF16)

    corr[2 * EXT :, :] = jnp.zeros((6 * EXT, COLS), F32)
    for t in range(2):
        rawx[t * 96 + 16 : t * 96 + 80, :] = raw_ref[t].astype(F32)
        mix(t, 12, 75)
        correct_own(t, 8, 24)
        correct_own(t, 32, 24)
    q_inner = mm_nt(frame_rows(16, ROWS), image[0:KD, 16 * COLS : ROWS * COLS])

    to_left.wait()
    to_right.wait()

    smalls = []
    valid = []
    for side in range(2):
        inside = me > 0 if side == 0 else me < n_slab - 1
        keep = jnp.where(inside, 1.0, 0.0).astype(F32)
        valid.append(keep)
        info = pkt_in[side, 96:128, :].astype(F32) * keep
        smalls.append(info)
        theirs = jnp.concatenate([pkt_in[side, 32:64, :], pkt_in[side, 64:96, :]], axis=1)
        wide = place_columns(theirs, info[:, 1:2], tiles)
        row = (info[:, 0:1] + jnp.zeros((KD, COLS), F32)).astype(jnp.int32)
        first = ROWS if side == 0 else 0
        low = 96 if side == 0 else 32
        for i, value in enumerate(place_rows(row, wide, first, 16)):
            if value is not None:
                y = i if side == 0 else ROWS + i
                image[low : low + KD, y * COLS : (y + 1) * COLS] = (value * keep).astype(BF16)
        for t in range(2):
            at = t * 96 + (0 if side == 0 else 80)
            rawx[at : at + 16, :] = pkt_in[side, 16 * t : 16 * t + 16, :].astype(F32) * keep
    gram_left = mm_nt(image[96:128, 0 : 16 * COLS], image[0:KD, 0 : 16 * COLS])
    gram_right = mm_nt(image[32:64, ROWS * COLS :], image[0:KD, ROWS * COLS :])

    for t in range(2):
        mix(t, 0, 12)
        mix(t, 75, 88)
        correct_own(t, 0, RIM)
        correct_own(t, ROWS - RIM, RIM)
        for side, y0 in ((0, -RIM), (1, ROWS)):
            info = smalls[side]
            down = jnp.broadcast_to(info[0:1, 8 + t : 9 + t], (RIM, COLS))
            across = jnp.broadcast_to(info[0:1, 10 + t : 11 + t], (RIM, COLS))
            correct(t, y0, RIM, down, across, valid[side])
    q = (
        q_inner
        + mm_nt(frame_rows(0, 16), image[0:KD, 0 : 16 * COLS])
        + mm_nt(frame_rows(ROWS, EXT), image[0:KD, ROWS * COLS :])
    )

    old = [start]
    for info in smalls:
        exact = info[:, 2:4] + info[:, 4:6] + info[:, 6:8]
        old.append([exact[:, t : t + 1] for t in range(2)])
    grams = (gram_own, gram_left, gram_right)
    late[HALO, 0:8, :] = compact(gram_left)
    late[HALO, 8:16, :] = jnp.zeros((8, COLS), F32)
    for t in range(2):
        rendered = sum(
            jnp.sum(gram * x[t], axis=0, keepdims=True) for gram, x in zip(grams, old)
        )
        late[HALO, 8 + t : 9 + t, 0:KD] = q[t : t + 1, :] - rendered
    lax.fori_loop(1, HALO + 1, functools.partial(send, *late_set), 0)

    lanes8 = iota((8, COLS), 1)
    wide_lane = iota((KD, COLS), 1)
    wide_row = iota((KD, COLS), 0)
    first_rows = []
    for x, low in zip(old, (0, 96, 32)):
        first_rows.append(
            [
                jnp.sum(
                    jnp.where(wide_lane - low == wide_row, x[t], 0.0),
                    axis=0,
                    keepdims=True,
                )
                for t in range(2)
            ]
        )

    def rows_of(pair):
        sub = iota((8, COLS), 0)
        return jnp.where(sub == 0, pair[0], 0.0) + jnp.where(sub == 1, pair[1], 0.0)

    own_x, left_x, right_x = (rows_of(pair) for pair in first_rows)

    lax.fori_loop(1, HALO + 1, functools.partial(arrive, *early_set), 0)
    lax.fori_loop(1, HALO + 1, functools.partial(arrive, *late_set), 0)

    group8 = lanes8 // KD

    def turned(value, turn):
        return value if turn % COLS == 0 else pltpu.roll(value, turn % COLS, 1)

    def keep_of(slot):
        where = me + (slot - HALO)
        return jnp.where((where >= 0) & (where < n_slab), 1.0, 0.0).astype(F32)

    def spread(tile, i):
        parts = [jnp.where(group8 == i, turned(tile, KD * (i - g)), 0.0) for g in range(4)]
        return jnp.concatenate(parts, axis=0)

    zero32 = jnp.zeros((KD, COLS), F32)
    zero8 = jnp.zeros((8, COLS), F32)
    state, gains = [], []
    before = zero32
    for m in range(CHUNKS):
        p_rows, gain_rows, diag, links = zero8, zero8, [], []
        for i in range(4):
            slot = 4 * m + i
            if slot < SLOTS:
                keep = keep_of(slot)
                rows = jnp.where(group8 == i, turned(late[slot, 8:16, :], KD * i), 0.0)
                p_rows = p_rows + rows * keep
                rows = jnp.where(group8 == i, turned(early[slot, 8:16, :], KD * i), 0.0)
                gain_rows = gain_rows + rows * keep
                diag.append(spread(early[slot, 0:8, :] * keep, i))
            else:
                diag.append(zero32)
            after = slot + 1
            if after < SLOTS:
                links.append(spread(late[after, 0:8, :] * keep_of(after), (i + 1) % 4))
            else:
                links.append(zero32)
        state.append(p_rows)
        gains.append(
            [jnp.where(gain_rows[1:2, :] == float(b), gain_rows[0:1, :], 0.0) for b in range(BLOCKS)]
        )
        upper = jnp.concatenate(links, axis=0)
        lower = upper.T
        corner = lower[0:KD, :]
        blocks = []
        for i in range(4):
            value = diag[i]
            if i < 3:
                value = value + links[i]
            if i > 0:
                value = value + lower[KD * i : KD * i + KD, :]
            blocks.append(value)
        for at, value in ((0, blocks[0]), (1, blocks[1]), (2, blocks[2]), (3, blocks[3]), (4, corner), (5, zero32), (6, zero32), (7, before)):
            hi, lo = split(value)
            band[m, at * KD : (at + 1) * KD, 0:COLS] = hi.astype(BF16)
            band[m, at * KD : (at + 1) * KD, COLS:] = lo.astype(BF16)
        before = links[3]

    total2 = jnp.where(lanes8 >= 96, left_x, 0.0)
    total3 = own_x + right_x
    for step in range(1, STEPS + 1):
        b = (step - 1) % BLOCKS
        low, high = max(step - 1, 0) // 4, min(2 * HALO + 1 - step, SLOTS - 1) // 4
        change = {m: state[m] * gains[m][b] for m in range(low, high + 1)}
        total2 = total2 + change[2]
        total3 = total3 + change[3]
        if step == STEPS:
            break
        zero = jnp.zeros((8, COLS), F32)
        for m in range(step // 4, (2 * HALO - step) // 4 + 1):
            beside = jnp.where(
                lanes8 >= 96,
                change.get(m - 1, zero),
                jnp.where(lanes8 < 32, change.get(m + 1, zero), 0.0),
            )
            a_hi, a_lo = split(change[m])
            b_hi, b_lo = split(beside)
            lhs = jnp.concatenate(
                [jnp.concatenate([a_hi, a_lo], axis=0), jnp.concatenate([b_hi, b_lo], axis=0)],
                axis=1,
            ).astype(BF16)
            out = mm(lhs, band[m])
            state[m] = state[m] - (out[0:8, 0:COLS] + out[8:16, 0:COLS] + out[0:8, COLS:])

    own_lane = lanes8 < 32
    two_rows = iota((8, COLS), 0) < 2
    final = jnp.where(own_lane & two_rows, total3, 0.0)
    mom_out[0:1, :] = jnp.sum(final, axis=0, keepdims=True)
    mom_out[1:2, :] = jnp.sum(final * final, axis=0, keepdims=True)
    mom_out[2:8, :] = jnp.zeros((6, COLS), F32)

    def moments(i):
        return pltpu.make_async_remote_copy(
            src_ref=mom_out,
            dst_ref=mom_in.at[n_frames - i],
            send_sem=e3_send.at[n_frames - i],
            recv_sem=e3_recv.at[n_frames - i],
            device_id={"frames": frame_at(i)},
            device_id_type=MESH,
        )

    def send_moments(i, carry):
        moments(i).start()
        return carry

    def arrive_moments(i, carry):
        moments(i).wait()
        return carry

    lax.fori_loop(1, n_frames, send_moments, 0)

    all_x = jnp.where(lanes8 < 64, total3, jnp.where(lanes8 >= 96, total2, 0.0))
    x_hi, x_lo = split(all_x)
    lhs = jnp.concatenate([x_hi, x_lo], axis=0).astype(BF16)
    pieces = (
        mm(lhs, image[:, RIM * COLS : 16 * COLS]),
        mm(lhs[:, 0:KD], image[0:KD, 16 * COLS : ROWS * COLS]),
        mm(lhs, image[:, ROWS * COLS : (ROWS + RIM) * COLS]),
    )
    y = 0
    for piece in pieces:
        rendered = piece[0:8, :] + piece[8:16, :]
        for i in range(piece.shape[1] // COLS):
            rows = corr[pl.ds(y + RIM, 8, stride=EXT), :] - rendered[:, i * COLS : (i + 1) * COLS]
            res_ref[pl.ds(y, 2, stride=ROWS), :] = rows[0:2, :]
            y += 1

    lax.fori_loop(1, n_frames, arrive_moments, 0)
    sums = mom_out[...]
    for i in range(1, n_frames):
        sums = sums + mom_in[i]
    count = 2 * n_frames
    mean = sums[0:1, :] / count
    square = sums[1:2, :] / count
    spread = square - mean * mean
    z_row = (total3[0:2, :] - mean) / jnp.sqrt(spread + EPSILON)
    z_ref[...] = z_row[:, 0:KD]


def hand_on(z_ref, res_ref, z_out, res_out, sems):
    copies = [
        pltpu.make_async_copy(res_ref, res_out, sems.at[0]),
        pltpu.make_async_copy(z_ref, z_out, sems.at[1]),
    ]
    for copy in copies:
        copy.start()
    for copy in copies:
        copy.wait()


def shards(n_slab, n_frames, raw_movie, shifts, footprints, anchors, block_of, init_traces):
    vmem = pl.BlockSpec(memory_space=pltpu.VMEM)
    smem = pl.BlockSpec(memory_space=pltpu.SMEM)
    dma = pltpu.SemaphoreType.DMA
    traces_z, residual = pl.pallas_call(
        functools.partial(kernel, n_slab, n_frames),
        out_shape=(
            pltpu.VMEM((2, KD), F32),
            pltpu.VMEM((2 * ROWS, COLS), F32),
        ),
        in_specs=[vmem, smem, vmem, vmem, vmem, vmem],
        out_specs=(vmem, vmem),
        scratch_shapes=[
            pltpu.VMEM((2, 128, COLS), BF16),
            pltpu.VMEM((2, 128, COLS), BF16),
            pltpu.VMEM((SLOTS, 16, COLS), F32),
            pltpu.VMEM((SLOTS, 16, COLS), F32),
            pltpu.VMEM((8, COLS), F32),
            pltpu.VMEM((n_frames, 8, COLS), F32),
            pltpu.VMEM((128, EXT * COLS), BF16),
            pltpu.VMEM((192, COLS), F32),
            pltpu.VMEM((192, COLS), F32),
            pltpu.VMEM((8 * EXT, COLS), F32),
            pltpu.VMEM((CHUNKS, 256, 256), BF16),
            pltpu.VMEM((KD, COLS), F32),
            dma((2,)),
            dma((2,)),
            dma((SLOTS,)),
            dma((SLOTS,)),
            dma((SLOTS,)),
            dma((SLOTS,)),
            dma((n_frames,)),
            dma((n_frames,)),
        ],
        compiler_params=pltpu.CompilerParams(collective_id=0, has_side_effects=True),
    )(
        raw_movie,
        shifts.transpose(0, 1, 3, 2),
        footprints.transpose(1, 2, 0).reshape(TILE * TILE, KD),
        anchors.T,
        block_of.reshape(1, KD),
        init_traces.T,
    )
    traces_z = pltpu.with_memory_space_constraint(traces_z, pltpu.VMEM)
    residual = pltpu.with_memory_space_constraint(residual, pltpu.VMEM)
    traces_z, residual = pl.pallas_call(
        hand_on,
        out_shape=(
            jax.ShapeDtypeStruct((2, KD), F32),
            jax.ShapeDtypeStruct((2 * ROWS, COLS), F32),
        ),
        in_specs=[pl.BlockSpec(memory_space=pltpu.VMEM)] * 2,
        out_specs=(pl.BlockSpec(memory_space=pltpu.HBM),) * 2,
        scratch_shapes=[dma((2,))],
    )(traces_z, residual)
    return traces_z.T, residual.reshape(2, ROWS, COLS)


def solution(mesh):
    in_specs = (
        P("frames", "slab", None),
        P(None, "frames", "slab", None),
        P("slab", None, None),
        P("slab", None),
        P("slab"),
        P("slab", "frames"),
    )
    out_specs = (P("slab", "frames"), P("frames", "slab", None))
    body = functools.partial(shards, mesh.shape["slab"], mesh.shape["frames"])
    return jax.shard_map(body, mesh=mesh, in_specs=in_specs, out_specs=out_specs, check_vma=False)
```

```python
import functools

import jax
import jax.numpy as jnp
from jax import lax
from jax.experimental import pallas as pl
from jax.experimental.pallas import tpu as pltpu
from jax.sharding import PartitionSpec as P

ROWS = 64
COLS = 128
KD = 32
TILE = 16
RIM = 8
EXT = 80
BLOCKS = 4
SWEEPS = 3
STEPS = BLOCKS * SWEEPS
HALO = STEPS
SLOTS = 2 * HALO + 1
CHUNKS = (SLOTS + 3) // 4
EPSILON = 1e-05
MESH = pl.DeviceIdType.MESH
F32 = jnp.float32
BF16 = jnp.bfloat16
NT = (((1,), (1,)), ((), ()))


def iota(shape, dim):
    return lax.broadcasted_iota(jnp.int32, shape, dim)


def mm(a, b):
    return jnp.dot(a, b, preferred_element_type=F32)


def mm_nt(a, b):
    return lax.dot_general(a, b, NT, preferred_element_type=F32)


def split(x):
    hi = x.astype(BF16).astype(F32)
    return hi, x - hi


def column_of(row):
    square = iota((KD, KD), 0) == iota((KD, KD), 1)
    return jnp.sum(jnp.where(square, row, 0.0), axis=1, keepdims=True)


def tile_map():
    lane = iota((COLS, 8 * COLS), 1)
    return jnp.where(
        iota((COLS, 8 * COLS), 0) == (lane // COLS) * TILE + lane % TILE, 1.0, 0.0
    ).astype(BF16)


def place_columns(flat, col, tiles):
    stacked = jnp.concatenate([flat[:, 0:COLS], flat[:, COLS:]], axis=0)
    spread = mm(stacked, tiles)
    own_group = iota((KD, COLS), 1) // TILE == iota((KD, COLS), 0) % 8
    rows = [
        jnp.where(
            own_group,
            spread[KD * (i // 8) : KD * (i // 8) + KD, (i % 8) * COLS : (i % 8 + 1) * COLS],
            0.0,
        )
        for i in range(TILE)
    ]
    anchor = col + jnp.zeros((KD, COLS), F32)
    offset = (iota((8, TILE, COLS), 2) - iota((8, TILE, COLS), 1)).astype(F32)
    out = []
    for g in range(4):
        lhs = jnp.concatenate([r[8 * g : 8 * g + 8, :] for r in rows], axis=0).astype(BF16)
        place = jnp.broadcast_to(anchor[8 * g : 8 * g + 8, None, :], (8, TILE, COLS))
        onehot = jnp.where(place == offset, 1.0, 0.0).astype(BF16).reshape(COLS, COLS)
        out.append(mm(lhs, onehot))
    return [
        jnp.concatenate([out[g][8 * i : 8 * i + 8, :] for g in range(4)], axis=0)
        for i in range(TILE)
    ]


def place_rows(row, tile_rows, first, count):
    known = {}
    bits = [((row >> b) & 1) == 1 for b in range(6)]

    def at(level, y):
        if y < 0 or y > TILE - 1 + (1 << level) - 1:
            return None
        if level == 0:
            return tile_rows[y]
        if (level, y) not in known:
            moved = at(level - 1, y - (1 << (level - 1)))
            kept = at(level - 1, y)
            zero = jnp.zeros((KD, COLS), F32)
            bit = bits[level - 1]
            known[level, y] = jnp.where(
                bit, zero if moved is None else moved, zero if kept is None else kept
            )
        return known[level, y]

    return [at(6, y) for y in range(first, first + count)]


def kernel(
    n_slab,
    n_frames,
    raw_in,
    shift_in,
    foot_in,
    anchor_in,
    block_in,
    trace_in,
    z_ref,
    res_ref,
    raw_ref,
    shift_ref,
    foot_ref,
    anchor_ref,
    block_ref,
    trace_ref,
    fetched,
    pkt_out,
    pkt_in,
    early,
    late,
    mom_out,
    mom_in,
    image,
    rawx,
    mixed,
    corr,
    band,
    square,
    e1_send,
    e1_recv,
    early_send,
    early_recv,
    late_send,
    late_recv,
    e3_send,
    e3_recv,
):
    me = lax.axis_index("slab")
    frame = lax.axis_index("frames")

    def slab_at(offset):
        return lax.rem(me + offset + 2 * n_slab, n_slab)

    def frame_at(offset):
        return lax.rem(frame + offset, n_frames)

    barrier = pltpu.get_barrier_semaphore()

    def greet_slab(i, carry):
        for sign in (1, -1):
            pl.semaphore_signal(
                barrier,
                1,
                device_id={"slab": slab_at(sign * (HALO + 1 - i))},
                device_id_type=MESH,
            )
        return carry

    def greet_frame(i, carry):
        pl.semaphore_signal(barrier, 1, device_id={"frames": frame_at(i)}, device_id_type=MESH)
        return carry

    lax.fori_loop(1, HALO + 1, greet_slab, 0)
    lax.fori_loop(1, n_frames, greet_frame, 0)

    fetches = [
        pltpu.make_async_copy(source, target, fetched.at[i])
        for i, (source, target) in enumerate(
            (
                (foot_in, foot_ref),
                (anchor_in, anchor_ref),
                (trace_in, trace_ref),
                (raw_in, raw_ref),
                (shift_in, shift_ref),
                (block_in, block_ref),
            )
        )
    ]
    for fetch in fetches:
        fetch.start()
    for fetch in fetches:
        fetch.wait()

    eye = iota((KD, KD), 0) == iota((KD, KD), 1)
    flat = mm_nt(jnp.where(eye, 1.0, 0.0).astype(BF16), foot_ref[...]).astype(BF16)
    own_row = column_of((anchor_ref[0:1, :] - (me * ROWS - RIM)).astype(F32))
    own_col = column_of(anchor_ref[1:2, :].astype(F32))
    start = [column_of(trace_ref[t : t + 1, :]) for t in range(2)]
    lane = iota((KD, COLS), 1)
    small = jnp.where(lane == 0, own_row, 0.0)
    small = jnp.where(lane == 1, own_col, small)
    for t in range(2):
        t_hi, t_rest = split(start[t])
        t_mid, t_lo = split(t_rest)
        for i, part in enumerate((t_hi, t_mid, t_lo)):
            small = jnp.where(lane == 2 + 2 * i + t, part, small)
    for side, patch in ((0, 0), (1, 1)):
        mine = small
        for which in range(2):
            for t in range(2):
                value = jnp.full((KD, COLS), shift_ref[which, t, 0, patch], jnp.int32).astype(F32)
                mine = jnp.where(lane == 8 + 2 * which + t, value, mine)
        top = 0 if side == 0 else ROWS - 16
        for t in range(2):
            pkt_out[side, 16 * t : 16 * t + 16, :] = raw_ref[t, top : top + 16, :]
        pkt_out[side, 32:64, :] = flat[:, 0:COLS]
        pkt_out[side, 64:96, :] = flat[:, COLS:]
        pkt_out[side, 96:128, :] = mine.astype(BF16)

    pl.semaphore_wait(barrier, 2 * HALO + n_frames - 1)

    def packet(side):
        return pltpu.make_async_remote_copy(
            src_ref=pkt_out.at[side],
            dst_ref=pkt_in.at[1 - side],
            send_sem=e1_send.at[side],
            recv_sem=e1_recv.at[1 - side],
            device_id={"slab": slab_at(-1 if side == 0 else 1)},
            device_id_type=MESH,
        )

    to_left, to_right = packet(0), packet(1)
    to_left.start()
    to_right.start()

    image[...] = jnp.zeros(image.shape, BF16)
    tiles = tile_map()
    own_int = (own_row + jnp.zeros((KD, COLS), F32)).astype(jnp.int32)
    for y, value in enumerate(place_rows(own_int, place_columns(flat, own_col, tiles), 0, EXT)):
        if value is not None:
            image[0:KD, y * COLS : (y + 1) * COLS] = value.astype(BF16)
    own = image[0:KD, :]
    gram_own = mm_nt(own, own)
    norm_sq = jnp.sum(jnp.where(eye, gram_own, 0.0), axis=0, keepdims=True)
    def message(ref, send_sem, recv_sem, offset):
        slot = HALO - offset
        return pltpu.make_async_remote_copy(
            src_ref=ref.at[HALO, 0:10],
            dst_ref=ref.at[slot, 0:10],
            send_sem=send_sem.at[slot],
            recv_sem=recv_sem.at[slot],
            device_id={"slab": slab_at(offset)},
            device_id_type=MESH,
        )

    def send(ref, send_sem, recv_sem, i, carry):
        message(ref, send_sem, recv_sem, HALO + 1 - i).start()
        message(ref, send_sem, recv_sem, i - HALO - 1).start()
        return carry

    def arrive(ref, send_sem, recv_sem, i, carry):
        message(ref, send_sem, recv_sem, i).wait()
        message(ref, send_sem, recv_sem, -i).wait()
        return carry

    early_set = (early, early_send, early_recv)
    late_set = (late, late_send, late_recv)

    def compact(gram):
        square[:, 0:KD] = gram
        total = square[0:8, :]
        for g in range(1, 4):
            total = total + pltpu.roll(square[8 * g : 8 * g + 8, :], KD * g, 1)
        return total

    square[...] = jnp.zeros((KD, COLS), F32)
    early[HALO, 0:8, :] = compact(gram_own)
    early[HALO, 8:16, :] = jnp.zeros((8, COLS), F32)
    early[HALO, 8:9, 0:KD] = 1.0 / norm_sq
    early[HALO, 9:10, 0:KD] = block_ref[...].astype(F32)
    lax.fori_loop(1, HALO + 1, functools.partial(send, *early_set), 0)

    def mix(t, low, high):
        at = t * 96 + low + 4
        mixed[t * 96 + low : t * 96 + high, :] = (
            0.75 * rawx[at : at + high - low, :] + 0.25 * rawx[at + 1 : at + 1 + high - low, :]
        )

    def correct(t, y0, n, down, across, keep):
        picked = jnp.zeros((n, COLS), F32)
        for a in range(-3, 4):
            at = t * 96 + y0 + 12 + a
            picked = jnp.where(down == a, mixed[at : at + n, :], picked)
        place = iota((n, COLS), 1)
        moved = jnp.zeros((n, COLS), F32)
        for c in range(-3, 4):
            turned = picked if c == 0 else pltpu.roll(picked, (-c) % COLS, 1)
            within = (place + c >= 0) & (place + c < COLS)
            moved = jnp.where((across == c) & within, turned, moved)
        moved = moved.astype(BF16).astype(F32)
        if keep is not None:
            moved = moved * keep
        at = t * EXT + y0 + RIM
        corr[at : at + n, :] = moved

    def correct_own(t, y0, n):
        down, across = (
            jnp.full((n, COLS), shift_ref[which, t, 0, y0 // 32], jnp.int32).astype(F32)
            for which in range(2)
        )
        correct(t, y0, n, down, across, None)

    def frame_rows(low, high):
        rows = [corr[pl.ds(y, 8, stride=EXT), :] for y in range(low, high)]
        return jnp.concatenate(rows, axis=1).astype(BF16)

    corr[2 * EXT :, :] = jnp.zeros((6 * EXT, COLS), F32)
    for t in range(2):
        rawx[t * 96 + 16 : t * 96 + 80, :] = raw_ref[t].astype(F32)
        mix(t, 12, 75)
        correct_own(t, 8, 24)
        correct_own(t, 32, 24)
    q_inner = mm_nt(frame_rows(16, ROWS), image[0:KD, 16 * COLS : ROWS * COLS])

    to_left.wait()
    to_right.wait()

    smalls = []
    valid = []
    for side in range(2):
        inside = me > 0 if side == 0 else me < n_slab - 1
        keep = jnp.where(inside, 1.0, 0.0).astype(F32)
        valid.append(keep)
        info = pkt_in[side, 96:128, :].astype(F32) * keep
        smalls.append(info)
        theirs = jnp.concatenate([pkt_in[side, 32:64, :], pkt_in[side, 64:96, :]], axis=1)
        wide = place_columns(theirs, info[:, 1:2], tiles)
        row = (info[:, 0:1] + jnp.zeros((KD, COLS), F32)).astype(jnp.int32)
        first = ROWS if side == 0 else 0
        low = 96 if side == 0 else 32
        for i, value in enumerate(place_rows(row, wide, first, 16)):
            if value is not None:
                y = i if side == 0 else ROWS + i
                image[low : low + KD, y * COLS : (y + 1) * COLS] = (value * keep).astype(BF16)
        for t in range(2):
            at = t * 96 + (0 if side == 0 else 80)
            rawx[at : at + 16, :] = pkt_in[side, 16 * t : 16 * t + 16, :].astype(F32) * keep
    gram_left = mm_nt(image[96:128, 0 : 16 * COLS], image[0:KD, 0 : 16 * COLS])
    gram_right = mm_nt(image[32:64, ROWS * COLS :], image[0:KD, ROWS * COLS :])

    for t in range(2):
        mix(t, 0, 12)
        mix(t, 75, 88)
        correct_own(t, 0, RIM)
        correct_own(t, ROWS - RIM, RIM)
        for side, y0 in ((0, -RIM), (1, ROWS)):
            info = smalls[side]
            down = jnp.broadcast_to(info[0:1, 8 + t : 9 + t], (RIM, COLS))
            across = jnp.broadcast_to(info[0:1, 10 + t : 11 + t], (RIM, COLS))
            correct(t, y0, RIM, down, across, valid[side])
    q = (
        q_inner
        + mm_nt(frame_rows(0, 16), image[0:KD, 0 : 16 * COLS])
        + mm_nt(frame_rows(ROWS, EXT), image[0:KD, ROWS * COLS :])
    )

    old = [start]
    for info in smalls:
        exact = info[:, 2:4] + info[:, 4:6] + info[:, 6:8]
        old.append([exact[:, t : t + 1] for t in range(2)])
    grams = (gram_own, gram_left, gram_right)
    late[HALO, 0:8, :] = compact(gram_left)
    late[HALO, 8:16, :] = jnp.zeros((8, COLS), F32)
    for t in range(2):
        rendered = sum(
            jnp.sum(gram * x[t], axis=0, keepdims=True) for gram, x in zip(grams, old)
        )
        late[HALO, 8 + t : 9 + t, 0:KD] = q[t : t + 1, :] - rendered
    lax.fori_loop(1, HALO + 1, functools.partial(send, *late_set), 0)

    lanes8 = iota((8, COLS), 1)
    wide_lane = iota((KD, COLS), 1)
    wide_row = iota((KD, COLS), 0)
    first_rows = []
    for x, low in zip(old, (0, 96, 32)):
        first_rows.append(
            [
                jnp.sum(
                    jnp.where(wide_lane - low == wide_row, x[t], 0.0),
                    axis=0,
                    keepdims=True,
                )
                for t in range(2)
            ]
        )

    def rows_of(pair):
        sub = iota((8, COLS), 0)
        return jnp.where(sub == 0, pair[0], 0.0) + jnp.where(sub == 1, pair[1], 0.0)

    own_x, left_x, right_x = (rows_of(pair) for pair in first_rows)

    lax.fori_loop(1, HALO + 1, functools.partial(arrive, *early_set), 0)
    lax.fori_loop(1, HALO + 1, functools.partial(arrive, *late_set), 0)

    group8 = lanes8 // KD

    def turned(value, turn):
        return value if turn % COLS == 0 else pltpu.roll(value, turn % COLS, 1)

    def keep_of(slot):
        where = me + (slot - HALO)
        return jnp.where((where >= 0) & (where < n_slab), 1.0, 0.0).astype(F32)

    def spread(tile, i):
        parts = [jnp.where(group8 == i, turned(tile, KD * (i - g)), 0.0) for g in range(4)]
        return jnp.concatenate(parts, axis=0)

    zero32 = jnp.zeros((KD, COLS), F32)
    zero8 = jnp.zeros((8, COLS), F32)
    state, gains = [], []
    before = zero32
    for m in range(CHUNKS):
        p_rows, gain_rows, diag, links = zero8, zero8, [], []
        for i in range(4):
            slot = 4 * m + i
            if slot < SLOTS:
                keep = keep_of(slot)
                rows = jnp.where(group8 == i, turned(late[slot, 8:16, :], KD * i), 0.0)
                p_rows = p_rows + rows * keep
                rows = jnp.where(group8 == i, turned(early[slot, 8:16, :], KD * i), 0.0)
                gain_rows = gain_rows + rows * keep
                diag.append(spread(early[slot, 0:8, :] * keep, i))
            else:
                diag.append(zero32)
            after = slot + 1
            if after < SLOTS:
                links.append(spread(late[after, 0:8, :] * keep_of(after), (i + 1) % 4))
            else:
                links.append(zero32)
        state.append(p_rows)
        gains.append(
            [jnp.where(gain_rows[1:2, :] == float(b), gain_rows[0:1, :], 0.0) for b in range(BLOCKS)]
        )
        upper = jnp.concatenate(links, axis=0)
        lower = upper.T
        corner = lower[0:KD, :]
        blocks = []
        for i in range(4):
            value = diag[i]
            if i < 3:
                value = value + links[i]
            if i > 0:
                value = value + lower[KD * i : KD * i + KD, :]
            blocks.append(value)
        for at, value in ((0, blocks[0]), (1, blocks[1]), (2, blocks[2]), (3, blocks[3]), (4, corner), (5, zero32), (6, zero32), (7, before)):
            hi, lo = split(value)
            band[m, at * KD : (at + 1) * KD, 0:COLS] = hi.astype(BF16)
            band[m, at * KD : (at + 1) * KD, COLS:] = lo.astype(BF16)
        before = links[3]

    total2 = jnp.where(lanes8 >= 96, left_x, 0.0)
    total3 = own_x + right_x
    for step in range(1, STEPS + 1):
        b = (step - 1) % BLOCKS
        low, high = max(step - 1, 0) // 4, min(2 * HALO + 1 - step, SLOTS - 1) // 4
        change = {m: state[m] * gains[m][b] for m in range(low, high + 1)}
        total2 = total2 + change[2]
        total3 = total3 + change[3]
        if step == STEPS:
            break
        zero = jnp.zeros((8, COLS), F32)
        for m in range(step // 4, (2 * HALO - step) // 4 + 1):
            beside = jnp.where(
                lanes8 >= 96,
                change.get(m - 1, zero),
                jnp.where(lanes8 < 32, change.get(m + 1, zero), 0.0),
            )
            a_hi, a_lo = split(change[m])
            b_hi, b_lo = split(beside)
            lhs = jnp.concatenate(
                [jnp.concatenate([a_hi, a_lo], axis=0), jnp.concatenate([b_hi, b_lo], axis=0)],
                axis=1,
            ).astype(BF16)
            out = mm(lhs, band[m])
            state[m] = state[m] - (out[0:8, 0:COLS] + out[8:16, 0:COLS] + out[0:8, COLS:])

    own_lane = lanes8 < 32
    two_rows = iota((8, COLS), 0) < 2
    final = jnp.where(own_lane & two_rows, total3, 0.0)
    mom_out[0:1, :] = jnp.sum(final, axis=0, keepdims=True)
    mom_out[1:2, :] = jnp.sum(final * final, axis=0, keepdims=True)

    def moments(i):
        return pltpu.make_async_remote_copy(
            src_ref=mom_out,
            dst_ref=mom_in.at[n_frames - i],
            send_sem=e3_send.at[n_frames - i],
            recv_sem=e3_recv.at[n_frames - i],
            device_id={"frames": frame_at(i)},
            device_id_type=MESH,
        )

    def send_moments(i, carry):
        moments(i).start()
        return carry

    def arrive_moments(i, carry):
        moments(i).wait()
        return carry

    lax.fori_loop(1, n_frames, send_moments, 0)

    all_x = jnp.where(lanes8 < 64, total3, jnp.where(lanes8 >= 96, total2, 0.0))
    x_hi, x_lo = split(all_x)
    lhs = jnp.concatenate([x_hi, x_lo], axis=0).astype(BF16)
    pieces = (
        mm(lhs, image[:, RIM * COLS : 16 * COLS]),
        mm(lhs[:, 0:KD], image[0:KD, 16 * COLS : ROWS * COLS]),
        mm(lhs, image[:, ROWS * COLS : (ROWS + RIM) * COLS]),
    )
    y = 0
    for piece in pieces:
        rendered = piece[0:8, :] + piece[8:16, :]
        for i in range(piece.shape[1] // COLS):
            rows = corr[pl.ds(y + RIM, 8, stride=EXT), :] - rendered[:, i * COLS : (i + 1) * COLS]
            res_ref[pl.ds(y, 2, stride=ROWS), :] = rows[0:2, :]
            y += 1

    lax.fori_loop(1, n_frames, arrive_moments, 0)
    sums = mom_out[...]
    for i in range(1, n_frames):
        sums = sums + mom_in[i]
    count = 2 * n_frames
    mean = sums[0:1, :] / count
    square = sums[1:2, :] / count
    spread = square - mean * mean
    z_row = (total3[0:2, :] - mean) / jnp.sqrt(spread + EPSILON)
    z_ref[...] = z_row[:, 0:KD]


def hand_on(z_ref, res_ref, z_out, res_out, sems):
    copies = [
        pltpu.make_async_copy(res_ref, res_out, sems.at[0]),
        pltpu.make_async_copy(z_ref, z_out, sems.at[1]),
    ]
    for copy in copies:
        copy.start()
    for copy in copies:
        copy.wait()


def shards(n_slab, n_frames, raw_movie, shifts, footprints, anchors, block_of, init_traces):
    vmem = pl.BlockSpec(memory_space=pltpu.VMEM)
    dma = pltpu.SemaphoreType.DMA
    traces_z, residual = pl.pallas_call(
        functools.partial(kernel, n_slab, n_frames),
        out_shape=(
            pltpu.VMEM((2, KD), F32),
            pltpu.VMEM((2 * ROWS, COLS), F32),
        ),
        in_specs=[pl.BlockSpec(memory_space=pl.ANY)] * 6,
        out_specs=(vmem, vmem),
        scratch_shapes=[
            pltpu.VMEM((2, ROWS, COLS), BF16),
            pltpu.SMEM((2, 2, 1, 2), jnp.int32),
            pltpu.VMEM((TILE * TILE, KD), BF16),
            pltpu.VMEM((2, KD), jnp.int32),
            pltpu.VMEM((1, KD), jnp.int32),
            pltpu.VMEM((2, KD), F32),
            dma((6,)),
            pltpu.VMEM((2, 128, COLS), BF16),
            pltpu.VMEM((2, 128, COLS), BF16),
            pltpu.VMEM((SLOTS, 16, COLS), F32),
            pltpu.VMEM((SLOTS, 16, COLS), F32),
            pltpu.VMEM((2, COLS), F32),
            pltpu.VMEM((n_frames, 2, COLS), F32),
            pltpu.VMEM((128, EXT * COLS), BF16),
            pltpu.VMEM((192, COLS), F32),
            pltpu.VMEM((192, COLS), F32),
            pltpu.VMEM((8 * EXT, COLS), F32),
            pltpu.VMEM((CHUNKS, 256, 256), BF16),
            pltpu.VMEM((KD, COLS), F32),
            dma((2,)),
            dma((2,)),
            dma((SLOTS,)),
            dma((SLOTS,)),
            dma((SLOTS,)),
            dma((SLOTS,)),
            dma((n_frames,)),
            dma((n_frames,)),
        ],
        compiler_params=pltpu.CompilerParams(collective_id=0, has_side_effects=True),
    )(
        raw_movie,
        shifts.transpose(0, 1, 3, 2),
        footprints.transpose(1, 2, 0).reshape(TILE * TILE, KD),
        anchors.T,
        block_of.reshape(1, KD),
        init_traces.T,
    )
    traces_z = pltpu.with_memory_space_constraint(traces_z, pltpu.VMEM)
    residual = pltpu.with_memory_space_constraint(residual, pltpu.VMEM)
    traces_z, residual = pl.pallas_call(
        hand_on,
        out_shape=(
            jax.ShapeDtypeStruct((2, KD), F32),
            jax.ShapeDtypeStruct((2 * ROWS, COLS), F32),
        ),
        in_specs=[pl.BlockSpec(memory_space=pltpu.VMEM)] * 2,
        out_specs=(pl.BlockSpec(memory_space=pltpu.HBM),) * 2,
        scratch_shapes=[dma((2,))],
    )(traces_z, residual)
    return traces_z.T, residual.reshape(2, ROWS, COLS)


def solution(mesh):
    in_specs = (
        P("frames", "slab", None),
        P(None, "frames", "slab", None),
        P("slab", None, None),
        P("slab", None),
        P("slab"),
        P("slab", "frames"),
    )
    out_specs = (P("slab", "frames"), P("frames", "slab", None))
    body = functools.partial(shards, mesh.shape["slab"], mesh.shape["frames"])
    return jax.shard_map(body, mesh=mesh, in_specs=in_specs, out_specs=out_specs, check_vma=False)
```

```python
import functools

import jax
import jax.numpy as jnp
from jax import lax
from jax.experimental import pallas as pl
from jax.experimental.pallas import tpu as pltpu
from jax.sharding import PartitionSpec as P

ROWS = 64
COLS = 128
KD = 32
TILE = 16
RIM = 8
EXT = 80
BLOCKS = 4
SWEEPS = 3
STEPS = BLOCKS * SWEEPS
HALO = STEPS
SLOTS = 2 * HALO + 1
CHUNKS = (SLOTS + 3) // 4
EPSILON = 1e-05
MESH = pl.DeviceIdType.MESH
F32 = jnp.float32
BF16 = jnp.bfloat16
NT = (((1,), (1,)), ((), ()))


def iota(shape, dim):
    return lax.broadcasted_iota(jnp.int32, shape, dim)


def mm(a, b):
    return jnp.dot(a, b, preferred_element_type=F32)


def mm_nt(a, b):
    return lax.dot_general(a, b, NT, preferred_element_type=F32)


def split(x):
    hi = x.astype(BF16).astype(F32)
    return hi, x - hi


def column_of(row):
    square = iota((KD, KD), 0) == iota((KD, KD), 1)
    return jnp.sum(jnp.where(square, row, 0.0), axis=1, keepdims=True)


def tile_map():
    lane = iota((COLS, 8 * COLS), 1)
    return jnp.where(
        iota((COLS, 8 * COLS), 0) == (lane // COLS) * TILE + lane % TILE, 1.0, 0.0
    ).astype(BF16)


def place_columns(flat, col, tiles):
    stacked = jnp.concatenate([flat[:, 0:COLS], flat[:, COLS:]], axis=0)
    spread = mm(stacked, tiles)
    own_group = iota((KD, COLS), 1) // TILE == iota((KD, COLS), 0) % 8
    rows = [
        jnp.where(
            own_group,
            spread[KD * (i // 8) : KD * (i // 8) + KD, (i % 8) * COLS : (i % 8 + 1) * COLS],
            0.0,
        )
        for i in range(TILE)
    ]
    anchor = col + jnp.zeros((KD, COLS), F32)
    offset = (iota((8, TILE, COLS), 2) - iota((8, TILE, COLS), 1)).astype(F32)
    out = []
    for g in range(4):
        lhs = jnp.concatenate([r[8 * g : 8 * g + 8, :] for r in rows], axis=0).astype(BF16)
        place = jnp.broadcast_to(anchor[8 * g : 8 * g + 8, None, :], (8, TILE, COLS))
        onehot = jnp.where(place == offset, 1.0, 0.0).astype(BF16).reshape(COLS, COLS)
        out.append(mm(lhs, onehot))
    return [
        jnp.concatenate([out[g][8 * i : 8 * i + 8, :] for g in range(4)], axis=0)
        for i in range(TILE)
    ]


def place_rows(row, tile_rows, first, count):
    known = {}
    bits = [((row >> b) & 1) == 1 for b in range(6)]

    def at(level, y):
        if y < 0 or y > TILE - 1 + (1 << level) - 1:
            return None
        if level == 0:
            return tile_rows[y]
        if (level, y) not in known:
            moved = at(level - 1, y - (1 << (level - 1)))
            kept = at(level - 1, y)
            zero = jnp.zeros((KD, COLS), F32)
            bit = bits[level - 1]
            known[level, y] = jnp.where(
                bit, zero if moved is None else moved, zero if kept is None else kept
            )
        return known[level, y]

    return [at(6, y) for y in range(first, first + count)]


def kernel(
    n_slab,
    n_frames,
    raw_in,
    shift_in,
    foot_in,
    anchor_in,
    block_in,
    trace_in,
    z_ref,
    res_ref,
    raw_ref,
    shift_ref,
    foot_ref,
    anchor_ref,
    block_ref,
    trace_ref,
    fetched,
    pkt_out,
    pkt_in,
    early,
    late,
    mom_out,
    mom_in,
    image,
    rawx,
    mixed,
    corr,
    band,
    square,
    e1_send,
    e1_recv,
    early_send,
    early_recv,
    late_send,
    late_recv,
    e3_send,
    e3_recv,
):
    me = lax.axis_index("slab")
    frame = lax.axis_index("frames")

    def slab_at(offset):
        return lax.rem(me + offset + 2 * n_slab, n_slab)

    def frame_at(offset):
        return lax.rem(frame + offset, n_frames)

    barrier = pltpu.get_barrier_semaphore()

    def greet_slab(i, carry):
        for sign in (1, -1):
            pl.semaphore_signal(
                barrier,
                1,
                device_id={"slab": slab_at(sign * (HALO + 1 - i))},
                device_id_type=MESH,
            )
        return carry

    def greet_frame(i, carry):
        pl.semaphore_signal(barrier, 1, device_id={"frames": frame_at(i)}, device_id_type=MESH)
        return carry

    lax.fori_loop(1, HALO + 1, greet_slab, 0)
    lax.fori_loop(1, n_frames, greet_frame, 0)

    fetches = [
        pltpu.make_async_copy(source, target, fetched.at[i])
        for i, (source, target) in enumerate(
            (
                (foot_in, foot_ref),
                (anchor_in, anchor_ref),
                (trace_in, trace_ref),
                (raw_in, raw_ref),
                (shift_in, shift_ref),
                (block_in, block_ref),
            )
        )
    ]
    for fetch in fetches:
        fetch.start()
    for fetch in fetches:
        fetch.wait()

    eye = iota((KD, KD), 0) == iota((KD, KD), 1)
    flat = mm_nt(jnp.where(eye, 1.0, 0.0).astype(BF16), foot_ref[...]).astype(BF16)
    own_row = column_of((anchor_ref[0:1, :] - (me * ROWS - RIM)).astype(F32))
    own_col = column_of(anchor_ref[1:2, :].astype(F32))
    start = [column_of(trace_ref[t : t + 1, :]) for t in range(2)]
    lane = iota((KD, COLS), 1)
    small = jnp.where(lane == 0, own_row, 0.0)
    small = jnp.where(lane == 1, own_col, small)
    for t in range(2):
        t_hi, t_rest = split(start[t])
        t_mid, t_lo = split(t_rest)
        for i, part in enumerate((t_hi, t_mid, t_lo)):
            small = jnp.where(lane == 2 + 2 * i + t, part, small)
    for side, patch in ((0, 0), (1, 1)):
        mine = small
        for which in range(2):
            for t in range(2):
                value = jnp.full((KD, COLS), shift_ref[which, t, 0, patch], jnp.int32).astype(F32)
                mine = jnp.where(lane == 8 + 2 * which + t, value, mine)
        top = 0 if side == 0 else ROWS - 16
        for t in range(2):
            pkt_out[side, 16 * t : 16 * t + 16, :] = raw_ref[t, top : top + 16, :]
        pkt_out[side, 32:64, :] = flat[:, 0:COLS]
        pkt_out[side, 64:96, :] = flat[:, COLS:]
        pkt_out[side, 96:128, :] = mine.astype(BF16)

    pl.semaphore_wait(barrier, 2 * HALO + n_frames - 1)

    def packet(side):
        return pltpu.make_async_remote_copy(
            src_ref=pkt_out.at[side],
            dst_ref=pkt_in.at[1 - side],
            send_sem=e1_send.at[side],
            recv_sem=e1_recv.at[1 - side],
            device_id={"slab": slab_at(-1 if side == 0 else 1)},
            device_id_type=MESH,
        )

    to_left, to_right = packet(0), packet(1)
    to_left.start()
    to_right.start()

    image[...] = jnp.zeros(image.shape, BF16)
    tiles = tile_map()
    own_int = (own_row + jnp.zeros((KD, COLS), F32)).astype(jnp.int32)
    for y, value in enumerate(place_rows(own_int, place_columns(flat, own_col, tiles), 0, EXT)):
        if value is not None:
            image[0:KD, y * COLS : (y + 1) * COLS] = value.astype(BF16)
    own = image[0:KD, :]
    gram_own = mm_nt(own, own)
    norm_sq = jnp.sum(jnp.where(eye, gram_own, 0.0), axis=0, keepdims=True)
    def message(ref, send_sem, recv_sem, offset):
        slot = HALO - offset
        return pltpu.make_async_remote_copy(
            src_ref=ref.at[HALO, 0:10],
            dst_ref=ref.at[slot, 0:10],
            send_sem=send_sem,
            recv_sem=recv_sem,
            device_id={"slab": slab_at(offset)},
            device_id_type=MESH,
        )

    def send(ref, send_sem, recv_sem, i, carry):
        message(ref, send_sem, recv_sem, HALO + 1 - i).start()
        message(ref, send_sem, recv_sem, i - HALO - 1).start()
        return carry

    def arrived(ref, sem):
        whole = ref.at[0 : 2 * HALO, 0:10]
        pltpu.make_async_copy(whole, whole, sem).wait()

    early_set = (early, early_send, early_recv)
    late_set = (late, late_send, late_recv)

    def compact(gram):
        square[:, 0:KD] = gram
        total = square[0:8, :]
        for g in range(1, 4):
            total = total + pltpu.roll(square[8 * g : 8 * g + 8, :], KD * g, 1)
        return total

    square[...] = jnp.zeros((KD, COLS), F32)
    early[HALO, 0:8, :] = compact(gram_own)
    early[HALO, 8:16, :] = jnp.zeros((8, COLS), F32)
    early[HALO, 8:9, 0:KD] = 1.0 / norm_sq
    early[HALO, 9:10, 0:KD] = block_ref[...].astype(F32)
    lax.fori_loop(1, HALO + 1, functools.partial(send, *early_set), 0)

    def mix(t, low, high):
        at = t * 96 + low + 4
        mixed[t * 96 + low : t * 96 + high, :] = (
            0.75 * rawx[at : at + high - low, :] + 0.25 * rawx[at + 1 : at + 1 + high - low, :]
        )

    def correct(t, y0, n, down, across, keep):
        picked = jnp.zeros((n, COLS), F32)
        for a in range(-3, 4):
            at = t * 96 + y0 + 12 + a
            picked = jnp.where(down == a, mixed[at : at + n, :], picked)
        place = iota((n, COLS), 1)
        moved = jnp.zeros((n, COLS), F32)
        for c in range(-3, 4):
            turned = picked if c == 0 else pltpu.roll(picked, (-c) % COLS, 1)
            within = (place + c >= 0) & (place + c < COLS)
            moved = jnp.where((across == c) & within, turned, moved)
        moved = moved.astype(BF16).astype(F32)
        if keep is not None:
            moved = moved * keep
        at = t * EXT + y0 + RIM
        corr[at : at + n, :] = moved

    def correct_own(t, y0, n):
        down, across = (
            jnp.full((n, COLS), shift_ref[which, t, 0, y0 // 32], jnp.int32).astype(F32)
            for which in range(2)
        )
        correct(t, y0, n, down, across, None)

    def frame_rows(low, high):
        rows = [corr[pl.ds(y, 8, stride=EXT), :] for y in range(low, high)]
        return jnp.concatenate(rows, axis=1).astype(BF16)

    corr[2 * EXT :, :] = jnp.zeros((6 * EXT, COLS), F32)
    for t in range(2):
        rawx[t * 96 + 16 : t * 96 + 80, :] = raw_ref[t].astype(F32)
        mix(t, 12, 75)
        correct_own(t, 8, 24)
        correct_own(t, 32, 24)
    q_inner = mm_nt(frame_rows(16, ROWS), image[0:KD, 16 * COLS : ROWS * COLS])

    to_left.wait()
    to_right.wait()

    smalls = []
    valid = []
    for side in range(2):
        inside = me > 0 if side == 0 else me < n_slab - 1
        keep = jnp.where(inside, 1.0, 0.0).astype(F32)
        valid.append(keep)
        info = pkt_in[side, 96:128, :].astype(F32) * keep
        smalls.append(info)
        theirs = jnp.concatenate([pkt_in[side, 32:64, :], pkt_in[side, 64:96, :]], axis=1)
        wide = place_columns(theirs, info[:, 1:2], tiles)
        row = (info[:, 0:1] + jnp.zeros((KD, COLS), F32)).astype(jnp.int32)
        first = ROWS if side == 0 else 0
        low = 96 if side == 0 else 32
        for i, value in enumerate(place_rows(row, wide, first, 16)):
            if value is not None:
                y = i if side == 0 else ROWS + i
                image[low : low + KD, y * COLS : (y + 1) * COLS] = (value * keep).astype(BF16)
        for t in range(2):
            at = t * 96 + (0 if side == 0 else 80)
            rawx[at : at + 16, :] = pkt_in[side, 16 * t : 16 * t + 16, :].astype(F32) * keep
    gram_left = mm_nt(image[96:128, 0 : 16 * COLS], image[0:KD, 0 : 16 * COLS])
    gram_right = mm_nt(image[32:64, ROWS * COLS :], image[0:KD, ROWS * COLS :])

    for t in range(2):
        mix(t, 0, 12)
        mix(t, 75, 88)
        correct_own(t, 0, RIM)
        correct_own(t, ROWS - RIM, RIM)
        for side, y0 in ((0, -RIM), (1, ROWS)):
            info = smalls[side]
            down = jnp.broadcast_to(info[0:1, 8 + t : 9 + t], (RIM, COLS))
            across = jnp.broadcast_to(info[0:1, 10 + t : 11 + t], (RIM, COLS))
            correct(t, y0, RIM, down, across, valid[side])
    q = (
        q_inner
        + mm_nt(frame_rows(0, 16), image[0:KD, 0 : 16 * COLS])
        + mm_nt(frame_rows(ROWS, EXT), image[0:KD, ROWS * COLS :])
    )

    old = [start]
    for info in smalls:
        exact = info[:, 2:4] + info[:, 4:6] + info[:, 6:8]
        old.append([exact[:, t : t + 1] for t in range(2)])
    grams = (gram_own, gram_left, gram_right)
    late[HALO, 0:8, :] = compact(gram_left)
    late[HALO, 8:16, :] = jnp.zeros((8, COLS), F32)
    for t in range(2):
        rendered = sum(
            jnp.sum(gram * x[t], axis=0, keepdims=True) for gram, x in zip(grams, old)
        )
        late[HALO, 8 + t : 9 + t, 0:KD] = q[t : t + 1, :] - rendered
    lax.fori_loop(1, HALO + 1, functools.partial(send, *late_set), 0)

    lanes8 = iota((8, COLS), 1)
    wide_lane = iota((KD, COLS), 1)
    wide_row = iota((KD, COLS), 0)
    first_rows = []
    for x, low in zip(old, (0, 96, 32)):
        first_rows.append(
            [
                jnp.sum(
                    jnp.where(wide_lane - low == wide_row, x[t], 0.0),
                    axis=0,
                    keepdims=True,
                )
                for t in range(2)
            ]
        )

    def rows_of(pair):
        sub = iota((8, COLS), 0)
        return jnp.where(sub == 0, pair[0], 0.0) + jnp.where(sub == 1, pair[1], 0.0)

    own_x, left_x, right_x = (rows_of(pair) for pair in first_rows)

    arrived(early, early_recv)
    arrived(late, late_recv)

    group8 = lanes8 // KD

    def turned(value, turn):
        return value if turn % COLS == 0 else pltpu.roll(value, turn % COLS, 1)

    def keep_of(slot):
        where = me + (slot - HALO)
        return jnp.where((where >= 0) & (where < n_slab), 1.0, 0.0).astype(F32)

    def spread(tile, i):
        parts = [jnp.where(group8 == i, turned(tile, KD * (i - g)), 0.0) for g in range(4)]
        return jnp.concatenate(parts, axis=0)

    zero32 = jnp.zeros((KD, COLS), F32)
    zero8 = jnp.zeros((8, COLS), F32)
    state, gains = [], []
    before = zero32
    for m in range(CHUNKS):
        p_rows, gain_rows, diag, links = zero8, zero8, [], []
        for i in range(4):
            slot = 4 * m + i
            if slot < SLOTS:
                keep = keep_of(slot)
                rows = jnp.where(group8 == i, turned(late[slot, 8:16, :], KD * i), 0.0)
                p_rows = p_rows + rows * keep
                rows = jnp.where(group8 == i, turned(early[slot, 8:16, :], KD * i), 0.0)
                gain_rows = gain_rows + rows * keep
                diag.append(spread(early[slot, 0:8, :] * keep, i))
            else:
                diag.append(zero32)
            after = slot + 1
            if after < SLOTS:
                links.append(spread(late[after, 0:8, :] * keep_of(after), (i + 1) % 4))
            else:
                links.append(zero32)
        state.append(p_rows)
        gains.append(
            [jnp.where(gain_rows[1:2, :] == float(b), gain_rows[0:1, :], 0.0) for b in range(BLOCKS)]
        )
        upper = jnp.concatenate(links, axis=0)
        lower = upper.T
        corner = lower[0:KD, :]
        blocks = []
        for i in range(4):
            value = diag[i]
            if i < 3:
                value = value + links[i]
            if i > 0:
                value = value + lower[KD * i : KD * i + KD, :]
            blocks.append(value)
        for at, value in ((0, blocks[0]), (1, blocks[1]), (2, blocks[2]), (3, blocks[3]), (4, corner), (5, zero32), (6, zero32), (7, before)):
            hi, lo = split(value)
            band[m, at * KD : (at + 1) * KD, 0:COLS] = hi.astype(BF16)
            band[m, at * KD : (at + 1) * KD, COLS:] = lo.astype(BF16)
        before = links[3]

    total2 = jnp.where(lanes8 >= 96, left_x, 0.0)
    total3 = own_x + right_x
    for step in range(1, STEPS + 1):
        b = (step - 1) % BLOCKS
        low, high = max(step - 1, 0) // 4, min(2 * HALO + 1 - step, SLOTS - 1) // 4
        change = {m: state[m] * gains[m][b] for m in range(low, high + 1)}
        total2 = total2 + change[2]
        total3 = total3 + change[3]
        if step == STEPS:
            break
        zero = jnp.zeros((8, COLS), F32)
        for m in range(step // 4, (2 * HALO - step) // 4 + 1):
            beside = jnp.where(
                lanes8 >= 96,
                change.get(m - 1, zero),
                jnp.where(lanes8 < 32, change.get(m + 1, zero), 0.0),
            )
            a_hi, a_lo = split(change[m])
            b_hi, b_lo = split(beside)
            lhs = jnp.concatenate(
                [jnp.concatenate([a_hi, a_lo], axis=0), jnp.concatenate([b_hi, b_lo], axis=0)],
                axis=1,
            ).astype(BF16)
            out = mm(lhs, band[m])
            state[m] = state[m] - (out[0:8, 0:COLS] + out[8:16, 0:COLS] + out[0:8, COLS:])

    own_lane = lanes8 < 32
    two_rows = iota((8, COLS), 0) < 2
    final = jnp.where(own_lane & two_rows, total3, 0.0)
    mom_out[0:1, :] = jnp.sum(final, axis=0, keepdims=True)
    mom_out[1:2, :] = jnp.sum(final * final, axis=0, keepdims=True)

    def moments(i):
        return pltpu.make_async_remote_copy(
            src_ref=mom_out,
            dst_ref=mom_in.at[n_frames - i],
            send_sem=e3_send,
            recv_sem=e3_recv,
            device_id={"frames": frame_at(i)},
            device_id_type=MESH,
        )

    def send_moments(i, carry):
        moments(i).start()
        return carry

    lax.fori_loop(1, n_frames, send_moments, 0)

    all_x = jnp.where(lanes8 < 64, total3, jnp.where(lanes8 >= 96, total2, 0.0))
    x_hi, x_lo = split(all_x)
    lhs = jnp.concatenate([x_hi, x_lo], axis=0).astype(BF16)
    pieces = (
        mm(lhs, image[:, RIM * COLS : 16 * COLS]),
        mm(lhs[:, 0:KD], image[0:KD, 16 * COLS : ROWS * COLS]),
        mm(lhs, image[:, ROWS * COLS : (ROWS + RIM) * COLS]),
    )
    y = 0
    for piece in pieces:
        rendered = piece[0:8, :] + piece[8:16, :]
        for i in range(piece.shape[1] // COLS):
            rows = corr[pl.ds(y + RIM, 8, stride=EXT), :] - rendered[:, i * COLS : (i + 1) * COLS]
            res_ref[pl.ds(y, 2, stride=ROWS), :] = rows[0:2, :]
            y += 1

    arrived(early, early_send)
    arrived(late, late_send)
    others = mom_in.at[1:n_frames]
    pltpu.make_async_copy(others, others, e3_send).wait()
    pltpu.make_async_copy(others, others, e3_recv).wait()
    sums = mom_out[...]
    for i in range(1, n_frames):
        sums = sums + mom_in[i]
    count = 2 * n_frames
    mean = sums[0:1, :] / count
    square = sums[1:2, :] / count
    spread = square - mean * mean
    z_row = (total3[0:2, :] - mean) / jnp.sqrt(spread + EPSILON)
    z_ref[...] = z_row[:, 0:KD]


def hand_on(z_ref, res_ref, z_out, res_out, sems):
    copies = [
        pltpu.make_async_copy(res_ref, res_out, sems.at[0]),
        pltpu.make_async_copy(z_ref, z_out, sems.at[1]),
    ]
    for copy in copies:
        copy.start()
    for copy in copies:
        copy.wait()


def shards(n_slab, n_frames, raw_movie, shifts, footprints, anchors, block_of, init_traces):
    vmem = pl.BlockSpec(memory_space=pltpu.VMEM)
    dma = pltpu.SemaphoreType.DMA
    traces_z, residual = pl.pallas_call(
        functools.partial(kernel, n_slab, n_frames),
        out_shape=(
            pltpu.VMEM((2, KD), F32),
            pltpu.VMEM((2 * ROWS, COLS), F32),
        ),
        in_specs=[pl.BlockSpec(memory_space=pl.ANY)] * 6,
        out_specs=(vmem, vmem),
        scratch_shapes=[
            pltpu.VMEM((2, ROWS, COLS), BF16),
            pltpu.SMEM((2, 2, 1, 2), jnp.int32),
            pltpu.VMEM((TILE * TILE, KD), BF16),
            pltpu.VMEM((2, KD), jnp.int32),
            pltpu.VMEM((1, KD), jnp.int32),
            pltpu.VMEM((2, KD), F32),
            dma((6,)),
            pltpu.VMEM((2, 128, COLS), BF16),
            pltpu.VMEM((2, 128, COLS), BF16),
            pltpu.VMEM((SLOTS, 16, COLS), F32),
            pltpu.VMEM((SLOTS, 16, COLS), F32),
            pltpu.VMEM((2, COLS), F32),
            pltpu.VMEM((n_frames, 2, COLS), F32),
            pltpu.VMEM((128, EXT * COLS), BF16),
            pltpu.VMEM((192, COLS), F32),
            pltpu.VMEM((192, COLS), F32),
            pltpu.VMEM((8 * EXT, COLS), F32),
            pltpu.VMEM((CHUNKS, 256, 256), BF16),
            pltpu.VMEM((KD, COLS), F32),
            dma((2,)),
            dma((2,)),
            dma,
            dma,
            dma,
            dma,
            dma,
            dma,
        ],
        compiler_params=pltpu.CompilerParams(collective_id=0, has_side_effects=True),
    )(
        raw_movie,
        shifts.transpose(0, 1, 3, 2),
        footprints.transpose(1, 2, 0).reshape(TILE * TILE, KD),
        anchors.T,
        block_of.reshape(1, KD),
        init_traces.T,
    )
    traces_z = pltpu.with_memory_space_constraint(traces_z, pltpu.VMEM)
    residual = pltpu.with_memory_space_constraint(residual, pltpu.VMEM)
    traces_z, residual = pl.pallas_call(
        hand_on,
        out_shape=(
            jax.ShapeDtypeStruct((2, KD), F32),
            jax.ShapeDtypeStruct((2 * ROWS, COLS), F32),
        ),
        in_specs=[pl.BlockSpec(memory_space=pltpu.VMEM)] * 2,
        out_specs=(pl.BlockSpec(memory_space=pltpu.HBM),) * 2,
        scratch_shapes=[dma((2,))],
    )(traces_z, residual)
    return traces_z.T, residual.reshape(2, ROWS, COLS)


def solution(mesh):
    in_specs = (
        P("frames", "slab", None),
        P(None, "frames", "slab", None),
        P("slab", None, None),
        P("slab", None),
        P("slab"),
        P("slab", "frames"),
    )
    out_specs = (P("slab", "frames"), P("frames", "slab", None))
    body = functools.partial(shards, mesh.shape["slab"], mesh.shape["frames"])
    return jax.shard_map(body, mesh=mesh, in_specs=in_specs, out_specs=out_specs, check_vma=False)
```

```python
import functools

import jax
import jax.numpy as jnp
from jax import lax
from jax.experimental import pallas as pl
from jax.experimental.pallas import tpu as pltpu
from jax.sharding import PartitionSpec as P

ROWS = 64
COLS = 128
KD = 32
TILE = 16
RIM = 8
EXT = 80
BLOCKS = 4
SWEEPS = 3
STEPS = BLOCKS * SWEEPS
HALO = STEPS
SLOTS = 2 * HALO + 1
CHUNKS = (SLOTS + 3) // 4
EPSILON = 1e-05
MESH = pl.DeviceIdType.MESH
F32 = jnp.float32
BF16 = jnp.bfloat16
NT = (((1,), (1,)), ((), ()))


def iota(shape, dim):
    return lax.broadcasted_iota(jnp.int32, shape, dim)


def mm(a, b):
    return jnp.dot(a, b, preferred_element_type=F32)


def mm_nt(a, b):
    return lax.dot_general(a, b, NT, preferred_element_type=F32)


def split(x):
    hi = x.astype(BF16).astype(F32)
    return hi, x - hi


def column_of(row):
    square = iota((KD, KD), 0) == iota((KD, KD), 1)
    return jnp.sum(jnp.where(square, row, 0.0), axis=1, keepdims=True)


def place_columns(flat, col):
    halves = [flat[:, 0:COLS].astype(F32), flat[:, COLS:].astype(F32)]
    offset = iota((KD, COLS), 1) - (col + jnp.zeros((KD, COLS), F32)).astype(jnp.int32)
    inside = (offset >= 0) & (offset < TILE)
    rows = []
    for i in range(TILE):
        lanes = (offset + TILE * (i % 8)) & (COLS - 1)
        taken = jnp.take_along_axis(halves[i // 8], lanes, axis=1, mode="promise_in_bounds")
        rows.append(jnp.where(inside, taken, 0.0))
    return rows


def place_rows(row, tile_rows, first, count):
    known = {}
    bits = [((row >> b) & 1) == 1 for b in range(6)]

    def at(level, y):
        if y < 0 or y > TILE - 1 + (1 << level) - 1:
            return None
        if level == 0:
            return tile_rows[y]
        if (level, y) not in known:
            moved = at(level - 1, y - (1 << (level - 1)))
            kept = at(level - 1, y)
            zero = jnp.zeros((KD, COLS), F32)
            bit = bits[level - 1]
            known[level, y] = jnp.where(
                bit, zero if moved is None else moved, zero if kept is None else kept
            )
        return known[level, y]

    return [at(6, y) for y in range(first, first + count)]


def kernel(
    n_slab,
    n_frames,
    raw_in,
    shift_in,
    foot_in,
    anchor_in,
    block_in,
    trace_in,
    z_ref,
    res_ref,
    raw_ref,
    shift_ref,
    foot_ref,
    anchor_ref,
    block_ref,
    trace_ref,
    fetched,
    pkt_out,
    pkt_in,
    early,
    late,
    mom_out,
    mom_in,
    image,
    rawx,
    mixed,
    corr,
    band,
    square,
    e1_send,
    e1_recv,
    early_send,
    early_recv,
    late_send,
    late_recv,
    e3_send,
    e3_recv,
):
    me = lax.axis_index("slab")
    frame = lax.axis_index("frames")

    def slab_at(offset):
        return lax.rem(me + offset + 2 * n_slab, n_slab)

    def frame_at(offset):
        return lax.rem(frame + offset, n_frames)

    fetches = [
        pltpu.make_async_copy(source, target, fetched.at[i])
        for i, (source, target) in enumerate(
            (
                (foot_in, foot_ref),
                (anchor_in, anchor_ref),
                (trace_in, trace_ref),
                (raw_in, raw_ref),
                (shift_in, shift_ref),
                (block_in, block_ref),
            )
        )
    ]
    for fetch in fetches:
        fetch.start()

    barrier = pltpu.get_barrier_semaphore()

    def greet_slab(i, carry):
        for sign in (1, -1):
            pl.semaphore_signal(
                barrier,
                1,
                device_id={"slab": slab_at(sign * (HALO + 1 - i))},
                device_id_type=MESH,
            )
        return carry

    def greet_frame(i, carry):
        pl.semaphore_signal(barrier, 1, device_id={"frames": frame_at(i)}, device_id_type=MESH)
        return carry

    lax.fori_loop(1, HALO + 1, greet_slab, 0)
    lax.fori_loop(1, n_frames, greet_frame, 0)

    for fetch in fetches:
        fetch.wait()

    eye = iota((KD, KD), 0) == iota((KD, KD), 1)
    flat = mm_nt(jnp.where(eye, 1.0, 0.0).astype(BF16), foot_ref[...]).astype(BF16)
    own_row = column_of((anchor_ref[0:1, :] - (me * ROWS - RIM)).astype(F32))
    own_col = column_of(anchor_ref[1:2, :].astype(F32))
    start = [column_of(trace_ref[t : t + 1, :]) for t in range(2)]
    lane = iota((KD, COLS), 1)
    small = jnp.where(lane == 0, own_row, 0.0)
    small = jnp.where(lane == 1, own_col, small)
    for t in range(2):
        t_hi, t_rest = split(start[t])
        t_mid, t_lo = split(t_rest)
        for i, part in enumerate((t_hi, t_mid, t_lo)):
            small = jnp.where(lane == 2 + 2 * i + t, part, small)
    for side, patch in ((0, 0), (1, 1)):
        mine = small
        for which in range(2):
            for t in range(2):
                value = jnp.full((KD, COLS), shift_ref[which, t, 0, patch], jnp.int32).astype(F32)
                mine = jnp.where(lane == 8 + 2 * which + t, value, mine)
        top = 0 if side == 0 else ROWS - 16
        for t in range(2):
            pkt_out[side, 16 * t : 16 * t + 16, :] = raw_ref[t, top : top + 16, :]
        pkt_out[side, 32:64, :] = flat[:, 0:COLS]
        pkt_out[side, 64:96, :] = flat[:, COLS:]
        pkt_out[side, 96:128, :] = mine.astype(BF16)

    pl.semaphore_wait(barrier, 2 * HALO + n_frames - 1)

    def packet(side):
        return pltpu.make_async_remote_copy(
            src_ref=pkt_out.at[side],
            dst_ref=pkt_in.at[1 - side],
            send_sem=e1_send.at[side],
            recv_sem=e1_recv.at[1 - side],
            device_id={"slab": slab_at(-1 if side == 0 else 1)},
            device_id_type=MESH,
        )

    to_left, to_right = packet(0), packet(1)
    to_left.start()
    to_right.start()

    image[...] = jnp.zeros(image.shape, BF16)
    own_int = (own_row + jnp.zeros((KD, COLS), F32)).astype(jnp.int32)
    for y, value in enumerate(place_rows(own_int, place_columns(flat, own_col), 0, EXT)):
        if value is not None:
            image[0:KD, y * COLS : (y + 1) * COLS] = value.astype(BF16)
    own = image[0:KD, :]
    gram_own = mm_nt(own, own)
    norm_sq = jnp.sum(jnp.where(eye, gram_own, 0.0), axis=0, keepdims=True)
    def message(ref, send_sem, recv_sem, offset):
        slot = HALO - offset
        return pltpu.make_async_remote_copy(
            src_ref=ref.at[HALO, 0:10],
            dst_ref=ref.at[slot, 0:10],
            send_sem=send_sem,
            recv_sem=recv_sem,
            device_id={"slab": slab_at(offset)},
            device_id_type=MESH,
        )

    def send(ref, send_sem, recv_sem, i, carry):
        message(ref, send_sem, recv_sem, HALO + 1 - i).start()
        message(ref, send_sem, recv_sem, i - HALO - 1).start()
        return carry

    def arrived(ref, sem):
        whole = ref.at[0 : 2 * HALO, 0:10]
        pltpu.make_async_copy(whole, whole, sem).wait()

    early_set = (early, early_send, early_recv)
    late_set = (late, late_send, late_recv)

    def compact(gram):
        square[:, 0:KD] = gram
        total = square[0:8, :]
        for g in range(1, 4):
            total = total + pltpu.roll(square[8 * g : 8 * g + 8, :], KD * g, 1)
        return total

    square[...] = jnp.zeros((KD, COLS), F32)
    early[HALO, 0:8, :] = compact(gram_own)
    early[HALO, 8:16, :] = jnp.zeros((8, COLS), F32)
    early[HALO, 8:9, 0:KD] = 1.0 / norm_sq
    early[HALO, 9:10, 0:KD] = block_ref[...].astype(F32)
    lax.fori_loop(1, HALO + 1, functools.partial(send, *early_set), 0)

    def mix(t, low, high):
        at = t * 96 + low + 4
        mixed[t * 96 + low : t * 96 + high, :] = (
            0.75 * rawx[at : at + high - low, :] + 0.25 * rawx[at + 1 : at + 1 + high - low, :]
        )

    def correct(t, y0, n, down, across, keep):
        picked = jnp.zeros((n, COLS), F32)
        for a in range(-3, 4):
            at = t * 96 + y0 + 12 + a
            picked = jnp.where(down == a, mixed[at : at + n, :], picked)
        place = iota((n, COLS), 1)
        moved = jnp.zeros((n, COLS), F32)
        for c in range(-3, 4):
            turned = picked if c == 0 else pltpu.roll(picked, (-c) % COLS, 1)
            within = (place + c >= 0) & (place + c < COLS)
            moved = jnp.where((across == c) & within, turned, moved)
        moved = moved.astype(BF16).astype(F32)
        if keep is not None:
            moved = moved * keep
        at = t * EXT + y0 + RIM
        corr[at : at + n, :] = moved

    def correct_own(t, y0, n):
        down, across = (
            jnp.full((n, COLS), shift_ref[which, t, 0, y0 // 32], jnp.int32).astype(F32)
            for which in range(2)
        )
        correct(t, y0, n, down, across, None)

    def frame_rows(low, high):
        rows = [corr[pl.ds(y, 8, stride=EXT), :] for y in range(low, high)]
        return jnp.concatenate(rows, axis=1).astype(BF16)

    corr[2 * EXT :, :] = jnp.zeros((6 * EXT, COLS), F32)
    for t in range(2):
        rawx[t * 96 + 16 : t * 96 + 80, :] = raw_ref[t].astype(F32)
        mix(t, 12, 75)
        correct_own(t, 8, 24)
        correct_own(t, 32, 24)
    q_inner = mm_nt(frame_rows(16, ROWS), image[0:KD, 16 * COLS : ROWS * COLS])

    to_left.wait()
    to_right.wait()

    smalls = []
    valid = []
    for side in range(2):
        inside = me > 0 if side == 0 else me < n_slab - 1
        keep = jnp.where(inside, 1.0, 0.0).astype(F32)
        valid.append(keep)
        info = pkt_in[side, 96:128, :].astype(F32) * keep
        smalls.append(info)
        theirs = jnp.concatenate([pkt_in[side, 32:64, :], pkt_in[side, 64:96, :]], axis=1)
        wide = place_columns(theirs, info[:, 1:2])
        row = (info[:, 0:1] + jnp.zeros((KD, COLS), F32)).astype(jnp.int32)
        first = ROWS if side == 0 else 0
        low = 96 if side == 0 else 32
        for i, value in enumerate(place_rows(row, wide, first, 16)):
            if value is not None:
                y = i if side == 0 else ROWS + i
                image[low : low + KD, y * COLS : (y + 1) * COLS] = (value * keep).astype(BF16)
        for t in range(2):
            at = t * 96 + (0 if side == 0 else 80)
            rawx[at : at + 16, :] = pkt_in[side, 16 * t : 16 * t + 16, :].astype(F32) * keep
    gram_left = mm_nt(image[96:128, 0 : 16 * COLS], image[0:KD, 0 : 16 * COLS])
    gram_right = mm_nt(image[32:64, ROWS * COLS :], image[0:KD, ROWS * COLS :])

    for t in range(2):
        mix(t, 0, 12)
        mix(t, 75, 88)
        correct_own(t, 0, RIM)
        correct_own(t, ROWS - RIM, RIM)
        for side, y0 in ((0, -RIM), (1, ROWS)):
            info = smalls[side]
            down = jnp.broadcast_to(info[0:1, 8 + t : 9 + t], (RIM, COLS))
            across = jnp.broadcast_to(info[0:1, 10 + t : 11 + t], (RIM, COLS))
            correct(t, y0, RIM, down, across, valid[side])
    q = (
        q_inner
        + mm_nt(frame_rows(0, 16), image[0:KD, 0 : 16 * COLS])
        + mm_nt(frame_rows(ROWS, EXT), image[0:KD, ROWS * COLS :])
    )

    old = [start]
    for info in smalls:
        exact = info[:, 2:4] + info[:, 4:6] + info[:, 6:8]
        old.append([exact[:, t : t + 1] for t in range(2)])
    grams = (gram_own, gram_left, gram_right)
    late[HALO, 0:8, :] = compact(gram_left)
    late[HALO, 8:16, :] = jnp.zeros((8, COLS), F32)
    for t in range(2):
        rendered = sum(
            jnp.sum(gram * x[t], axis=0, keepdims=True) for gram, x in zip(grams, old)
        )
        late[HALO, 8 + t : 9 + t, 0:KD] = q[t : t + 1, :] - rendered
    lax.fori_loop(1, HALO + 1, functools.partial(send, *late_set), 0)

    lanes8 = iota((8, COLS), 1)
    wide_lane = iota((KD, COLS), 1)
    wide_row = iota((KD, COLS), 0)
    first_rows = []
    for x, low in zip(old, (0, 96, 32)):
        first_rows.append(
            [
                jnp.sum(
                    jnp.where(wide_lane - low == wide_row, x[t], 0.0),
                    axis=0,
                    keepdims=True,
                )
                for t in range(2)
            ]
        )

    def rows_of(pair):
        sub = iota((8, COLS), 0)
        return jnp.where(sub == 0, pair[0], 0.0) + jnp.where(sub == 1, pair[1], 0.0)

    own_x, left_x, right_x = (rows_of(pair) for pair in first_rows)

    arrived(early, early_recv)
    arrived(late, late_recv)

    group8 = lanes8 // KD

    def turned(value, turn):
        return value if turn % COLS == 0 else pltpu.roll(value, turn % COLS, 1)

    def keep_of(slot):
        where = me + (slot - HALO)
        return jnp.where((where >= 0) & (where < n_slab), 1.0, 0.0).astype(F32)

    def spread(tile, i):
        parts = [jnp.where(group8 == i, turned(tile, KD * (i - g)), 0.0) for g in range(4)]
        return jnp.concatenate(parts, axis=0)

    zero32 = jnp.zeros((KD, COLS), F32)
    zero8 = jnp.zeros((8, COLS), F32)
    state, gains = [], []
    before = zero32
    for m in range(CHUNKS):
        p_rows, gain_rows, diag, links = zero8, zero8, [], []
        for i in range(4):
            slot = 4 * m + i
            if slot < SLOTS:
                keep = keep_of(slot)
                rows = jnp.where(group8 == i, turned(late[slot, 8:16, :], KD * i), 0.0)
                p_rows = p_rows + rows * keep
                rows = jnp.where(group8 == i, turned(early[slot, 8:16, :], KD * i), 0.0)
                gain_rows = gain_rows + rows * keep
                diag.append(spread(early[slot, 0:8, :] * keep, i))
            else:
                diag.append(zero32)
            after = slot + 1
            if after < SLOTS:
                links.append(spread(late[after, 0:8, :] * keep_of(after), (i + 1) % 4))
            else:
                links.append(zero32)
        state.append(p_rows)
        gains.append(
            [jnp.where(gain_rows[1:2, :] == float(b), gain_rows[0:1, :], 0.0) for b in range(BLOCKS)]
        )
        upper = jnp.concatenate(links, axis=0)
        lower = upper.T
        corner = lower[0:KD, :]
        blocks = []
        for i in range(4):
            value = diag[i]
            if i < 3:
                value = value + links[i]
            if i > 0:
                value = value + lower[KD * i : KD * i + KD, :]
            blocks.append(value)
        for at, value in ((0, blocks[0]), (1, blocks[1]), (2, blocks[2]), (3, blocks[3]), (4, corner), (5, zero32), (6, zero32), (7, before)):
            hi, lo = split(value)
            band[m, at * KD : (at + 1) * KD, 0:COLS] = hi.astype(BF16)
            band[m, at * KD : (at + 1) * KD, COLS:] = lo.astype(BF16)
        before = links[3]

    total2 = jnp.where(lanes8 >= 96, left_x, 0.0)
    total3 = own_x + right_x
    for step in range(1, STEPS + 1):
        b = (step - 1) % BLOCKS
        low, high = max(step - 1, 0) // 4, min(2 * HALO + 1 - step, SLOTS - 1) // 4
        change = {m: state[m] * gains[m][b] for m in range(low, high + 1)}
        total2 = total2 + change[2]
        total3 = total3 + change[3]
        if step == STEPS:
            break
        zero = jnp.zeros((8, COLS), F32)
        for m in range(step // 4, (2 * HALO - step) // 4 + 1):
            beside = jnp.where(
                lanes8 >= 96,
                change.get(m - 1, zero),
                jnp.where(lanes8 < 32, change.get(m + 1, zero), 0.0),
            )
            a_hi, a_lo = split(change[m])
            b_hi, b_lo = split(beside)
            lhs = jnp.concatenate(
                [jnp.concatenate([a_hi, a_lo], axis=0), jnp.concatenate([b_hi, b_lo], axis=0)],
                axis=1,
            ).astype(BF16)
            out = mm(lhs, band[m])
            state[m] = state[m] - (out[0:8, 0:COLS] + out[8:16, 0:COLS] + out[0:8, COLS:])

    own_lane = lanes8 < 32
    two_rows = iota((8, COLS), 0) < 2
    final = jnp.where(own_lane & two_rows, total3, 0.0)
    mom_out[0:1, :] = jnp.sum(final, axis=0, keepdims=True)
    mom_out[1:2, :] = jnp.sum(final * final, axis=0, keepdims=True)

    def moments(i):
        return pltpu.make_async_remote_copy(
            src_ref=mom_out,
            dst_ref=mom_in.at[n_frames - i],
            send_sem=e3_send,
            recv_sem=e3_recv,
            device_id={"frames": frame_at(i)},
            device_id_type=MESH,
        )

    def send_moments(i, carry):
        moments(i).start()
        return carry

    lax.fori_loop(1, n_frames, send_moments, 0)

    all_x = jnp.where(lanes8 < 64, total3, jnp.where(lanes8 >= 96, total2, 0.0))
    x_hi, x_lo = split(all_x)
    lhs = jnp.concatenate([x_hi, x_lo], axis=0).astype(BF16)
    pieces = (
        mm(lhs, image[:, RIM * COLS : 16 * COLS]),
        mm(lhs[:, 0:KD], image[0:KD, 16 * COLS : ROWS * COLS]),
        mm(lhs, image[:, ROWS * COLS : (ROWS + RIM) * COLS]),
    )
    y = 0
    for piece in pieces:
        rendered = piece[0:8, :] + piece[8:16, :]
        for i in range(piece.shape[1] // COLS):
            rows = corr[pl.ds(y + RIM, 8, stride=EXT), :] - rendered[:, i * COLS : (i + 1) * COLS]
            res_ref[pl.ds(y, 2, stride=ROWS), :] = rows[0:2, :]
            y += 1

    arrived(early, early_send)
    arrived(late, late_send)
    others = mom_in.at[1:n_frames]
    pltpu.make_async_copy(others, others, e3_send).wait()
    pltpu.make_async_copy(others, others, e3_recv).wait()
    sums = mom_out[...]
    for i in range(1, n_frames):
        sums = sums + mom_in[i]
    count = 2 * n_frames
    mean = sums[0:1, :] / count
    square = sums[1:2, :] / count
    spread = square - mean * mean
    z_row = (total3[0:2, :] - mean) / jnp.sqrt(spread + EPSILON)
    z_ref[...] = z_row[:, 0:KD]


def hand_on(z_ref, res_ref, z_out, res_out, sems):
    copies = [
        pltpu.make_async_copy(res_ref, res_out, sems.at[0]),
        pltpu.make_async_copy(z_ref, z_out, sems.at[1]),
    ]
    for copy in copies:
        copy.start()
    for copy in copies:
        copy.wait()


def shards(n_slab, n_frames, raw_movie, shifts, footprints, anchors, block_of, init_traces):
    vmem = pl.BlockSpec(memory_space=pltpu.VMEM)
    dma = pltpu.SemaphoreType.DMA
    traces_z, residual = pl.pallas_call(
        functools.partial(kernel, n_slab, n_frames),
        out_shape=(
            pltpu.VMEM((2, KD), F32),
            pltpu.VMEM((2 * ROWS, COLS), F32),
        ),
        in_specs=[pl.BlockSpec(memory_space=pl.ANY)] * 6,
        out_specs=(vmem, vmem),
        scratch_shapes=[
            pltpu.VMEM((2, ROWS, COLS), BF16),
            pltpu.SMEM((2, 2, 1, 2), jnp.int32),
            pltpu.VMEM((TILE * TILE, KD), BF16),
            pltpu.VMEM((2, KD), jnp.int32),
            pltpu.VMEM((1, KD), jnp.int32),
            pltpu.VMEM((2, KD), F32),
            dma((6,)),
            pltpu.VMEM((2, 128, COLS), BF16),
            pltpu.VMEM((2, 128, COLS), BF16),
            pltpu.VMEM((SLOTS, 16, COLS), F32),
            pltpu.VMEM((SLOTS, 16, COLS), F32),
            pltpu.VMEM((2, COLS), F32),
            pltpu.VMEM((n_frames, 2, COLS), F32),
            pltpu.VMEM((128, EXT * COLS), BF16),
            pltpu.VMEM((192, COLS), F32),
            pltpu.VMEM((192, COLS), F32),
            pltpu.VMEM((8 * EXT, COLS), F32),
            pltpu.VMEM((CHUNKS, 256, 256), BF16),
            pltpu.VMEM((KD, COLS), F32),
            dma((2,)),
            dma((2,)),
            dma,
            dma,
            dma,
            dma,
            dma,
            dma,
        ],
        compiler_params=pltpu.CompilerParams(collective_id=0, has_side_effects=True),
    )(
        raw_movie,
        shifts.transpose(0, 1, 3, 2),
        footprints.transpose(1, 2, 0).reshape(TILE * TILE, KD),
        anchors.T,
        block_of.reshape(1, KD),
        init_traces.T,
    )
    traces_z = pltpu.with_memory_space_constraint(traces_z, pltpu.VMEM)
    residual = pltpu.with_memory_space_constraint(residual, pltpu.VMEM)
    traces_z, residual = pl.pallas_call(
        hand_on,
        out_shape=(
            jax.ShapeDtypeStruct((2, KD), F32),
            jax.ShapeDtypeStruct((2 * ROWS, COLS), F32),
        ),
        in_specs=[pl.BlockSpec(memory_space=pltpu.VMEM)] * 2,
        out_specs=(pl.BlockSpec(memory_space=pltpu.HBM),) * 2,
        scratch_shapes=[dma((2,))],
    )(traces_z, residual)
    return traces_z.T, residual.reshape(2, ROWS, COLS)


def solution(mesh):
    in_specs = (
        P("frames", "slab", None),
        P(None, "frames", "slab", None),
        P("slab", None, None),
        P("slab", None),
        P("slab"),
        P("slab", "frames"),
    )
    out_specs = (P("slab", "frames"), P("frames", "slab", None))
    body = functools.partial(shards, mesh.shape["slab"], mesh.shape["frames"])
    return jax.shard_map(body, mesh=mesh, in_specs=in_specs, out_specs=out_specs, check_vma=False)
```

```python
import functools

import jax
import jax.numpy as jnp
from jax import lax
from jax.experimental import pallas as pl
from jax.experimental.pallas import tpu as pltpu
from jax.sharding import PartitionSpec as P

ROWS = 64
COLS = 128
KD = 32
TILE = 16
RIM = 8
EXT = 80
BLOCKS = 4
SWEEPS = 3
STEPS = BLOCKS * SWEEPS
HALO = STEPS
SLOTS = 2 * HALO + 1
CHUNKS = (SLOTS + 3) // 4
EPSILON = 1e-05
MESH = pl.DeviceIdType.MESH
F32 = jnp.float32
BF16 = jnp.bfloat16
NT = (((1,), (1,)), ((), ()))


def iota(shape, dim):
    return lax.broadcasted_iota(jnp.int32, shape, dim)


def mm(a, b):
    return jnp.dot(a, b, preferred_element_type=F32)


def mm_nt(a, b):
    return lax.dot_general(a, b, NT, preferred_element_type=F32)


def split(x):
    hi = x.astype(BF16).astype(F32)
    return hi, x - hi


def column_of(row):
    square = iota((KD, KD), 0) == iota((KD, KD), 1)
    return jnp.sum(jnp.where(square, row, 0.0), axis=1, keepdims=True)


def place_columns(flat, col):
    halves = [flat[:, 0:COLS].astype(F32), flat[:, COLS:].astype(F32)]
    offset = iota((KD, COLS), 1) - (col + jnp.zeros((KD, COLS), F32)).astype(jnp.int32)
    inside = (offset >= 0) & (offset < TILE)
    rows = []
    for i in range(TILE):
        lanes = (offset + TILE * (i % 8)) & (COLS - 1)
        taken = jnp.take_along_axis(halves[i // 8], lanes, axis=1, mode="promise_in_bounds")
        rows.append(jnp.where(inside, taken, 0.0))
    return rows


def place_rows(row, tile_rows, first, count):
    known = {}
    bits = [((row >> b) & 1) == 1 for b in range(6)]

    def at(level, y):
        if y < 0 or y > TILE - 1 + (1 << level) - 1:
            return None
        if level == 0:
            return tile_rows[y]
        if (level, y) not in known:
            moved = at(level - 1, y - (1 << (level - 1)))
            kept = at(level - 1, y)
            zero = jnp.zeros((KD, COLS), F32)
            bit = bits[level - 1]
            known[level, y] = jnp.where(
                bit, zero if moved is None else moved, zero if kept is None else kept
            )
        return known[level, y]

    return [at(6, y) for y in range(first, first + count)]


def kernel(
    n_slab,
    n_frames,
    raw_in,
    shift_in,
    foot_in,
    anchor_in,
    block_in,
    trace_in,
    z_ref,
    res_ref,
    raw_ref,
    shift_ref,
    foot_ref,
    anchor_ref,
    block_ref,
    trace_ref,
    fetched,
    pkt_out,
    pkt_in,
    early,
    late,
    mom_out,
    mom_in,
    image,
    rawx,
    mixed,
    corr,
    band,
    square,
    base_ref,
    e1_send,
    e1_recv,
    early_send,
    early_recv,
    late_send,
    late_recv,
    e3_send,
    e3_recv,
):
    me = lax.axis_index("slab")
    frame = lax.axis_index("frames")

    def slab_at(offset):
        return lax.rem(me + offset + 2 * n_slab, n_slab)

    def frame_at(offset):
        return lax.rem(frame + offset, n_frames)

    fetches = [
        pltpu.make_async_copy(source, target, fetched.at[i])
        for i, (source, target) in enumerate(
            (
                (foot_in, foot_ref),
                (anchor_in, anchor_ref),
                (trace_in, trace_ref),
                (raw_in, raw_ref),
                (shift_in, shift_ref),
                (block_in, block_ref),
            )
        )
    ]
    for fetch in fetches:
        fetch.start()

    barrier = pltpu.get_barrier_semaphore()

    def greet_slab(i, carry):
        for sign in (1, -1):
            pl.semaphore_signal(
                barrier,
                1,
                device_id={"slab": slab_at(sign * (HALO + 1 - i))},
                device_id_type=MESH,
            )
        return carry

    def greet_frame(i, carry):
        pl.semaphore_signal(barrier, 1, device_id={"frames": frame_at(i)}, device_id_type=MESH)
        return carry

    lax.fori_loop(1, HALO + 1, greet_slab, 0)
    lax.fori_loop(1, n_frames, greet_frame, 0)

    for fetch in fetches:
        fetch.wait()

    eye = iota((KD, KD), 0) == iota((KD, KD), 1)
    flat = mm_nt(jnp.where(eye, 1.0, 0.0).astype(BF16), foot_ref[...]).astype(BF16)
    own_row = column_of((anchor_ref[0:1, :] - (me * ROWS - RIM)).astype(F32))
    own_col = column_of(anchor_ref[1:2, :].astype(F32))
    start = [column_of(trace_ref[t : t + 1, :]) for t in range(2)]
    lane = iota((KD, COLS), 1)
    small = jnp.where(lane == 0, own_row, 0.0)
    small = jnp.where(lane == 1, own_col, small)
    for t in range(2):
        t_hi, t_rest = split(start[t])
        t_mid, t_lo = split(t_rest)
        for i, part in enumerate((t_hi, t_mid, t_lo)):
            small = jnp.where(lane == 2 + 2 * i + t, part, small)
    for side, patch in ((0, 0), (1, 1)):
        mine = small
        for which in range(2):
            for t in range(2):
                value = jnp.full((KD, COLS), shift_ref[which, t, 0, patch], jnp.int32).astype(F32)
                mine = jnp.where(lane == 8 + 2 * which + t, value, mine)
        top = 0 if side == 0 else ROWS - 16
        for t in range(2):
            pkt_out[side, 16 * t : 16 * t + 16, :] = raw_ref[t, top : top + 16, :]
        pkt_out[side, 32:64, :] = flat[:, 0:COLS]
        pkt_out[side, 64:96, :] = flat[:, COLS:]
        pkt_out[side, 96:128, :] = mine.astype(BF16)

    pl.semaphore_wait(barrier, 2 * HALO + n_frames - 1)

    def packet(side):
        return pltpu.make_async_remote_copy(
            src_ref=pkt_out.at[side],
            dst_ref=pkt_in.at[1 - side],
            send_sem=e1_send.at[side],
            recv_sem=e1_recv.at[1 - side],
            device_id={"slab": slab_at(-1 if side == 0 else 1)},
            device_id_type=MESH,
        )

    to_left, to_right = packet(0), packet(1)
    to_left.start()
    to_right.start()

    image[...] = jnp.zeros(image.shape, BF16)
    own_int = (own_row + jnp.zeros((KD, COLS), F32)).astype(jnp.int32)
    for y, value in enumerate(place_rows(own_int, place_columns(flat, own_col), 0, EXT)):
        if value is not None:
            image[0:KD, y * COLS : (y + 1) * COLS] = value.astype(BF16)
    own = image[0:KD, :]
    gram_own = mm_nt(own, own)
    norm_sq = jnp.sum(jnp.where(eye, gram_own, 0.0), axis=0, keepdims=True)
    def message(ref, send_sem, recv_sem, offset):
        slot = HALO - offset
        return pltpu.make_async_remote_copy(
            src_ref=ref.at[HALO, 0:10],
            dst_ref=ref.at[slot, 0:10],
            send_sem=send_sem,
            recv_sem=recv_sem,
            device_id={"slab": slab_at(offset)},
            device_id_type=MESH,
        )

    def send(ref, send_sem, recv_sem, i, carry):
        message(ref, send_sem, recv_sem, HALO + 1 - i).start()
        message(ref, send_sem, recv_sem, i - HALO - 1).start()
        return carry

    def arrived(ref, sem):
        whole = ref.at[0 : 2 * HALO, 0:10]
        pltpu.make_async_copy(whole, whole, sem).wait()

    early_set = (early, early_send, early_recv)
    late_set = (late, late_send, late_recv)

    def compact(gram):
        square[:, 0:KD] = gram
        total = square[0:8, :]
        for g in range(1, 4):
            total = total + pltpu.roll(square[8 * g : 8 * g + 8, :], KD * g, 1)
        return total

    square[...] = jnp.zeros((KD, COLS), F32)
    early[HALO, 0:8, :] = compact(gram_own)
    early[HALO, 8:16, :] = jnp.zeros((8, COLS), F32)
    early[HALO, 8:9, 0:KD] = 1.0 / norm_sq
    early[HALO, 9:10, 0:KD] = block_ref[...].astype(F32)
    lax.fori_loop(1, HALO + 1, functools.partial(send, *early_set), 0)

    def mix(t, low, high):
        at = t * 96 + low + 4
        mixed[t * 96 + low : t * 96 + high, :] = (
            0.75 * rawx[at : at + high - low, :] + 0.25 * rawx[at + 1 : at + 1 + high - low, :]
        )

    def correct(t, y0, n, down, across, keep):
        picked = jnp.zeros((n, COLS), F32)
        for a in range(-3, 4):
            at = t * 96 + y0 + 12 + a
            picked = jnp.where(down == a, mixed[at : at + n, :], picked)
        place = iota((n, COLS), 1)
        source = place + across.astype(jnp.int32)
        moved = jnp.take_along_axis(
            picked, source & (COLS - 1), axis=1, mode="promise_in_bounds"
        )
        moved = jnp.where((source >= 0) & (source < COLS), moved, 0.0)
        moved = moved.astype(BF16).astype(F32)
        if keep is not None:
            moved = moved * keep
        at = t * EXT + y0 + RIM
        corr[at : at + n, :] = moved

    def correct_own(t, y0, n):
        down, across = (
            jnp.full((n, COLS), shift_ref[which, t, 0, y0 // 32], jnp.int32).astype(F32)
            for which in range(2)
        )
        correct(t, y0, n, down, across, None)

    def frame_rows(low, high):
        rows = [corr[pl.ds(y, 8, stride=EXT), :] for y in range(low, high)]
        return jnp.concatenate(rows, axis=1).astype(BF16)

    corr[2 * EXT :, :] = jnp.zeros((6 * EXT, COLS), F32)
    for t in range(2):
        rawx[t * 96 + 16 : t * 96 + 80, :] = raw_ref[t].astype(F32)
        mix(t, 12, 75)
        correct_own(t, 8, 24)
        correct_own(t, 32, 24)
    q_inner = mm_nt(frame_rows(16, ROWS), image[0:KD, 16 * COLS : ROWS * COLS])

    for t in range(2):
        base_ref[t : t + 1, 0:KD] = q_inner[t : t + 1, :] - jnp.sum(
            gram_own * start[t], axis=0, keepdims=True
        )

    to_left.wait()
    to_right.wait()

    smalls = []
    valid = []
    for side in range(2):
        inside = me > 0 if side == 0 else me < n_slab - 1
        keep = jnp.where(inside, 1.0, 0.0).astype(F32)
        valid.append(keep)
        info = pkt_in[side, 96:128, :].astype(F32) * keep
        smalls.append(info)
        theirs = jnp.concatenate([pkt_in[side, 32:64, :], pkt_in[side, 64:96, :]], axis=1)
        wide = place_columns(theirs, info[:, 1:2])
        row = (info[:, 0:1] + jnp.zeros((KD, COLS), F32)).astype(jnp.int32)
        first = ROWS if side == 0 else 0
        low = 96 if side == 0 else 32
        for i, value in enumerate(place_rows(row, wide, first, 16)):
            if value is not None:
                y = i if side == 0 else ROWS + i
                image[low : low + KD, y * COLS : (y + 1) * COLS] = (value * keep).astype(BF16)
        for t in range(2):
            at = t * 96 + (0 if side == 0 else 80)
            rawx[at : at + 16, :] = pkt_in[side, 16 * t : 16 * t + 16, :].astype(F32) * keep

    for t in range(2):
        mix(t, 0, 12)
        mix(t, 75, 88)
        correct_own(t, 0, RIM)
        correct_own(t, ROWS - RIM, RIM)
        for side, y0 in ((0, -RIM), (1, ROWS)):
            info = smalls[side]
            down = jnp.broadcast_to(info[0:1, 8 + t : 9 + t], (RIM, COLS))
            across = jnp.broadcast_to(info[0:1, 10 + t : 11 + t], (RIM, COLS))
            correct(t, y0, RIM, down, across, valid[side])
    def edge(low, high, theirs):
        both = jnp.concatenate([theirs, frame_rows(low, high)], axis=0)
        out = mm_nt(both, image[0:KD, low * COLS : high * COLS])
        return out[0:KD, :], out[KD : KD + 8, :]

    gram_left, q_left = edge(0, 16, image[96:128, 0 : 16 * COLS])
    gram_right, q_right = edge(ROWS, EXT, image[32:64, ROWS * COLS :])
    q = base_ref[0:2, 0:KD] + q_left[0:2, :] + q_right[0:2, :]

    old = [start]
    for info in smalls:
        exact = info[:, 2:4] + info[:, 4:6] + info[:, 6:8]
        old.append([exact[:, t : t + 1] for t in range(2)])
    grams = (gram_left, gram_right)
    late[HALO, 0:8, :] = compact(gram_left)
    late[HALO, 8:16, :] = jnp.zeros((8, COLS), F32)
    for t in range(2):
        rendered = sum(
            jnp.sum(gram * x[t], axis=0, keepdims=True) for gram, x in zip(grams, old[1:])
        )
        late[HALO, 8 + t : 9 + t, 0:KD] = q[t : t + 1, :] - rendered
    lax.fori_loop(1, HALO + 1, functools.partial(send, *late_set), 0)

    lanes8 = iota((8, COLS), 1)
    wide_lane = iota((KD, COLS), 1)
    wide_row = iota((KD, COLS), 0)
    first_rows = []
    for x, low in zip(old, (0, 96, 32)):
        first_rows.append(
            [
                jnp.sum(
                    jnp.where(wide_lane - low == wide_row, x[t], 0.0),
                    axis=0,
                    keepdims=True,
                )
                for t in range(2)
            ]
        )

    def rows_of(pair):
        sub = iota((8, COLS), 0)
        return jnp.where(sub == 0, pair[0], 0.0) + jnp.where(sub == 1, pair[1], 0.0)

    own_x, left_x, right_x = (rows_of(pair) for pair in first_rows)

    arrived(early, early_recv)
    arrived(late, late_recv)

    group8 = lanes8 // KD

    def turned(value, turn):
        return value if turn % COLS == 0 else pltpu.roll(value, turn % COLS, 1)

    def keep_of(slot):
        where = me + (slot - HALO)
        return jnp.where((where >= 0) & (where < n_slab), 1.0, 0.0).astype(F32)

    def spread(tile, i):
        parts = [jnp.where(group8 == i, turned(tile, KD * (i - g)), 0.0) for g in range(4)]
        return jnp.concatenate(parts, axis=0)

    zero32 = jnp.zeros((KD, COLS), F32)
    zero8 = jnp.zeros((8, COLS), F32)
    state, gains = [], []
    before = zero32
    for m in range(CHUNKS):
        p_rows, gain_rows, diag, links = zero8, zero8, [], []
        for i in range(4):
            slot = 4 * m + i
            if slot < SLOTS:
                keep = keep_of(slot)
                rows = jnp.where(group8 == i, turned(late[slot, 8:16, :], KD * i), 0.0)
                p_rows = p_rows + rows * keep
                rows = jnp.where(group8 == i, turned(early[slot, 8:16, :], KD * i), 0.0)
                gain_rows = gain_rows + rows * keep
                diag.append(spread(early[slot, 0:8, :] * keep, i))
            else:
                diag.append(zero32)
            after = slot + 1
            if after < SLOTS:
                links.append(spread(late[after, 0:8, :] * keep_of(after), (i + 1) % 4))
            else:
                links.append(zero32)
        state.append(p_rows)
        gains.append(
            [jnp.where(gain_rows[1:2, :] == float(b), gain_rows[0:1, :], 0.0) for b in range(BLOCKS)]
        )
        upper = jnp.concatenate(links, axis=0)
        lower = upper.T
        corner = lower[0:KD, :]
        blocks = []
        for i in range(4):
            value = diag[i]
            if i < 3:
                value = value + links[i]
            if i > 0:
                value = value + lower[KD * i : KD * i + KD, :]
            blocks.append(value)
        for at, value in ((0, blocks[0]), (1, blocks[1]), (2, blocks[2]), (3, blocks[3]), (4, corner), (5, zero32), (6, zero32), (7, before)):
            hi, lo = split(value)
            band[m, at * KD : (at + 1) * KD, 0:COLS] = hi.astype(BF16)
            band[m, at * KD : (at + 1) * KD, COLS:] = lo.astype(BF16)
        before = links[3]

    total2 = jnp.where(lanes8 >= 96, left_x, 0.0)
    total3 = own_x + right_x
    for step in range(1, STEPS + 1):
        b = (step - 1) % BLOCKS
        low, high = max(step - 1, 0) // 4, min(2 * HALO + 1 - step, SLOTS - 1) // 4
        change = {m: state[m] * gains[m][b] for m in range(low, high + 1)}
        total2 = total2 + change[2]
        total3 = total3 + change[3]
        if step == STEPS:
            break
        zero = jnp.zeros((8, COLS), F32)
        for m in range(step // 4, (2 * HALO - step) // 4 + 1):
            beside = jnp.where(
                lanes8 >= 96,
                change.get(m - 1, zero),
                jnp.where(lanes8 < 32, change.get(m + 1, zero), 0.0),
            )
            a_hi, a_lo = split(change[m])
            b_hi, b_lo = split(beside)
            lhs = jnp.concatenate(
                [jnp.concatenate([a_hi, a_lo], axis=0), jnp.concatenate([b_hi, b_lo], axis=0)],
                axis=1,
            ).astype(BF16)
            out = mm(lhs, band[m])
            state[m] = state[m] - (out[0:8, 0:COLS] + out[8:16, 0:COLS] + out[0:8, COLS:])

    own_lane = lanes8 < 32
    two_rows = iota((8, COLS), 0) < 2
    final = jnp.where(own_lane & two_rows, total3, 0.0)
    mom_out[0:1, :] = jnp.sum(final, axis=0, keepdims=True)
    mom_out[1:2, :] = jnp.sum(final * final, axis=0, keepdims=True)

    def moments(i):
        return pltpu.make_async_remote_copy(
            src_ref=mom_out,
            dst_ref=mom_in.at[n_frames - i],
            send_sem=e3_send,
            recv_sem=e3_recv,
            device_id={"frames": frame_at(i)},
            device_id_type=MESH,
        )

    def send_moments(i, carry):
        moments(i).start()
        return carry

    lax.fori_loop(1, n_frames, send_moments, 0)

    all_x = jnp.where(lanes8 < 64, total3, jnp.where(lanes8 >= 96, total2, 0.0))
    x_hi, x_lo = split(all_x)
    lhs = jnp.concatenate([x_hi, x_lo], axis=0).astype(BF16)
    pieces = (
        mm(lhs, image[:, RIM * COLS : 16 * COLS]),
        mm(lhs[:, 0:KD], image[0:KD, 16 * COLS : ROWS * COLS]),
        mm(lhs, image[:, ROWS * COLS : (ROWS + RIM) * COLS]),
    )
    y = 0
    for piece in pieces:
        rendered = piece[0:8, :] + piece[8:16, :]
        for i in range(piece.shape[1] // COLS):
            rows = corr[pl.ds(y + RIM, 8, stride=EXT), :] - rendered[:, i * COLS : (i + 1) * COLS]
            res_ref[pl.ds(y, 2, stride=ROWS), :] = rows[0:2, :]
            y += 1

    arrived(early, early_send)
    arrived(late, late_send)
    others = mom_in.at[1:n_frames]
    pltpu.make_async_copy(others, others, e3_send).wait()
    pltpu.make_async_copy(others, others, e3_recv).wait()
    sums = mom_out[...]
    for i in range(1, n_frames):
        sums = sums + mom_in[i]
    count = 2 * n_frames
    mean = sums[0:1, :] / count
    square = sums[1:2, :] / count
    spread = square - mean * mean
    z_row = (total3[0:2, :] - mean) / jnp.sqrt(spread + EPSILON)
    z_ref[...] = z_row[:, 0:KD]


def hand_on(z_ref, res_ref, z_out, res_out, sems):
    copies = [
        pltpu.make_async_copy(res_ref, res_out, sems.at[0]),
        pltpu.make_async_copy(z_ref, z_out, sems.at[1]),
    ]
    for copy in copies:
        copy.start()
    for copy in copies:
        copy.wait()


def shards(n_slab, n_frames, raw_movie, shifts, footprints, anchors, block_of, init_traces):
    vmem = pl.BlockSpec(memory_space=pltpu.VMEM)
    dma = pltpu.SemaphoreType.DMA
    traces_z, residual = pl.pallas_call(
        functools.partial(kernel, n_slab, n_frames),
        out_shape=(
            pltpu.VMEM((2, KD), F32),
            pltpu.VMEM((2 * ROWS, COLS), F32),
        ),
        in_specs=[pl.BlockSpec(memory_space=pl.ANY)] * 6,
        out_specs=(vmem, vmem),
        scratch_shapes=[
            pltpu.VMEM((2, ROWS, COLS), BF16),
            pltpu.SMEM((2, 2, 1, 2), jnp.int32),
            pltpu.VMEM((TILE * TILE, KD), BF16),
            pltpu.VMEM((2, KD), jnp.int32),
            pltpu.VMEM((1, KD), jnp.int32),
            pltpu.VMEM((2, KD), F32),
            dma((6,)),
            pltpu.VMEM((2, 128, COLS), BF16),
            pltpu.VMEM((2, 128, COLS), BF16),
            pltpu.VMEM((SLOTS, 16, COLS), F32),
            pltpu.VMEM((SLOTS, 16, COLS), F32),
            pltpu.VMEM((2, COLS), F32),
            pltpu.VMEM((n_frames, 2, COLS), F32),
            pltpu.VMEM((128, EXT * COLS), BF16),
            pltpu.VMEM((192, COLS), F32),
            pltpu.VMEM((192, COLS), F32),
            pltpu.VMEM((8 * EXT, COLS), F32),
            pltpu.VMEM((CHUNKS, 256, 256), BF16),
            pltpu.VMEM((KD, COLS), F32),
            pltpu.VMEM((8, COLS), F32),
            dma((2,)),
            dma((2,)),
            dma,
            dma,
            dma,
            dma,
            dma,
            dma,
        ],
        compiler_params=pltpu.CompilerParams(collective_id=0, has_side_effects=True),
    )(
        raw_movie,
        shifts.transpose(0, 1, 3, 2),
        footprints.transpose(1, 2, 0).reshape(TILE * TILE, KD),
        anchors.T,
        block_of.reshape(1, KD),
        init_traces.T,
    )
    traces_z = pltpu.with_memory_space_constraint(traces_z, pltpu.VMEM)
    residual = pltpu.with_memory_space_constraint(residual, pltpu.VMEM)
    traces_z, residual = pl.pallas_call(
        hand_on,
        out_shape=(
            jax.ShapeDtypeStruct((2, KD), F32),
            jax.ShapeDtypeStruct((2 * ROWS, COLS), F32),
        ),
        in_specs=[pl.BlockSpec(memory_space=pltpu.VMEM)] * 2,
        out_specs=(pl.BlockSpec(memory_space=pltpu.HBM),) * 2,
        scratch_shapes=[dma((2,))],
    )(traces_z, residual)
    return traces_z.T, residual.reshape(2, ROWS, COLS)


def solution(mesh):
    in_specs = (
        P("frames", "slab", None),
        P(None, "frames", "slab", None),
        P("slab", None, None),
        P("slab", None),
        P("slab"),
        P("slab", "frames"),
    )
    out_specs = (P("slab", "frames"), P("frames", "slab", None))
    body = functools.partial(shards, mesh.shape["slab"], mesh.shape["frames"])
    return jax.shard_map(body, mesh=mesh, in_specs=in_specs, out_specs=out_specs, check_vma=False)
```

```python
import functools

import jax
import jax.numpy as jnp
from jax import lax
from jax.experimental import pallas as pl
from jax.experimental.pallas import tpu as pltpu
from jax.sharding import PartitionSpec as P

ROWS = 64
COLS = 128
KD = 32
TILE = 16
RIM = 8
EXT = 80
BLOCKS = 4
SWEEPS = 3
STEPS = BLOCKS * SWEEPS
HALO = STEPS
SLOTS = 2 * HALO + 1
CHUNKS = (SLOTS + 3) // 4
EPSILON = 1e-05
MESH = pl.DeviceIdType.MESH
F32 = jnp.float32
BF16 = jnp.bfloat16
NT = (((1,), (1,)), ((), ()))


def iota(shape, dim):
    return lax.broadcasted_iota(jnp.int32, shape, dim)


def mm(a, b):
    return jnp.dot(a, b, preferred_element_type=F32)


def mm_nt(a, b):
    return lax.dot_general(a, b, NT, preferred_element_type=F32)


def split(x):
    hi = x.astype(BF16).astype(F32)
    return hi, x - hi


def column_of(row):
    square = iota((KD, KD), 0) == iota((KD, KD), 1)
    return jnp.sum(jnp.where(square, row, 0.0), axis=1, keepdims=True)


def place_columns(flat, col):
    halves = [flat[:, 0:COLS].astype(F32), flat[:, COLS:].astype(F32)]
    offset = iota((KD, COLS), 1) - (col + jnp.zeros((KD, COLS), F32)).astype(jnp.int32)
    inside = (offset >= 0) & (offset < TILE)
    rows = []
    for i in range(TILE):
        lanes = (offset + TILE * (i % 8)) & (COLS - 1)
        taken = jnp.take_along_axis(halves[i // 8], lanes, axis=1, mode="promise_in_bounds")
        rows.append(jnp.where(inside, taken, 0.0))
    return rows


def place_rows(row, tile_rows, first, count):
    known = {}
    bits = [((row >> b) & 1) == 1 for b in range(6)]

    def at(level, y):
        if y < 0 or y > TILE - 1 + (1 << level) - 1:
            return None
        if level == 0:
            return tile_rows[y]
        if (level, y) not in known:
            moved = at(level - 1, y - (1 << (level - 1)))
            kept = at(level - 1, y)
            zero = jnp.zeros((KD, COLS), F32)
            bit = bits[level - 1]
            known[level, y] = jnp.where(
                bit, zero if moved is None else moved, zero if kept is None else kept
            )
        return known[level, y]

    return [at(6, y) for y in range(first, first + count)]


def kernel(
    n_slab,
    n_frames,
    raw_in,
    shift_in,
    foot_in,
    anchor_in,
    block_in,
    trace_in,
    z_ref,
    res_ref,
    raw_ref,
    shift_ref,
    foot_ref,
    anchor_ref,
    block_ref,
    trace_ref,
    fetched,
    pkt_out,
    pkt_in,
    early,
    late,
    mom_out,
    mom_in,
    image,
    rawx,
    mixed,
    corr,
    band,
    square,
    diag,
    gain_rows_ref,
    base_ref,
    e1_send,
    e1_recv,
    early_send,
    early_recv,
    late_send,
    late_recv,
    e3_send,
    e3_recv,
):
    me = lax.axis_index("slab")
    frame = lax.axis_index("frames")

    def slab_at(offset):
        return lax.rem(me + offset + 2 * n_slab, n_slab)

    def frame_at(offset):
        return lax.rem(frame + offset, n_frames)

    fetches = [
        pltpu.make_async_copy(source, target, fetched.at[i])
        for i, (source, target) in enumerate(
            (
                (foot_in, foot_ref),
                (anchor_in, anchor_ref),
                (trace_in, trace_ref),
                (raw_in, raw_ref),
                (shift_in, shift_ref),
                (block_in, block_ref),
            )
        )
    ]
    for fetch in fetches:
        fetch.start()

    barrier = pltpu.get_barrier_semaphore()

    def greet_slab(i, carry):
        for sign in (1, -1):
            pl.semaphore_signal(
                barrier,
                1,
                device_id={"slab": slab_at(sign * (HALO + 1 - i))},
                device_id_type=MESH,
            )
        return carry

    def greet_frame(i, carry):
        pl.semaphore_signal(barrier, 1, device_id={"frames": frame_at(i)}, device_id_type=MESH)
        return carry

    lax.fori_loop(1, HALO + 1, greet_slab, 0)
    lax.fori_loop(1, n_frames, greet_frame, 0)

    for fetch in fetches:
        fetch.wait()

    eye = iota((KD, KD), 0) == iota((KD, KD), 1)
    flat = mm_nt(jnp.where(eye, 1.0, 0.0).astype(BF16), foot_ref[...]).astype(BF16)
    own_row = column_of((anchor_ref[0:1, :] - (me * ROWS - RIM)).astype(F32))
    own_col = column_of(anchor_ref[1:2, :].astype(F32))
    start = [column_of(trace_ref[t : t + 1, :]) for t in range(2)]
    lane = iota((KD, COLS), 1)
    small = jnp.where(lane == 0, own_row, 0.0)
    small = jnp.where(lane == 1, own_col, small)
    for t in range(2):
        t_hi, t_rest = split(start[t])
        t_mid, t_lo = split(t_rest)
        for i, part in enumerate((t_hi, t_mid, t_lo)):
            small = jnp.where(lane == 2 + 2 * i + t, part, small)
    for side, patch in ((0, 0), (1, 1)):
        mine = small
        for which in range(2):
            for t in range(2):
                value = jnp.full((KD, COLS), shift_ref[which, t, 0, patch], jnp.int32).astype(F32)
                mine = jnp.where(lane == 8 + 2 * which + t, value, mine)
        top = 0 if side == 0 else ROWS - 16
        for t in range(2):
            pkt_out[side, 16 * t : 16 * t + 16, :] = raw_ref[t, top : top + 16, :]
        pkt_out[side, 32:64, :] = flat[:, 0:COLS]
        pkt_out[side, 64:96, :] = flat[:, COLS:]
        pkt_out[side, 96:128, :] = mine.astype(BF16)

    pl.semaphore_wait(barrier, 2 * HALO + n_frames - 1)

    def packet(side):
        return pltpu.make_async_remote_copy(
            src_ref=pkt_out.at[side],
            dst_ref=pkt_in.at[1 - side],
            send_sem=e1_send.at[side],
            recv_sem=e1_recv.at[1 - side],
            device_id={"slab": slab_at(-1 if side == 0 else 1)},
            device_id_type=MESH,
        )

    to_left, to_right = packet(0), packet(1)
    to_left.start()
    to_right.start()

    image[...] = jnp.zeros(image.shape, BF16)
    own_int = (own_row + jnp.zeros((KD, COLS), F32)).astype(jnp.int32)
    for y, value in enumerate(place_rows(own_int, place_columns(flat, own_col), 0, EXT)):
        if value is not None:
            image[0:KD, y * COLS : (y + 1) * COLS] = value.astype(BF16)
    own = image[0:KD, :]
    gram_own = mm_nt(own, own)
    norm_sq = jnp.sum(jnp.where(eye, gram_own, 0.0), axis=0, keepdims=True)
    def message(ref, send_sem, recv_sem, offset):
        slot = HALO - offset
        return pltpu.make_async_remote_copy(
            src_ref=ref.at[HALO, 0:10],
            dst_ref=ref.at[slot, 0:10],
            send_sem=send_sem,
            recv_sem=recv_sem,
            device_id={"slab": slab_at(offset)},
            device_id_type=MESH,
        )

    def send(ref, send_sem, recv_sem, i, carry):
        message(ref, send_sem, recv_sem, HALO + 1 - i).start()
        message(ref, send_sem, recv_sem, i - HALO - 1).start()
        return carry

    def arrived(ref, sem):
        whole = ref.at[0 : 2 * HALO, 0:10]
        pltpu.make_async_copy(whole, whole, sem).wait()

    early_set = (early, early_send, early_recv)
    late_set = (late, late_send, late_recv)

    def compact(gram):
        square[:, 0:KD] = gram
        total = square[0:8, :]
        for g in range(1, 4):
            total = total + pltpu.roll(square[8 * g : 8 * g + 8, :], KD * g, 1)
        return total

    square[...] = jnp.zeros((KD, COLS), F32)
    early[HALO, 0:8, :] = compact(gram_own)
    early[HALO, 8:16, :] = jnp.zeros((8, COLS), F32)
    early[HALO, 8:9, 0:KD] = 1.0 / norm_sq
    early[HALO, 9:10, 0:KD] = block_ref[...].astype(F32)
    lax.fori_loop(1, HALO + 1, functools.partial(send, *early_set), 0)

    def mix(t, low, high):
        at = t * 96 + low + 4
        mixed[t * 96 + low : t * 96 + high, :] = (
            0.75 * rawx[at : at + high - low, :] + 0.25 * rawx[at + 1 : at + 1 + high - low, :]
        )

    def correct(t, y0, n, down, across, keep):
        picked = jnp.zeros((n, COLS), F32)
        for a in range(-3, 4):
            at = t * 96 + y0 + 12 + a
            picked = jnp.where(down == a, mixed[at : at + n, :], picked)
        place = iota((n, COLS), 1)
        source = place + across.astype(jnp.int32)
        moved = jnp.take_along_axis(
            picked, source & (COLS - 1), axis=1, mode="promise_in_bounds"
        )
        moved = jnp.where((source >= 0) & (source < COLS), moved, 0.0)
        moved = moved.astype(BF16).astype(F32)
        if keep is not None:
            moved = moved * keep
        at = t * EXT + y0 + RIM
        corr[at : at + n, :] = moved

    def correct_own(t, y0, n):
        down, across = (
            jnp.full((n, COLS), shift_ref[which, t, 0, y0 // 32], jnp.int32).astype(F32)
            for which in range(2)
        )
        correct(t, y0, n, down, across, None)

    def frame_rows(low, high):
        rows = [corr[pl.ds(y, 8, stride=EXT), :] for y in range(low, high)]
        return jnp.concatenate(rows, axis=1).astype(BF16)

    corr[2 * EXT :, :] = jnp.zeros((6 * EXT, COLS), F32)
    for t in range(2):
        rawx[t * 96 + 16 : t * 96 + 80, :] = raw_ref[t].astype(F32)
        mix(t, 12, 75)
        correct_own(t, 8, 24)
        correct_own(t, 32, 24)
    q_inner = mm_nt(frame_rows(16, ROWS), image[0:KD, 16 * COLS : ROWS * COLS])

    for t in range(2):
        base_ref[t : t + 1, 0:KD] = q_inner[t : t + 1, :] - jnp.sum(
            gram_own * start[t], axis=0, keepdims=True
        )

    to_left.wait()
    to_right.wait()

    smalls = []
    valid = []
    for side in range(2):
        inside = me > 0 if side == 0 else me < n_slab - 1
        keep = jnp.where(inside, 1.0, 0.0).astype(F32)
        valid.append(keep)
        info = pkt_in[side, 96:128, :].astype(F32) * keep
        smalls.append(info)
        theirs = jnp.concatenate([pkt_in[side, 32:64, :], pkt_in[side, 64:96, :]], axis=1)
        wide = place_columns(theirs, info[:, 1:2])
        row = (info[:, 0:1] + jnp.zeros((KD, COLS), F32)).astype(jnp.int32)
        first = ROWS if side == 0 else 0
        low = 96 if side == 0 else 32
        for i, value in enumerate(place_rows(row, wide, first, 16)):
            if value is not None:
                y = i if side == 0 else ROWS + i
                image[low : low + KD, y * COLS : (y + 1) * COLS] = (value * keep).astype(BF16)
        for t in range(2):
            at = t * 96 + (0 if side == 0 else 80)
            rawx[at : at + 16, :] = pkt_in[side, 16 * t : 16 * t + 16, :].astype(F32) * keep

    for t in range(2):
        mix(t, 0, 12)
        mix(t, 75, 88)
        correct_own(t, 0, RIM)
        correct_own(t, ROWS - RIM, RIM)
        for side, y0 in ((0, -RIM), (1, ROWS)):
            info = smalls[side]
            down = jnp.broadcast_to(info[0:1, 8 + t : 9 + t], (RIM, COLS))
            across = jnp.broadcast_to(info[0:1, 10 + t : 11 + t], (RIM, COLS))
            correct(t, y0, RIM, down, across, valid[side])
    def edge(low, high, theirs):
        both = jnp.concatenate([theirs, frame_rows(low, high)], axis=0)
        out = mm_nt(both, image[0:KD, low * COLS : high * COLS])
        return out[0:KD, :], out[KD : KD + 8, :]

    gram_left, q_left = edge(0, 16, image[96:128, 0 : 16 * COLS])
    gram_right, q_right = edge(ROWS, EXT, image[32:64, ROWS * COLS :])
    q = base_ref[0:2, 0:KD] + q_left[0:2, :] + q_right[0:2, :]

    old = [start]
    for info in smalls:
        exact = info[:, 2:4] + info[:, 4:6] + info[:, 6:8]
        old.append([exact[:, t : t + 1] for t in range(2)])
    grams = (gram_left, gram_right)
    late[HALO, 0:8, :] = compact(gram_left)
    late[HALO, 8:16, :] = jnp.zeros((8, COLS), F32)
    for t in range(2):
        rendered = sum(
            jnp.sum(gram * x[t], axis=0, keepdims=True) for gram, x in zip(grams, old[1:])
        )
        late[HALO, 8 + t : 9 + t, 0:KD] = q[t : t + 1, :] - rendered
    lax.fori_loop(1, HALO + 1, functools.partial(send, *late_set), 0)

    lanes8 = iota((8, COLS), 1)
    wide_lane = iota((KD, COLS), 1)
    wide_row = iota((KD, COLS), 0)
    first_rows = []
    for x, low in zip(old, (0, 96, 32)):
        first_rows.append(
            [
                jnp.sum(
                    jnp.where(wide_lane - low == wide_row, x[t], 0.0),
                    axis=0,
                    keepdims=True,
                )
                for t in range(2)
            ]
        )

    def rows_of(pair):
        sub = iota((8, COLS), 0)
        return jnp.where(sub == 0, pair[0], 0.0) + jnp.where(sub == 1, pair[1], 0.0)

    own_x, left_x, right_x = (rows_of(pair) for pair in first_rows)

    arrived(early, early_recv)

    group8 = lanes8 // KD

    def turned(value, turn):
        return value if turn % COLS == 0 else pltpu.roll(value, turn % COLS, 1)

    def keep_of(slot):
        where = me + (slot - HALO)
        return jnp.where((where >= 0) & (where < n_slab), 1.0, 0.0).astype(F32)

    def spread(tile, i):
        parts = [jnp.where(group8 == i, turned(tile, KD * (i - g)), 0.0) for g in range(4)]
        return jnp.concatenate(parts, axis=0)

    zero32 = jnp.zeros((KD, COLS), F32)
    zero8 = jnp.zeros((8, COLS), F32)
    gains = []
    for m in range(CHUNKS):
        gain_rows = zero8
        for i in range(4):
            slot = 4 * m + i
            if slot < SLOTS:
                keep = keep_of(slot)
                rows = jnp.where(group8 == i, turned(early[slot, 8:16, :], KD * i), 0.0)
                gain_rows = gain_rows + rows * keep
                diag[m, KD * i : KD * i + KD, :] = spread(early[slot, 0:8, :] * keep, i)
            else:
                diag[m, KD * i : KD * i + KD, :] = zero32
        gain_rows_ref[m] = gain_rows

    arrived(late, late_recv)

    state = []
    before = zero32
    for m in range(CHUNKS):
        gain_rows = gain_rows_ref[m]
        gains.append(
            [jnp.where(gain_rows[1:2, :] == float(b), gain_rows[0:1, :], 0.0) for b in range(BLOCKS)]
        )
        p_rows, links = zero8, []
        for i in range(4):
            slot = 4 * m + i
            if slot < SLOTS:
                rows = jnp.where(group8 == i, turned(late[slot, 8:16, :], KD * i), 0.0)
                p_rows = p_rows + rows * keep_of(slot)
            after = slot + 1
            if after < SLOTS:
                links.append(spread(late[after, 0:8, :] * keep_of(after), (i + 1) % 4))
            else:
                links.append(zero32)
        state.append(p_rows)
        lower = jnp.concatenate(links, axis=0).T
        blocks = []
        for i in range(4):
            value = diag[m, KD * i : KD * i + KD, :]
            if i < 3:
                value = value + links[i]
            if i > 0:
                value = value + lower[KD * i : KD * i + KD, :]
            blocks.append(value)
        blocks += [lower[0:KD, :], zero32, zero32, before]
        for at, value in enumerate(blocks):
            hi, lo = split(value)
            band[m, at * KD : (at + 1) * KD, 0:COLS] = hi.astype(BF16)
            band[m, at * KD : (at + 1) * KD, COLS:] = lo.astype(BF16)
        before = links[3]

    total2 = jnp.where(lanes8 >= 96, left_x, 0.0)
    total3 = own_x + right_x
    for step in range(1, STEPS + 1):
        b = (step - 1) % BLOCKS
        low, high = max(step - 1, 0) // 4, min(2 * HALO + 1 - step, SLOTS - 1) // 4
        change = {m: state[m] * gains[m][b] for m in range(low, high + 1)}
        total2 = total2 + change[2]
        total3 = total3 + change[3]
        if step == STEPS:
            break
        zero = jnp.zeros((8, COLS), F32)
        for m in range(step // 4, (2 * HALO - step) // 4 + 1):
            beside = jnp.where(
                lanes8 >= 96,
                change.get(m - 1, zero),
                jnp.where(lanes8 < 32, change.get(m + 1, zero), 0.0),
            )
            a_hi, a_lo = split(change[m])
            b_hi, b_lo = split(beside)
            lhs = jnp.concatenate(
                [jnp.concatenate([a_hi, a_lo], axis=0), jnp.concatenate([b_hi, b_lo], axis=0)],
                axis=1,
            ).astype(BF16)
            out = mm(lhs, band[m])
            state[m] = state[m] - (out[0:8, 0:COLS] + out[8:16, 0:COLS] + out[0:8, COLS:])

    own_lane = lanes8 < 32
    two_rows = iota((8, COLS), 0) < 2
    final = jnp.where(own_lane & two_rows, total3, 0.0)
    mom_out[0:1, :] = jnp.sum(final, axis=0, keepdims=True)
    mom_out[1:2, :] = jnp.sum(final * final, axis=0, keepdims=True)

    def moments(i):
        return pltpu.make_async_remote_copy(
            src_ref=mom_out,
            dst_ref=mom_in.at[n_frames - i],
            send_sem=e3_send,
            recv_sem=e3_recv,
            device_id={"frames": frame_at(i)},
            device_id_type=MESH,
        )

    def send_moments(i, carry):
        moments(i).start()
        return carry

    lax.fori_loop(1, n_frames, send_moments, 0)

    all_x = jnp.where(lanes8 < 64, total3, jnp.where(lanes8 >= 96, total2, 0.0))
    x_hi, x_lo = split(all_x)
    lhs = jnp.concatenate([x_hi, x_lo], axis=0).astype(BF16)
    pieces = (
        mm(lhs, image[:, RIM * COLS : 16 * COLS]),
        mm(lhs[:, 0:KD], image[0:KD, 16 * COLS : ROWS * COLS]),
        mm(lhs, image[:, ROWS * COLS : (ROWS + RIM) * COLS]),
    )
    y = 0
    for piece in pieces:
        rendered = piece[0:8, :] + piece[8:16, :]
        for i in range(piece.shape[1] // COLS):
            rows = corr[pl.ds(y + RIM, 8, stride=EXT), :] - rendered[:, i * COLS : (i + 1) * COLS]
            res_ref[pl.ds(y, 2, stride=ROWS), :] = rows[0:2, :]
            y += 1

    arrived(early, early_send)
    arrived(late, late_send)
    others = mom_in.at[1:n_frames]
    pltpu.make_async_copy(others, others, e3_send).wait()
    pltpu.make_async_copy(others, others, e3_recv).wait()
    sums = mom_out[...]
    for i in range(1, n_frames):
        sums = sums + mom_in[i]
    count = 2 * n_frames
    mean = sums[0:1, :] / count
    square = sums[1:2, :] / count
    spread = square - mean * mean
    z_row = (total3[0:2, :] - mean) / jnp.sqrt(spread + EPSILON)
    z_ref[...] = z_row[:, 0:KD]


def hand_on(z_ref, res_ref, z_out, res_out, sems):
    copies = [
        pltpu.make_async_copy(res_ref, res_out, sems.at[0]),
        pltpu.make_async_copy(z_ref, z_out, sems.at[1]),
    ]
    for copy in copies:
        copy.start()
    for copy in copies:
        copy.wait()


def shards(n_slab, n_frames, raw_movie, shifts, footprints, anchors, block_of, init_traces):
    vmem = pl.BlockSpec(memory_space=pltpu.VMEM)
    dma = pltpu.SemaphoreType.DMA
    traces_z, residual = pl.pallas_call(
        functools.partial(kernel, n_slab, n_frames),
        out_shape=(
            pltpu.VMEM((2, KD), F32),
            pltpu.VMEM((2 * ROWS, COLS), F32),
        ),
        in_specs=[pl.BlockSpec(memory_space=pl.ANY)] * 6,
        out_specs=(vmem, vmem),
        scratch_shapes=[
            pltpu.VMEM((2, ROWS, COLS), BF16),
            pltpu.SMEM((2, 2, 1, 2), jnp.int32),
            pltpu.VMEM((TILE * TILE, KD), BF16),
            pltpu.VMEM((2, KD), jnp.int32),
            pltpu.VMEM((1, KD), jnp.int32),
            pltpu.VMEM((2, KD), F32),
            dma((6,)),
            pltpu.VMEM((2, 128, COLS), BF16),
            pltpu.VMEM((2, 128, COLS), BF16),
            pltpu.VMEM((SLOTS, 16, COLS), F32),
            pltpu.VMEM((SLOTS, 16, COLS), F32),
            pltpu.VMEM((2, COLS), F32),
            pltpu.VMEM((n_frames, 2, COLS), F32),
            pltpu.VMEM((128, EXT * COLS), BF16),
            pltpu.VMEM((192, COLS), F32),
            pltpu.VMEM((192, COLS), F32),
            pltpu.VMEM((8 * EXT, COLS), F32),
            pltpu.VMEM((CHUNKS, 256, 256), BF16),
            pltpu.VMEM((KD, COLS), F32),
            pltpu.VMEM((CHUNKS, COLS, COLS), F32),
            pltpu.VMEM((CHUNKS, 8, COLS), F32),
            pltpu.VMEM((8, COLS), F32),
            dma((2,)),
            dma((2,)),
            dma,
            dma,
            dma,
            dma,
            dma,
            dma,
        ],
        compiler_params=pltpu.CompilerParams(collective_id=0, has_side_effects=True),
    )(
        raw_movie,
        shifts.transpose(0, 1, 3, 2),
        footprints.transpose(1, 2, 0).reshape(TILE * TILE, KD),
        anchors.T,
        block_of.reshape(1, KD),
        init_traces.T,
    )
    traces_z = pltpu.with_memory_space_constraint(traces_z, pltpu.VMEM)
    residual = pltpu.with_memory_space_constraint(residual, pltpu.VMEM)
    traces_z, residual = pl.pallas_call(
        hand_on,
        out_shape=(
            jax.ShapeDtypeStruct((2, KD), F32),
            jax.ShapeDtypeStruct((2 * ROWS, COLS), F32),
        ),
        in_specs=[pl.BlockSpec(memory_space=pltpu.VMEM)] * 2,
        out_specs=(pl.BlockSpec(memory_space=pltpu.HBM),) * 2,
        scratch_shapes=[dma((2,))],
    )(traces_z, residual)
    return traces_z.T, residual.reshape(2, ROWS, COLS)


def solution(mesh):
    in_specs = (
        P("frames", "slab", None),
        P(None, "frames", "slab", None),
        P("slab", None, None),
        P("slab", None),
        P("slab"),
        P("slab", "frames"),
    )
    out_specs = (P("slab", "frames"), P("frames", "slab", None))
    body = functools.partial(shards, mesh.shape["slab"], mesh.shape["frames"])
    return jax.shard_map(body, mesh=mesh, in_specs=in_specs, out_specs=out_specs, check_vma=False)
```

```python
import functools

import jax
import jax.numpy as jnp
from jax import lax
from jax.experimental import pallas as pl
from jax.experimental.pallas import tpu as pltpu
from jax.sharding import PartitionSpec as P

ROWS = 64
COLS = 128
KD = 32
TILE = 16
RIM = 8
EXT = 80
BLOCKS = 4
SWEEPS = 3
STEPS = BLOCKS * SWEEPS
HALO = STEPS
SLOTS = 2 * HALO + 1
CHUNKS = (SLOTS + 3) // 4
EPSILON = 1e-05
MESH = pl.DeviceIdType.MESH
F32 = jnp.float32
BF16 = jnp.bfloat16
NT = (((1,), (1,)), ((), ()))


def iota(shape, dim):
    return lax.broadcasted_iota(jnp.int32, shape, dim)


def mm(a, b):
    return jnp.dot(a, b, preferred_element_type=F32)


def mm_nt(a, b):
    return lax.dot_general(a, b, NT, preferred_element_type=F32)


def split(x):
    hi = x.astype(BF16).astype(F32)
    return hi, x - hi


def column_of(row):
    square = iota((KD, KD), 0) == iota((KD, KD), 1)
    return jnp.sum(jnp.where(square, row, 0.0), axis=1, keepdims=True)


def place_columns(flat, col):
    halves = [flat[:, 0:COLS].astype(F32), flat[:, COLS:].astype(F32)]
    offset = iota((KD, COLS), 1) - (col + jnp.zeros((KD, COLS), F32)).astype(jnp.int32)
    inside = (offset >= 0) & (offset < TILE)
    rows = []
    for i in range(TILE):
        lanes = (offset + TILE * (i % 8)) & (COLS - 1)
        taken = jnp.take_along_axis(halves[i // 8], lanes, axis=1, mode="promise_in_bounds")
        rows.append(jnp.where(inside, taken, 0.0))
    return rows


def place_rows(row, tile_rows, first, count):
    known = {}
    bits = [((row >> b) & 1) == 1 for b in range(6)]

    def at(level, y):
        if y < 0 or y > TILE - 1 + (1 << level) - 1:
            return None
        if level == 0:
            return tile_rows[y]
        if (level, y) not in known:
            moved = at(level - 1, y - (1 << (level - 1)))
            kept = at(level - 1, y)
            zero = jnp.zeros((KD, COLS), F32)
            bit = bits[level - 1]
            known[level, y] = jnp.where(
                bit, zero if moved is None else moved, zero if kept is None else kept
            )
        return known[level, y]

    return [at(6, y) for y in range(first, first + count)]


def kernel(
    n_slab,
    n_frames,
    raw_in,
    shift_in,
    foot_in,
    anchor_in,
    block_in,
    trace_in,
    z_ref,
    res_ref,
    raw_ref,
    shift_ref,
    foot_ref,
    anchor_ref,
    block_ref,
    trace_ref,
    fetched,
    pkt_out,
    pkt_in,
    early,
    late,
    mom_out,
    mom_in,
    image,
    rawx,
    mixed,
    corr,
    band,
    square,
    base_ref,
    e1_send,
    e1_recv,
    early_send,
    early_recv,
    late_send,
    late_recv,
    e3_send,
    e3_recv,
):
    me = lax.axis_index("slab")
    frame = lax.axis_index("frames")

    def slab_at(offset):
        return lax.rem(me + offset + 2 * n_slab, n_slab)

    def frame_at(offset):
        return lax.rem(frame + offset, n_frames)

    fetches = [
        pltpu.make_async_copy(source, target, fetched.at[i])
        for i, (source, target) in enumerate(
            (
                (foot_in, foot_ref),
                (anchor_in, anchor_ref),
                (trace_in, trace_ref),
                (raw_in, raw_ref),
                (shift_in, shift_ref),
                (block_in, block_ref),
            )
        )
    ]
    for fetch in fetches:
        fetch.start()

    barrier = pltpu.get_barrier_semaphore()

    def greet_slab(i, carry):
        for sign in (1, -1):
            pl.semaphore_signal(
                barrier,
                1,
                device_id={"slab": slab_at(sign * (HALO + 1 - i))},
                device_id_type=MESH,
            )
        return carry

    def greet_frame(i, carry):
        pl.semaphore_signal(barrier, 1, device_id={"frames": frame_at(i)}, device_id_type=MESH)
        return carry

    lax.fori_loop(1, HALO + 1, greet_slab, 0)
    lax.fori_loop(1, n_frames, greet_frame, 0)

    for fetch in fetches:
        fetch.wait()

    eye = iota((KD, KD), 0) == iota((KD, KD), 1)
    flat = mm_nt(jnp.where(eye, 1.0, 0.0).astype(BF16), foot_ref[...]).astype(BF16)
    own_row = column_of((anchor_ref[0:1, :] - (me * ROWS - RIM)).astype(F32))
    own_col = column_of(anchor_ref[1:2, :].astype(F32))
    start = [column_of(trace_ref[t : t + 1, :]) for t in range(2)]
    lane = iota((KD, COLS), 1)
    small = jnp.where(lane == 0, own_row, 0.0)
    small = jnp.where(lane == 1, own_col, small)
    for t in range(2):
        t_hi, t_rest = split(start[t])
        t_mid, t_lo = split(t_rest)
        for i, part in enumerate((t_hi, t_mid, t_lo)):
            small = jnp.where(lane == 2 + 2 * i + t, part, small)
    for side, patch in ((0, 0), (1, 1)):
        mine = small
        for which in range(2):
            for t in range(2):
                value = jnp.full((KD, COLS), shift_ref[which, t, 0, patch], jnp.int32).astype(F32)
                mine = jnp.where(lane == 8 + 2 * which + t, value, mine)
        top = 0 if side == 0 else ROWS - 16
        for t in range(2):
            pkt_out[side, 16 * t : 16 * t + 16, :] = raw_ref[t, top : top + 16, :]
        pkt_out[side, 32:64, :] = flat[:, 0:COLS]
        pkt_out[side, 64:96, :] = flat[:, COLS:]
        pkt_out[side, 96:128, :] = mine.astype(BF16)

    pl.semaphore_wait(barrier, 2 * HALO + n_frames - 1)

    def packet(side):
        return pltpu.make_async_remote_copy(
            src_ref=pkt_out.at[side],
            dst_ref=pkt_in.at[1 - side],
            send_sem=e1_send.at[side],
            recv_sem=e1_recv.at[1 - side],
            device_id={"slab": slab_at(-1 if side == 0 else 1)},
            device_id_type=MESH,
        )

    to_left, to_right = packet(0), packet(1)
    to_left.start()
    to_right.start()

    image[...] = jnp.zeros(image.shape, BF16)
    own_int = (own_row + jnp.zeros((KD, COLS), F32)).astype(jnp.int32)
    for y, value in enumerate(place_rows(own_int, place_columns(flat, own_col), 0, EXT)):
        if value is not None:
            image[0:KD, y * COLS : (y + 1) * COLS] = value.astype(BF16)
    own = image[0:KD, :]
    gram_own = mm_nt(own, own)
    norm_sq = jnp.sum(jnp.where(eye, gram_own, 0.0), axis=0, keepdims=True)
    def message(ref, send_sem, recv_sem, offset):
        slot = HALO - offset
        return pltpu.make_async_remote_copy(
            src_ref=ref.at[HALO, 0:10],
            dst_ref=ref.at[slot, 0:10],
            send_sem=send_sem,
            recv_sem=recv_sem,
            device_id={"slab": slab_at(offset)},
            device_id_type=MESH,
        )

    def send(ref, send_sem, recv_sem, i, carry):
        message(ref, send_sem, recv_sem, HALO + 1 - i).start()
        message(ref, send_sem, recv_sem, i - HALO - 1).start()
        return carry

    def arrived(ref, sem):
        whole = ref.at[0 : 2 * HALO, 0:10]
        pltpu.make_async_copy(whole, whole, sem).wait()

    early_set = (early, early_send, early_recv)
    late_set = (late, late_send, late_recv)

    def compact(gram):
        square[:, 0:KD] = gram
        total = square[0:8, :]
        for g in range(1, 4):
            total = total + pltpu.roll(square[8 * g : 8 * g + 8, :], KD * g, 1)
        return total

    square[...] = jnp.zeros((KD, COLS), F32)
    early[HALO, 0:8, :] = compact(gram_own)
    early[HALO, 8:16, :] = jnp.zeros((8, COLS), F32)
    early[HALO, 8:9, 0:KD] = 1.0 / norm_sq
    early[HALO, 9:10, 0:KD] = block_ref[...].astype(F32)
    lax.fori_loop(1, HALO + 1, functools.partial(send, *early_set), 0)

    def mix(t, low, high):
        at = t * 96 + low + 4
        mixed[t * 96 + low : t * 96 + high, :] = (
            0.75 * rawx[at : at + high - low, :] + 0.25 * rawx[at + 1 : at + 1 + high - low, :]
        )

    def correct(t, y0, n, down, across, keep):
        picked = jnp.zeros((n, COLS), F32)
        for a in range(-3, 4):
            at = t * 96 + y0 + 12 + a
            picked = jnp.where(down == a, mixed[at : at + n, :], picked)
        place = iota((n, COLS), 1)
        source = place + across.astype(jnp.int32)
        moved = jnp.take_along_axis(
            picked, source & (COLS - 1), axis=1, mode="promise_in_bounds"
        )
        moved = jnp.where((source >= 0) & (source < COLS), moved, 0.0)
        moved = moved.astype(BF16).astype(F32)
        if keep is not None:
            moved = moved * keep
        at = t * EXT + y0 + RIM
        corr[at : at + n, :] = moved

    def correct_own(t, y0, n):
        down, across = (
            jnp.full((n, COLS), shift_ref[which, t, 0, y0 // 32], jnp.int32).astype(F32)
            for which in range(2)
        )
        correct(t, y0, n, down, across, None)

    def frame_rows(low, high):
        rows = [corr[pl.ds(y, 8, stride=EXT), :] for y in range(low, high)]
        return jnp.concatenate(rows, axis=1).astype(BF16)

    corr[2 * EXT :, :] = jnp.zeros((6 * EXT, COLS), F32)
    for t in range(2):
        rawx[t * 96 + 16 : t * 96 + 80, :] = raw_ref[t].astype(F32)
        mix(t, 12, 75)
        correct_own(t, 8, 24)
        correct_own(t, 32, 24)
    q_inner = mm_nt(frame_rows(16, ROWS), image[0:KD, 16 * COLS : ROWS * COLS])

    for t in range(2):
        base_ref[t : t + 1, 0:KD] = q_inner[t : t + 1, :] - jnp.sum(
            gram_own * start[t], axis=0, keepdims=True
        )

    to_left.wait()
    to_right.wait()

    smalls = []
    valid = []
    for side in range(2):
        inside = me > 0 if side == 0 else me < n_slab - 1
        keep = jnp.where(inside, 1.0, 0.0).astype(F32)
        valid.append(keep)
        info = pkt_in[side, 96:128, :].astype(F32) * keep
        smalls.append(info)
        theirs = jnp.concatenate([pkt_in[side, 32:64, :], pkt_in[side, 64:96, :]], axis=1)
        wide = place_columns(theirs, info[:, 1:2])
        row = (info[:, 0:1] + jnp.zeros((KD, COLS), F32)).astype(jnp.int32)
        first = ROWS if side == 0 else 0
        low = 96 if side == 0 else 32
        for i, value in enumerate(place_rows(row, wide, first, 16)):
            if value is not None:
                y = i if side == 0 else ROWS + i
                image[low : low + KD, y * COLS : (y + 1) * COLS] = (value * keep).astype(BF16)
        for t in range(2):
            at = t * 96 + (0 if side == 0 else 80)
            rawx[at : at + 16, :] = pkt_in[side, 16 * t : 16 * t + 16, :].astype(F32) * keep

    for t in range(2):
        mix(t, 0, 12)
        mix(t, 75, 88)
        correct_own(t, 0, RIM)
        correct_own(t, ROWS - RIM, RIM)
        for side, y0 in ((0, -RIM), (1, ROWS)):
            info = smalls[side]
            down = jnp.broadcast_to(info[0:1, 8 + t : 9 + t], (RIM, COLS))
            across = jnp.broadcast_to(info[0:1, 10 + t : 11 + t], (RIM, COLS))
            correct(t, y0, RIM, down, across, valid[side])
    def edge(low, high, theirs):
        both = jnp.concatenate([theirs, frame_rows(low, high)], axis=0)
        out = mm_nt(both, image[0:KD, low * COLS : high * COLS])
        return out[0:KD, :], out[KD : KD + 8, :]

    gram_left, q_left = edge(0, 16, image[96:128, 0 : 16 * COLS])
    gram_right, q_right = edge(ROWS, EXT, image[32:64, ROWS * COLS :])
    q = base_ref[0:2, 0:KD] + q_left[0:2, :] + q_right[0:2, :]

    old = [start]
    for info in smalls:
        exact = info[:, 2:4] + info[:, 4:6] + info[:, 6:8]
        old.append([exact[:, t : t + 1] for t in range(2)])
    grams = (gram_left, gram_right)
    late[HALO, 0:8, :] = compact(gram_left)
    late[HALO, 8:16, :] = jnp.zeros((8, COLS), F32)
    for t in range(2):
        rendered = sum(
            jnp.sum(gram * x[t], axis=0, keepdims=True) for gram, x in zip(grams, old[1:])
        )
        late[HALO, 8 + t : 9 + t, 0:KD] = q[t : t + 1, :] - rendered
    lax.fori_loop(1, HALO + 1, functools.partial(send, *late_set), 0)

    lanes8 = iota((8, COLS), 1)
    wide_lane = iota((KD, COLS), 1)
    wide_row = iota((KD, COLS), 0)
    first_rows = []
    for x, low in zip(old, (0, 96, 32)):
        first_rows.append(
            [
                jnp.sum(
                    jnp.where(wide_lane - low == wide_row, x[t], 0.0),
                    axis=0,
                    keepdims=True,
                )
                for t in range(2)
            ]
        )

    def rows_of(pair):
        sub = iota((8, COLS), 0)
        return jnp.where(sub == 0, pair[0], 0.0) + jnp.where(sub == 1, pair[1], 0.0)

    own_x, left_x, right_x = (rows_of(pair) for pair in first_rows)

    arrived(early, early_recv)
    arrived(late, late_recv)

    group8 = lanes8 // KD

    def turned(value, turn):
        return value if turn % COLS == 0 else pltpu.roll(value, turn % COLS, 1)

    def keep_of(slot):
        where = me + (slot - HALO)
        return jnp.where((where >= 0) & (where < n_slab), 1.0, 0.0).astype(F32)

    def spread(tile, i):
        parts = [jnp.where(group8 == i, turned(tile, KD * (i - g)), 0.0) for g in range(4)]
        return jnp.concatenate(parts, axis=0)

    zero32 = jnp.zeros((KD, COLS), F32)
    zero8 = jnp.zeros((8, COLS), F32)
    state, gains = [], []
    before = zero32
    for m in range(CHUNKS):
        p_rows, gain_rows, diag, links = zero8, zero8, [], []
        for i in range(4):
            slot = 4 * m + i
            if slot < SLOTS:
                keep = keep_of(slot)
                rows = jnp.where(group8 == i, turned(late[slot, 8:16, :], KD * i), 0.0)
                p_rows = p_rows + rows * keep
                rows = jnp.where(group8 == i, turned(early[slot, 8:16, :], KD * i), 0.0)
                gain_rows = gain_rows + rows * keep
                diag.append(spread(early[slot, 0:8, :] * keep, i))
            else:
                diag.append(zero32)
            after = slot + 1
            if after < SLOTS:
                links.append(spread(late[after, 0:8, :] * keep_of(after), (i + 1) % 4))
            else:
                links.append(zero32)
        state.append(p_rows)
        gains.append(
            [jnp.where(gain_rows[1:2, :] == float(b), gain_rows[0:1, :], 0.0) for b in range(BLOCKS)]
        )
        upper = jnp.concatenate(links, axis=0)
        lower = upper.T
        corner = lower[0:KD, :]
        blocks = []
        for i in range(4):
            value = diag[i]
            if i < 3:
                value = value + links[i]
            if i > 0:
                value = value + lower[KD * i : KD * i + KD, :]
            blocks.append(value)
        for at, value in ((0, blocks[0]), (1, blocks[1]), (2, blocks[2]), (3, blocks[3]), (4, corner), (5, zero32), (6, zero32), (7, before)):
            hi, lo = split(value)
            band[m, at * KD : (at + 1) * KD, 0:COLS] = hi.astype(BF16)
            band[m, at * KD : (at + 1) * KD, COLS:] = lo.astype(BF16)
        before = links[3]

    low_rows = (iota((8, COLS), 0) // 2) % 2 == 1
    state = [p + pltpu.roll(p, 2, 0) for p in state]
    state = [p + pltpu.roll(p, 4, 0) for p in state]
    total2 = jnp.where(lanes8 >= 96, left_x, 0.0)
    total3 = own_x + right_x
    for step in range(1, STEPS + 1):
        b = (step - 1) % BLOCKS
        low, high = max(step - 1, 0) // 4, min(2 * HALO + 1 - step, SLOTS - 1) // 4
        change = {m: state[m] * gains[m][b] for m in range(low, high + 1)}
        total2 = total2 + change[2]
        total3 = total3 + change[3]
        if step == STEPS:
            break
        parts = {}
        for m, value in change.items():
            hi, lo = split(value)
            parts[m] = jnp.where(low_rows, lo, hi)
        for m in range(step // 4, (2 * HALO - step) // 4 + 1):
            beside = jnp.where(
                lanes8 >= 96,
                parts.get(m - 1, zero8),
                jnp.where(lanes8 < 32, parts.get(m + 1, zero8), 0.0),
            )
            lhs = jnp.concatenate([parts[m], beside], axis=1).astype(BF16)
            out = mm(lhs, band[m])
            both = out[:, 0:COLS] + out[:, COLS:]
            state[m] = state[m] - (both + pltpu.roll(both, 2, 0))

    own_lane = lanes8 < 32
    two_rows = iota((8, COLS), 0) < 2
    final = jnp.where(own_lane & two_rows, total3, 0.0)
    mom_out[0:1, :] = jnp.sum(final, axis=0, keepdims=True)
    mom_out[1:2, :] = jnp.sum(final * final, axis=0, keepdims=True)

    def moments(i):
        return pltpu.make_async_remote_copy(
            src_ref=mom_out,
            dst_ref=mom_in.at[n_frames - i],
            send_sem=e3_send,
            recv_sem=e3_recv,
            device_id={"frames": frame_at(i)},
            device_id_type=MESH,
        )

    def send_moments(i, carry):
        moments(i).start()
        return carry

    lax.fori_loop(1, n_frames, send_moments, 0)

    all_x = jnp.where(lanes8 < 64, total3, jnp.where(lanes8 >= 96, total2, 0.0))
    x_hi, x_lo = split(all_x)
    lhs = jnp.concatenate([x_hi, x_lo], axis=0).astype(BF16)
    pieces = (
        mm(lhs, image[:, RIM * COLS : 16 * COLS]),
        mm(lhs[:, 0:KD], image[0:KD, 16 * COLS : ROWS * COLS]),
        mm(lhs, image[:, ROWS * COLS : (ROWS + RIM) * COLS]),
    )
    y = 0
    for piece in pieces:
        rendered = piece[0:8, :] + piece[8:16, :]
        for i in range(piece.shape[1] // COLS):
            rows = corr[pl.ds(y + RIM, 8, stride=EXT), :] - rendered[:, i * COLS : (i + 1) * COLS]
            res_ref[pl.ds(y, 2, stride=ROWS), :] = rows[0:2, :]
            y += 1

    arrived(early, early_send)
    arrived(late, late_send)
    others = mom_in.at[1:n_frames]
    pltpu.make_async_copy(others, others, e3_send).wait()
    pltpu.make_async_copy(others, others, e3_recv).wait()
    sums = mom_out[...]
    for i in range(1, n_frames):
        sums = sums + mom_in[i]
    count = 2 * n_frames
    mean = sums[0:1, :] / count
    square = sums[1:2, :] / count
    spread = square - mean * mean
    z_row = (total3[0:2, :] - mean) / jnp.sqrt(spread + EPSILON)
    z_ref[...] = z_row[:, 0:KD]


def hand_on(z_ref, res_ref, z_out, res_out, sems):
    copies = [
        pltpu.make_async_copy(res_ref, res_out, sems.at[0]),
        pltpu.make_async_copy(z_ref, z_out, sems.at[1]),
    ]
    for copy in copies:
        copy.start()
    for copy in copies:
        copy.wait()


def shards(n_slab, n_frames, raw_movie, shifts, footprints, anchors, block_of, init_traces):
    vmem = pl.BlockSpec(memory_space=pltpu.VMEM)
    dma = pltpu.SemaphoreType.DMA
    traces_z, residual = pl.pallas_call(
        functools.partial(kernel, n_slab, n_frames),
        out_shape=(
            pltpu.VMEM((2, KD), F32),
            pltpu.VMEM((2 * ROWS, COLS), F32),
        ),
        in_specs=[pl.BlockSpec(memory_space=pl.ANY)] * 6,
        out_specs=(vmem, vmem),
        scratch_shapes=[
            pltpu.VMEM((2, ROWS, COLS), BF16),
            pltpu.SMEM((2, 2, 1, 2), jnp.int32),
            pltpu.VMEM((TILE * TILE, KD), BF16),
            pltpu.VMEM((2, KD), jnp.int32),
            pltpu.VMEM((1, KD), jnp.int32),
            pltpu.VMEM((2, KD), F32),
            dma((6,)),
            pltpu.VMEM((2, 128, COLS), BF16),
            pltpu.VMEM((2, 128, COLS), BF16),
            pltpu.VMEM((SLOTS, 16, COLS), F32),
            pltpu.VMEM((SLOTS, 16, COLS), F32),
            pltpu.VMEM((2, COLS), F32),
            pltpu.VMEM((n_frames, 2, COLS), F32),
            pltpu.VMEM((128, EXT * COLS), BF16),
            pltpu.VMEM((192, COLS), F32),
            pltpu.VMEM((192, COLS), F32),
            pltpu.VMEM((8 * EXT, COLS), F32),
            pltpu.VMEM((CHUNKS, 256, 256), BF16),
            pltpu.VMEM((KD, COLS), F32),
            pltpu.VMEM((8, COLS), F32),
            dma((2,)),
            dma((2,)),
            dma,
            dma,
            dma,
            dma,
            dma,
            dma,
        ],
        compiler_params=pltpu.CompilerParams(collective_id=0, has_side_effects=True),
    )(
        raw_movie,
        shifts.transpose(0, 1, 3, 2),
        footprints.transpose(1, 2, 0).reshape(TILE * TILE, KD),
        anchors.T,
        block_of.reshape(1, KD),
        init_traces.T,
    )
    traces_z = pltpu.with_memory_space_constraint(traces_z, pltpu.VMEM)
    residual = pltpu.with_memory_space_constraint(residual, pltpu.VMEM)
    traces_z, residual = pl.pallas_call(
        hand_on,
        out_shape=(
            jax.ShapeDtypeStruct((2, KD), F32),
            jax.ShapeDtypeStruct((2 * ROWS, COLS), F32),
        ),
        in_specs=[pl.BlockSpec(memory_space=pltpu.VMEM)] * 2,
        out_specs=(pl.BlockSpec(memory_space=pltpu.HBM),) * 2,
        scratch_shapes=[dma((2,))],
    )(traces_z, residual)
    return traces_z.T, residual.reshape(2, ROWS, COLS)


def solution(mesh):
    in_specs = (
        P("frames", "slab", None),
        P(None, "frames", "slab", None),
        P("slab", None, None),
        P("slab", None),
        P("slab"),
        P("slab", "frames"),
    )
    out_specs = (P("slab", "frames"), P("frames", "slab", None))
    body = functools.partial(shards, mesh.shape["slab"], mesh.shape["frames"])
    return jax.shard_map(body, mesh=mesh, in_specs=in_specs, out_specs=out_specs, check_vma=False)
```
